1024 devices in a mesh: gx: 32 (over z, core), gy: 32 (over x, y).
Axes of the slice: x: 4, y: 8, z: 16, core: 2. Of those that a mesh axis runs over, the one named last changes fastest.
Arguments:
- density: bfloat16 [128, 128, 1024], P('gx', 'gy'), may hold values from -6 to 6
- p2m_operator: bfloat16 [64, 56], replicated, may hold values from -0.75 to 0.75
- m2l_table: bfloat16 [7, 7, 7, 56, 56], replicated, may hold values from -0.0625 to 0.0625
- near_table: bfloat16 [3, 3, 3, 64, 64], replicated, may hold values from -0.15625 to 0.15625
- l2p_operator: bfloat16 [56, 64], replicated, may hold values from -0.75 to 0.75
Outputs:
- potential: float32 [128, 128, 1024], P('gx', 'gy')
The draws below stay inside these ranges and needn't reach their ends.
All inputs are finite; a program needn't handle non-finite values.
Results may differ from the reference program's by a relative error of at most 0.003.
Values may be sent and summed in bfloat16 or wider, within the bound.
A program may use at most 128 MiB of HBM per device.

```python
import jax
import jax.numpy as jnp
from jax import lax

Q = 64
NE = 56
LZ = 16
LX = 128
LY = 128


def shard_levels(own_key, shape, split, least, top_value):
    loudness, own = 1.0, jax.random.fold_in(own_key, 6)
    for dim, parts in split:
        steps = jnp.exp(jax.random.uniform(jax.random.fold_in(own, dim), (parts,), jnp.float32, least / len(split), top_value / len(split)))
        loudness = loudness * jnp.repeat(steps, shape[dim] // parts).reshape([-1 if axis == dim else 1 for axis in range(len(shape))])
    return loudness


def gaussian(rng, extent, spread, reach, cuts=(), held_as=jnp.bfloat16):
    array = spread * jax.random.normal(rng, extent, jnp.float32)
    if cuts:
        array = array * shard_levels(rng, extent, cuts, -0.22, 0.18)
    return jnp.clip(array, -reach, reach).astype(held_as)


def setup_inputs(seed: int = 0) -> dict:
    streams_of = jax.random.split(jax.random.key(seed), 6)
    return {
        "density": gaussian(streams_of[0], (LX, LY, LZ * Q), 1.0, 6.0, ((0, 32), (1, 32))),
        "p2m_operator": gaussian(streams_of[1], (Q, NE), Q ** -0.5, 0.75),
        "m2l_table": gaussian(streams_of[2], (7, 7, 7, NE, NE), (189 * NE) ** -0.5, 0.0625),
        "near_table": gaussian(streams_of[3], (3, 3, 3, Q, Q), (27 * Q) ** -0.5, 0.15625),
        "l2p_operator": gaussian(streams_of[4], (NE, Q), NE ** -0.5, 0.75),
    }


def masked_table(kernel_table):
    offsets = jnp.abs(jnp.arange(7) - 3)
    largest = jnp.maximum(jnp.maximum(offsets[:, None, None], offsets[None, :, None]), offsets[None, None, :])
    distant = (largest >= 2).astype(kernel_table.dtype)
    return kernel_table * distant[:, :, :, None, None]


def class_matrix(kernel_table):
    surface = kernel_table.shape[-1]
    blocks = []
    for parity_x in range(2):
        for parity_y in range(2):
            for parity_z in range(2):
                window = kernel_table[1 - parity_x:7 - parity_x, 1 - parity_y:7 - parity_y, 1 - parity_z:7 - parity_z]
                blocks.append(window.reshape(216 * surface, surface))
    return jnp.concatenate(blocks, axis=1)


def far_local(blocked, weights):
    across = blocked.shape[0] - 2
    sideways = blocked.shape[2] - 2
    height = blocked.shape[4] - 2
    surface = blocked.shape[-1]
    pieces = []
    for offset_x in range(3):
        for offset_y in range(3):
            for offset_z in range(3):
                pieces.append(blocked[offset_x:offset_x + across, :, offset_y:offset_y + sideways, :, offset_z:offset_z + height, :, :])
    stacked = jnp.stack(pieces, 0).reshape((3, 3, 3, across, 2, sideways, 2, height, 2, surface))
    stacked = stacked.transpose(3, 5, 7, 0, 4, 1, 6, 2, 8, 9).reshape(across * sideways * height, 216 * surface)
    expansion = jnp.dot(stacked, weights, preferred_element_type=jnp.float32)
    expansion = expansion.reshape(across, sideways, height, 2, 2, 2, surface).transpose(0, 3, 1, 4, 2, 5, 6)
    return expansion.reshape(2 * across, 2 * sideways, 2 * height, surface)


def near_field(padded, near_matrix):
    across = padded.shape[0] - 2
    sideways = padded.shape[1] - 2
    height = padded.shape[2] - 2
    node_count = padded.shape[-1]
    pieces = []
    for offset_x in range(3):
        for offset_y in range(3):
            for offset_z in range(3):
                pieces.append(padded[offset_x:offset_x + across, offset_y:offset_y + sideways, offset_z:offset_z + height, :])
    stacked = jnp.concatenate(pieces, axis=-1).reshape(across * sideways * height, 27 * node_count)
    result = jnp.dot(stacked, near_matrix, preferred_element_type=jnp.float32)
    return result.reshape(across, sideways, height, node_count)


def reference(density, p2m_operator, m2l_table, near_table, l2p_operator):
    leaf_cells = density.reshape(LX, LY, LZ, Q)
    multipole = jnp.dot(leaf_cells.reshape(LX * LY * LZ, Q), p2m_operator, preferred_element_type=jnp.float32).astype(jnp.bfloat16)
    multipole = multipole.reshape(LX, LY, LZ, NE)
    weights = class_matrix(masked_table(m2l_table))
    blocked = jnp.pad(multipole, ((2, 2), (2, 2), (2, 2), (0, 0))).reshape(LX // 2 + 2, 2, LY // 2 + 2, 2, LZ // 2 + 2, 2, NE)

    def far_slab(position):
        slab_rows = lax.dynamic_slice_in_dim(blocked, position, 3, 0)
        return far_local(slab_rows, weights)

    expansion = lax.map(far_slab, jnp.arange(LX // 2, dtype=jnp.int32)).reshape(LX, LY, LZ, NE)
    rounded = expansion.astype(jnp.bfloat16)
    padded = jnp.pad(leaf_cells, ((1, 1), (1, 1), (1, 1), (0, 0)))
    near_matrix = near_table.reshape(27 * Q, Q)

    def near_slab(position):
        slab_rows = lax.dynamic_slice_in_dim(padded, position, 3, 0)
        return near_field(slab_rows, near_matrix)

    close_part = lax.map(near_slab, jnp.arange(LX, dtype=jnp.int32)).reshape(LX, LY, LZ, Q)
    distant_part = jnp.dot(rounded.reshape(LX * LY * LZ, NE), l2p_operator, preferred_element_type=jnp.float32)
    potential = close_part + distant_part.reshape(LX, LY, LZ, Q)
    return potential.reshape(LX, LY, LZ * Q)
```

```python
import jax
import jax.numpy as jnp
from jax import lax
from jax.experimental import pallas as pl
from jax.experimental.pallas import tpu as pltpu
from jax.sharding import PartitionSpec as P

BF = jnp.bfloat16
F32 = jnp.float32
MESH = pl.DeviceIdType.MESH
HALO = 2
SIDES = [(dx, dy) for dx in (-1, 0, 1) for dy in (-1, 0, 1) if (dx, dy) != (0, 0)]
SOURCE = {-1: slice(0, 2), 0: slice(0, 4), 1: slice(2, 4)}
TARGET = {-1: slice(6, 8), 0: slice(2, 6), 1: slice(0, 2)}
BLOCKS = (1, 2, 5, 6, 3, 4)


def dot(a, b):
    return jnp.dot(a, b, preferred_element_type=F32)


def left(block):
    rows, lanes = block.shape
    block = jnp.concatenate([block, jnp.zeros((rows, 128 - lanes), BF)], axis=1)
    if rows < 64:
        block = jnp.concatenate([block, jnp.zeros((64 - rows, 128), BF)], axis=0)
    return block


def swap(block):
    return pltpu.roll(block, 64, 1)


def kernel(
    density, p2m_t, m2l, near, l2p, out,
    raw, cells, table, near_raw, p2m_raw, l2p_raw,
    weights, near_weights, far0, far1, far2, near0, near1,
    in_sems, table_sems, send_sems, recv_sems,
):
    gx, gy = lax.axis_index("gx"), lax.axis_index("gy")
    nx, ny = lax.axis_size("gx"), lax.axis_size("gy")

    def present(dx, dy):
        ok = None
        for d, g, n in ((dx, gx, nx), (dy, gy, ny)):
            if d:
                test = (g + d >= 0) & (g + d < n)
                ok = test if ok is None else ok & test
        return ok

    copies_in = [
        pltpu.make_async_copy(density, raw, in_sems.at[0]),
        pltpu.make_async_copy(near, near_raw, in_sems.at[1]),
        pltpu.make_async_copy(p2m_t, p2m_raw, in_sems.at[2]),
        pltpu.make_async_copy(l2p, l2p_raw, in_sems.at[3]),
    ]
    copies_in[0].start()
    barrier = pltpu.get_barrier_semaphore()
    count = jnp.int32(0)
    for dx, dy in SIDES:
        ok = present(dx, dy)
        count = count + ok.astype(jnp.int32)

        @pl.when(ok)
        def _():
            pl.semaphore_signal(
                barrier, inc=1, device_id=(gx + dx, gy + dy), device_id_type=MESH
            )
    for c in copies_in[1:]:
        c.start()
    table_copies = [
        pltpu.make_async_copy(m2l.at[i], table.at[i], table_sems.at[i]) for i in range(7)
    ]
    for c in table_copies:
        c.start()

    for dx, dy in SIDES:
        @pl.when(jnp.logical_not(present(dx, dy)))
        def _():
            ys, xs = TARGET[-dy], TARGET[-dx]
            cells[ys, xs] = jnp.zeros((ys.stop - ys.start, xs.stop - xs.start, 8, 128), BF)

    copies_in[0].wait()
    own = raw[...].astype(F32)
    for y in range(4):
        for x in range(4):
            tile = jnp.concatenate(
                [own[x, y : y + 1, 128 * z : 128 * z + 128] for z in range(8)], axis=0
            )
            cells[HALO + y, HALO + x] = tile.astype(BF)

    lane = lax.broadcasted_iota(jnp.int32, (64, 128), 1)
    low = lane < 64
    zero = jnp.zeros((64, 128), BF)
    copies_in[1].wait()

    def build_near(i, carry):
        a = near_raw[i // 3, i % 3, 0]
        b = near_raw[i // 3, i % 3, 1]
        c = near_raw[i // 3, i % 3, 2]
        a, b, c = left(a), left(b), left(c)
        near_weights[i, 0:64] = jnp.where(low, b, swap(a))
        near_weights[i, 64:128] = jnp.where(low, c, swap(b))
        near_weights[i, 128:192] = swap(c)
        near_weights[i, 192:256] = a
        return carry

    lax.fori_loop(0, 9, build_near, 0)

    copies_in[2].wait()
    copies_in[3].wait()
    p2m_block = left(p2m_raw[...])
    p2m = jnp.concatenate([p2m_block, swap(p2m_block)], axis=0)
    l2p_block = left(l2p_raw[...])
    l2p_pair = jnp.concatenate([l2p_block, swap(l2p_block)], axis=0)

    pl.semaphore_wait(barrier, count)

    def remote(k):
        dx, dy = SIDES[k]
        return pltpu.make_async_remote_copy(
            src_ref=cells.at[
                slice(HALO + SOURCE[dy].start, HALO + SOURCE[dy].stop),
                slice(HALO + SOURCE[dx].start, HALO + SOURCE[dx].stop),
            ],
            dst_ref=cells.at[TARGET[dy], TARGET[dx]],
            send_sem=send_sems.at[k],
            recv_sem=recv_sems.at[k],
            device_id=(gx + dx, gy + dy),
            device_id_type=MESH,
        )

    for k, (dx, dy) in enumerate(SIDES):
        @pl.when(present(dx, dy))
        def _():
            remote(k).start()

    for ox in range(7):
        table_copies[ox].wait()

        def build(oy, carry):
            blocks = [left(table[ox, oy, k]) for k in range(7)]
            for slot, k in enumerate(BLOCKS):
                weights[ox, oy, 64 * slot : 64 * slot + 64] = jnp.where(
                    low, blocks[k], swap(blocks[k - 1])
                )
            return carry

        lax.fori_loop(0, 7, build, 0)
        if 2 <= ox <= 4:
            def build_close(oy, carry):
                weights[ox, oy, 64:128] = swap(left(table[ox, oy, 1]))
                weights[ox, oy, 128:192] = left(table[ox, oy, 5])
                return carry

            lax.fori_loop(2, 5, build_close, 0)

    for k, (dx, dy) in enumerate(SIDES):
        @pl.when(present(-dx, -dy))
        def _():
            remote(k).wait_recv()

    row = lax.broadcasted_iota(jnp.int32, (8, 8, 128), 1)
    half = lax.broadcasted_iota(jnp.int32, (8, 8, 128), 2) < 64

    def below(v):
        return jnp.where(row == 0, 0.0, pltpu.roll(v, 1, 1))

    def above(v):
        return jnp.where(row == 7, 0.0, pltpu.roll(v, 7, 1))

    def spread(y, carry):
        raw_rows = cells[y]
        rows = raw_rows.astype(F32)
        packed = rows.reshape(64, 128).astype(BF)
        m = lax.dot_general(
            packed, p2m, (((1,), (1,)), ((), ())), preferred_element_type=F32
        ).reshape(8, 8, 128)
        for part, v in enumerate((below(m), above(m), m)):
            ln = slice(128 * part, 128 * part + 128)
            far0[y, :, ln] = v.reshape(64, 128).astype(BF)
            far1[y, :, ln] = v[1:7].reshape(48, 128).astype(BF)
            far2[y, 0:16, ln] = jnp.concatenate([v[0], v[2]], axis=0).astype(BF)
            far2[y, 16:32, ln] = jnp.concatenate([v[5], v[7]], axis=0).astype(BF)
        edge = jnp.where(half, above(rows), below(rows))
        for part, v in enumerate((rows, edge)):
            ln = slice(128 * part, 128 * part + 128)
            near0[y, :, ln] = v.reshape(64, 128).astype(BF)
            near1[y, :, ln] = v[1:7].reshape(48, 128).astype(BF)
        return carry

    lax.fori_loop(0, 8, spread, 0)

    def sources(even, odd, x0, y0, count, lanes):
        if x0 % 2 == 0:
            ref, start = even, 8 * x0
        else:
            ref, start = odd, 8 * (x0 - 1)
        return ref[y0 : y0 + count, start : start + 32, 0:lanes].reshape(32 * count, lanes)

    close = jnp.zeros((128, 128), F32)
    for dx in range(3):
        for dy in range(3):
            close += dot(
                sources(near0, near1, 1 + dx, 1 + dy, 4, 256), near_weights[3 * dx + dy]
            )

    total = jnp.zeros((128, 128), F32)
    for ox in range(1, 6):
        for oy in range(1, 6):
            lanes = 256 if 2 <= ox <= 4 and 2 <= oy <= 4 else 384
            total += dot(
                sources(far0, far1, ox - 1, oy - 1, 4, lanes), weights[ox, oy, 0:lanes]
            )
    total = [[total[32 * y + 8 * x : 32 * y + 8 * x + 8] for x in range(4)] for y in range(4)]

    def add(value, ys, xs):
        i = 0
        for y in ys:
            for x in xs:
                total[y][x] = total[y][x] + value[8 * i : 8 * i + 8]
                i += 1

    for oy, ys, places in ((0, (1, 3), (0, 2)), (6, (0, 2), (5, 7))):
        acc = jnp.zeros((64, 128), F32)
        for ox in range(1, 6):
            lhs = jnp.concatenate(
                [sources(far0, far1, ox - 1, place, 1, 384) for place in places], axis=0
            )
            acc += dot(lhs, weights[ox, oy])
        add(acc, ys, range(4))
    for ox, xs, group in ((0, (1, 3), 0), (6, (0, 2), 1)):
        acc = jnp.zeros((64, 128), F32)
        for oy in range(1, 6):
            lhs = far2[oy - 1 : oy + 3, 16 * group : 16 * group + 16].reshape(64, 384)
            acc += dot(lhs, weights[ox, oy])
        add(acc, range(4), xs)
        for oy, ys, places in ((0, (1, 3), (0, 2)), (6, (0, 2), (5, 7))):
            lhs = jnp.concatenate(
                [far2[place, 16 * group : 16 * group + 16] for place in places], axis=0
            )
            add(dot(lhs, weights[ox, oy]), ys, xs)

    expansion = jnp.concatenate([total[y][x] for y in range(4) for x in range(4)], axis=0)
    result = close + dot(expansion.astype(BF), l2p_pair)
    for y in range(4):
        for x in range(4):
            for z in range(8):
                r = 32 * y + 8 * x + z
                out[x, y : y + 1, 128 * z : 128 * z + 128] = result[r : r + 1]

    for k, (dx, dy) in enumerate(SIDES):
        @pl.when(present(dx, dy))
        def _():
            remote(k).wait_send()


def local(density, p2m_operator, m2l_table, near_table, l2p_operator):
    anywhere = pl.BlockSpec(memory_space=pltpu.HBM)
    operands = [
        pltpu.with_memory_space_constraint(v, pltpu.HBM)
        for v in (density, p2m_operator.T, m2l_table, near_table, l2p_operator)
    ]
    return pl.pallas_call(
        kernel,
        out_shape=jax.ShapeDtypeStruct(density.shape, F32),
        in_specs=[anywhere] * 5,
        out_specs=pl.BlockSpec(memory_space=pltpu.VMEM),
        scratch_shapes=[
            pltpu.VMEM((4, 4, 1024), BF),
            pltpu.VMEM((8, 8, 8, 128), BF),
            pltpu.VMEM((7, 7, 7, 56, 56), BF),
            pltpu.VMEM((3, 3, 3, 64, 64), BF),
            pltpu.VMEM((56, 64), BF),
            pltpu.VMEM((56, 64), BF),
            pltpu.VMEM((7, 7, 384, 128), BF),
            pltpu.VMEM((9, 256, 128), BF),
            pltpu.VMEM((8, 64, 384), BF),
            pltpu.VMEM((8, 48, 384), BF),
            pltpu.VMEM((8, 32, 384), BF),
            pltpu.VMEM((8, 64, 256), BF),
            pltpu.VMEM((8, 48, 256), BF),
            pltpu.SemaphoreType.DMA((4,)),
            pltpu.SemaphoreType.DMA((7,)),
            pltpu.SemaphoreType.DMA((8,)),
            pltpu.SemaphoreType.DMA((8,)),
        ],
        compiler_params=pltpu.CompilerParams(
            collective_id=0, has_side_effects=True, vmem_limit_bytes=32 * 1024 * 1024
        ),
    )(*operands)


def solution(mesh):
    placed = (P("gx", "gy", None), P(), P(), P(), P())
    return jax.shard_map(
        local, mesh=mesh, in_specs=placed, out_specs=P("gx", "gy", None), check_vma=False
    )
```

```python
import jax
import jax.numpy as jnp
from jax import lax
from jax.experimental import pallas as pl
from jax.experimental.pallas import tpu as pltpu
from jax.sharding import PartitionSpec as P

BF = jnp.bfloat16
F32 = jnp.float32
MESH = pl.DeviceIdType.MESH
HALO = 2
SIDES = [(dx, dy) for dx in (-1, 0, 1) for dy in (-1, 0, 1) if (dx, dy) != (0, 0)]
SOURCE = {-1: slice(2, 4), 0: slice(2, 6), 1: slice(4, 6)}
TARGET = {-1: slice(6, 8), 0: slice(2, 6), 1: slice(0, 2)}


def near_offset(ox, oy):
    return 2 <= ox <= 4 and 2 <= oy <= 4


def far_tiles():
    classes = {}
    for ox in range(7):
        pars = tuple(p for p in (0, 1) if 0 <= ox - 1 + p <= 5)
        for oy in range(7):
            if oy in (0, 6):
                ys = (1, 3) if oy == 0 else (0, 2)
            else:
                ys = (0, 1, 2, 3)
            for c in (0, 2) if near_offset(ox, oy) else (0, 1, 2):
                classes.setdefault((pars, ys), []).append((ox, oy, c))
    tiles = []
    for (pars, ys), chunks in classes.items():
        for i in range(0, len(chunks), 2):
            tiles.append((pars, ys, chunks[i : i + 2]))
    return tiles


def widen(block):
    rows, lanes = block.shape
    block = jnp.concatenate([block, jnp.zeros((rows, 128 - lanes), BF)], axis=1)
    if rows < 64:
        block = jnp.concatenate([block, jnp.zeros((64 - rows, 128), BF)], axis=0)
    return block


def kernel(
    density, p2m_t, m2l, near, l2p, out,
    raw, cells, table, near_raw, p2m_raw, l2p_raw, wide, near_wide, far_rows, near_rows,
    in_sems, table_sems, send_sems, recv_sems,
):
    gx, gy = lax.axis_index("gx"), lax.axis_index("gy")
    nx, ny = lax.axis_size("gx"), lax.axis_size("gy")

    def present(dx, dy):
        ok = None
        for d, g, n in ((dx, gx, nx), (dy, gy, ny)):
            if d:
                test = (g + d >= 0) & (g + d < n)
                ok = test if ok is None else ok & test
        return ok

    copies_in = [
        pltpu.make_async_copy(density, raw, in_sems.at[0]),
        pltpu.make_async_copy(near, near_raw, in_sems.at[1]),
        pltpu.make_async_copy(p2m_t, p2m_raw, in_sems.at[2]),
        pltpu.make_async_copy(l2p, l2p_raw, in_sems.at[3]),
    ]
    copies_in[0].start()
    barrier = pltpu.get_barrier_semaphore()
    count = jnp.int32(0)
    for dx, dy in SIDES:
        ok = present(dx, dy)
        count = count + ok.astype(jnp.int32)

        @pl.when(ok)
        def _():
            pl.semaphore_signal(
                barrier, inc=1, device_id=(gx + dx, gy + dy), device_id_type=MESH
            )
    for c in copies_in[1:]:
        c.start()
    table_copies = [
        pltpu.make_async_copy(m2l.at[i], table.at[i], table_sems.at[i]) for i in range(7)
    ]
    for c in table_copies:
        c.start()

    for dx, dy in SIDES:
        @pl.when(jnp.logical_not(present(dx, dy)))
        def _():
            ys, xs = TARGET[-dy], TARGET[-dx]
            cells[ys, xs] = jnp.zeros((ys.stop - ys.start, xs.stop - xs.start, 8, 128), BF)

    copies_in[0].wait()
    own = raw[...].astype(F32)
    for y in range(4):
        for x in range(4):
            tile = jnp.concatenate(
                [own[x, y : y + 1, 128 * z : 128 * z + 128] for z in range(8)], axis=0
            )
            cells[HALO + y, HALO + x] = tile.astype(BF)

    pl.semaphore_wait(barrier, count)

    def remote(k):
        dx, dy = SIDES[k]
        return pltpu.make_async_remote_copy(
            src_ref=cells.at[SOURCE[dy], SOURCE[dx]],
            dst_ref=cells.at[TARGET[dy], TARGET[dx]],
            send_sem=send_sems.at[k],
            recv_sem=recv_sems.at[k],
            device_id=(gx + dx, gy + dy),
            device_id_type=MESH,
        )

    for k, (dx, dy) in enumerate(SIDES):
        @pl.when(present(dx, dy))
        def _():
            remote(k).start()

    for c in copies_in[1:]:
        c.wait()
    p2m_block = widen(p2m_raw[...])
    p2m = jnp.concatenate([p2m_block, pltpu.roll(p2m_block, 64, 1)], axis=0)
    l2p_block = jnp.concatenate([widen(l2p_raw[...]), jnp.zeros((64, 128), BF)], axis=0)
    zero_block = jnp.zeros((128, 128), BF)
    l2p_pair = jnp.concatenate(
        [
            jnp.concatenate([l2p_block, zero_block], axis=1),
            jnp.concatenate([zero_block, l2p_block], axis=1),
        ],
        axis=0,
    )

    def widen_near(i, carry):
        for k in range(3):
            near_wide[i, k] = widen(near_raw[i // 3, i % 3, k])
        return carry

    lax.fori_loop(0, 9, widen_near, 0)
    for ox in range(7):
        table_copies[ox].wait()

        def widen_far(oy, carry):
            for k in range(7):
                wide[ox, oy, k] = widen(table[ox, oy, k])
            return carry

        lax.fori_loop(0, 7, widen_far, 0)
        if 2 <= ox <= 4:
            for oy in range(2, 5):
                wide[ox, oy, 2:5] = jnp.zeros((3, 64, 128), BF)

    for k, (dx, dy) in enumerate(SIDES):
        @pl.when(present(-dx, -dy))
        def _():
            remote(k).wait_recv()

    row = lax.broadcasted_iota(jnp.int32, (8, 8, 128), 1)
    half = lax.broadcasted_iota(jnp.int32, (8, 8, 128), 2) < 64

    def below(v):
        return jnp.where(row == 0, 0.0, pltpu.roll(v, 1, 1))

    def above(v):
        return jnp.where(row == 7, 0.0, pltpu.roll(v, 7, 1))

    p2m_pair = jnp.concatenate(
        [
            jnp.concatenate([p2m, zero_block], axis=1),
            jnp.concatenate([zero_block, p2m], axis=1),
        ],
        axis=0,
    )

    def spread(*accs):
        for mxu in range(2):
            pltpu.matmul_push_rhs(p2m_pair, 0, mxu, transpose=True)
        for i in range(4):
            lhs = jnp.concatenate([cells[2 * i + j].reshape(64, 128) for j in range(2)], axis=1)
            pltpu.matmul_acc_lhs(accs[i], lhs, load_staged_rhs=0 if i < 2 else None)
        for i in range(4):
            pair = pltpu.matmul_pop(accs[i])
            for j in range(2):
                y = 2 * i + j
                m = pair[:, 128 * j : 128 * j + 128].reshape(8, 8, 128)
                rows = cells[y].astype(F32)
                for part, v in enumerate((below(m), m, above(m))):
                    for x in range(6):
                        far_rows[y, x, :, 128 * part : 128 * part + 128] = jnp.concatenate(
                            [v[x], v[x + 2]], axis=0
                        ).astype(BF)
                if y in (0, 7):
                    continue
                edge = jnp.where(half, above(rows), below(rows))
                for part, v in enumerate((rows, edge)):
                    for x in range(1, 5):
                        near_rows[y, x - 1, :, 128 * part : 128 * part + 128] = jnp.concatenate(
                            [v[x], v[x + 2]], axis=0
                        ).astype(BF)

    pl.run_scoped(spread, *[pltpu.ACC(i % 2)((64, 256), F32) for i in range(4)])

    def products(*accs):
        acc_far = [accs[0:8], accs[8:16]]
        acc_near = [accs[16:24], accs[24:32]]
        staged = [0, 0]

        def push(rhs, mxu):
            slot = staged[mxu] % 2
            staged[mxu] += 1
            pltpu.matmul_push_rhs(rhs, slot, mxu)
            return slot

        for i in range(9):
            mxu = i % 2
            dx, dy = i // 3, i % 3
            below_w, own_w, above_w = (near_wide[i, k] for k in range(3))
            zero = jnp.zeros((64, 128), BF)
            rhs = jnp.concatenate(
                [
                    jnp.concatenate([own_w, above_w, zero, below_w], axis=0),
                    jnp.concatenate([below_w, own_w, above_w, zero], axis=0),
                ],
                axis=1,
            )
            slot = push(rhs, mxu)
            for y in range(4):
                for par in range(2):
                    pltpu.matmul_acc_lhs(
                        acc_near[mxu][2 * y + par], near_rows[y + dy + 1, dx + par],
                        load_staged_rhs=slot,
                    )
                    slot = None

        def far_rhs(ox, oy, c):
            return jnp.concatenate(
                [
                    wide[ox, oy, 2 * c + 1 : 2 * c + 3].reshape(128, 128),
                    wide[ox, oy, 2 * c : 2 * c + 2].reshape(128, 128),
                ],
                axis=1,
            )

        for i, (pars, ys, chunks) in enumerate(far_tiles()):
            mxu = (i + 1) % 2
            parts = [far_rhs(*chunk) for chunk in chunks]
            if len(parts) == 1:
                parts.append(jnp.zeros((128, 256), BF))
            slot = push(jnp.concatenate(parts, axis=0), mxu)
            for y in ys:
                for par in pars:
                    lhs = [
                        far_rows[y + oy - 1, ox - 1 + par, :, 128 * c : 128 * c + 128]
                        for ox, oy, c in chunks
                    ]
                    if len(lhs) == 1:
                        lhs.append(jnp.zeros((16, 128), BF))
                    pltpu.matmul_acc_lhs(
                        acc_far[mxu][2 * y + par], jnp.concatenate(lhs, axis=1), load_staged_rhs=slot
                    )
                    slot = None

        slot = push(l2p_pair, 0)
        for unit in range(8):
            expansion = pltpu.matmul_pop(acc_far[0][unit]) + pltpu.matmul_pop(acc_far[1][unit])
            pltpu.matmul_acc_lhs(acc_near[0][unit], expansion.astype(BF), load_staged_rhs=slot)
            slot = None
        for y in range(4):
            for par in range(2):
                unit = 2 * y + par
                both = pltpu.matmul_pop(acc_near[0][unit]) + pltpu.matmul_pop(acc_near[1][unit])
                low = lax.broadcasted_iota(jnp.int32, (16, 128), 1) < 64
                value = jnp.where(low, both[:, :128], pltpu.roll(both[:, 128:], 64, 1))
                for i in range(2):
                    for z in range(8):
                        r = 8 * i + z
                        out[2 * i + par, y : y + 1, 128 * z : 128 * z + 128] = value[r : r + 1]
    pl.run_scoped(
        products,
        *[pltpu.ACC(mxu)((16, 256), F32) for _ in range(2) for mxu in range(2) for _ in range(8)],
    )

    for k, (dx, dy) in enumerate(SIDES):
        @pl.when(present(dx, dy))
        def _():
            remote(k).wait_send()


def local(density, p2m_operator, m2l_table, near_table, l2p_operator):
    in_hbm = pl.BlockSpec(memory_space=pltpu.HBM)
    operands = [
        pltpu.with_memory_space_constraint(v, pltpu.HBM)
        for v in (density, p2m_operator.T, m2l_table, near_table, l2p_operator)
    ]
    return pl.pallas_call(
        kernel,
        out_shape=jax.ShapeDtypeStruct(density.shape, F32),
        in_specs=[in_hbm] * 5,
        out_specs=pl.BlockSpec(memory_space=pltpu.VMEM),
        scratch_shapes=[
            pltpu.VMEM((4, 4, 1024), BF),
            pltpu.VMEM((8, 8, 8, 128), BF),
            pltpu.VMEM((7, 7, 7, 56, 56), BF),
            pltpu.VMEM((3, 3, 3, 64, 64), BF),
            pltpu.VMEM((56, 64), BF),
            pltpu.VMEM((56, 64), BF),
            pltpu.VMEM((7, 7, 7, 64, 128), BF),
            pltpu.VMEM((9, 3, 64, 128), BF),
            pltpu.VMEM((8, 6, 16, 384), BF),
            pltpu.VMEM((8, 4, 16, 256), BF),
            pltpu.SemaphoreType.DMA((4,)),
            pltpu.SemaphoreType.DMA((7,)),
            pltpu.SemaphoreType.DMA((8,)),
            pltpu.SemaphoreType.DMA((8,)),
        ],
        compiler_params=pltpu.CompilerParams(
            collective_id=0, has_side_effects=True, vmem_limit_bytes=32 * 1024 * 1024
        ),
    )(*operands)


def solution(mesh):
    placed = (P("gx", "gy", None), P(), P(), P(), P())

    def build(*args):
        with jax.sharding.use_abstract_mesh(mesh.abstract_mesh):
            return jax.shard_map(
                local, mesh=mesh, in_specs=placed, out_specs=P("gx", "gy", None), check_vma=False
            )(*args)

    return build
```

```python
import jax
import jax.numpy as jnp
from jax import lax
from jax.experimental import pallas as pl
from jax.experimental.pallas import tpu as pltpu
from jax.sharding import PartitionSpec as P

BF = jnp.bfloat16
F32 = jnp.float32
MESH = pl.DeviceIdType.MESH
HALO = 2
SIDES = [(dx, dy) for dx in (-1, 0, 1) for dy in (-1, 0, 1) if (dx, dy) != (0, 0)]
SOURCE = {-1: slice(2, 4), 0: slice(2, 6), 1: slice(4, 6)}
TARGET = {-1: slice(6, 8), 0: slice(2, 6), 1: slice(0, 2)}


def near_offset(ox, oy):
    return 2 <= ox <= 4 and 2 <= oy <= 4


def chunks(ox, oy):
    return (0, 2) if near_offset(ox, oy) else (0, 1, 2)


def parities(offset):
    return tuple(p for p in (0, 1) if 0 <= offset - 1 + p <= 5)


def early_columns():
    return {0: ((1, 0),), 1: ((0, 0), (1, 1)), 2: ((0, 1),)}


def late_products():
    classes = {}
    for ox in range(7):
        for oy in range(7):
            units = []
            for t, s in early_columns().get(ox, ()):
                units += [("x", t, p) for p in parities(oy)]
            for t, s in early_columns().get(oy, ()):
                units += [("y", t, p) for p in parities(ox)]
            if units:
                classes.setdefault(tuple(units), []).append((ox, oy))
    return classes


def dot(a, b):
    return jnp.dot(a, b, preferred_element_type=F32)


def widen(block):
    rows, lanes = block.shape
    block = jnp.concatenate([block, jnp.zeros((rows, 128 - lanes), BF)], axis=1)
    if rows < 64:
        block = jnp.concatenate([block, jnp.zeros((64 - rows, 128), BF)], axis=0)
    return block


def swap(block):
    return pltpu.roll(block, 64, 1)


def kernel(
    density, p2m_t, m2l, near, l2p, out,
    raw, cells, table, near_raw, p2m_raw, l2p_raw, weights, near_weights,
    far_rows, near_rows, far_x, far_y, near_x, near_y, total_ref, close_ref,
    in_sems, table_sems, send_sems, recv_sems,
):
    gx, gy = lax.axis_index("gx"), lax.axis_index("gy")
    nx, ny = lax.axis_size("gx"), lax.axis_size("gy")

    def present(dx, dy):
        ok = None
        for d, g, n in ((dx, gx, nx), (dy, gy, ny)):
            if d:
                test = (g + d >= 0) & (g + d < n)
                ok = test if ok is None else ok & test
        return ok

    copies_in = [
        pltpu.make_async_copy(density, raw, in_sems.at[0]),
        pltpu.make_async_copy(near, near_raw, in_sems.at[1]),
        pltpu.make_async_copy(p2m_t, p2m_raw, in_sems.at[2]),
        pltpu.make_async_copy(l2p, l2p_raw, in_sems.at[3]),
    ]
    copies_in[0].start()
    barrier = pltpu.get_barrier_semaphore()
    count = jnp.int32(0)
    for dx, dy in SIDES:
        ok = present(dx, dy)
        count = count + ok.astype(jnp.int32)

        @pl.when(ok)
        def _():
            pl.semaphore_signal(
                barrier, inc=1, device_id=(gx + dx, gy + dy), device_id_type=MESH
            )
    for c in copies_in[1:]:
        c.start()
    table_copies = [
        pltpu.make_async_copy(m2l.at[i], table.at[i], table_sems.at[i]) for i in range(7)
    ]
    for c in table_copies:
        c.start()

    for dx, dy in SIDES:
        @pl.when(jnp.logical_not(present(dx, dy)))
        def _():
            ys, xs = TARGET[-dy], TARGET[-dx]
            cells[ys, xs] = jnp.zeros((ys.stop - ys.start, xs.stop - xs.start, 8, 128), BF)

    copies_in[0].wait()
    own = raw[...].astype(F32)
    for y in range(4):
        for x in range(4):
            tile = jnp.concatenate(
                [own[x, y : y + 1, 128 * z : 128 * z + 128] for z in range(8)], axis=0
            )
            cells[HALO + y, HALO + x] = tile.astype(BF)

    pl.semaphore_wait(barrier, count)

    def remote(k):
        dx, dy = SIDES[k]
        return pltpu.make_async_remote_copy(
            src_ref=cells.at[SOURCE[dy], SOURCE[dx]],
            dst_ref=cells.at[TARGET[dy], TARGET[dx]],
            send_sem=send_sems.at[k],
            recv_sem=recv_sems.at[k],
            device_id=(gx + dx, gy + dy),
            device_id_type=MESH,
        )

    for k, (dx, dy) in enumerate(SIDES):
        @pl.when(present(dx, dy))
        def _():
            remote(k).start()

    def arrive(sides):
        for k, (dx, dy) in enumerate(SIDES):
            if (dx, dy) in sides:
                @pl.when(present(-dx, -dy))
                def _():
                    remote(k).wait_recv()

    for c in copies_in[1:]:
        c.wait()
    p2m_block = widen(p2m_raw[...])
    p2m = jnp.concatenate([p2m_block, swap(p2m_block)], axis=0)
    l2p_block = widen(l2p_raw[...])
    l2p_pair = jnp.concatenate([l2p_block, swap(l2p_block)], axis=0)
    low = lax.broadcasted_iota(jnp.int32, (64, 128), 1) < 64

    def build_near(i, carry):
        a, b, c = (widen(near_raw[i // 3, i % 3, k]) for k in range(3))
        near_weights[i, 0:64] = jnp.where(low, b, swap(a))
        near_weights[i, 64:128] = jnp.where(low, c, swap(b))
        near_weights[i, 128:192] = swap(c)
        near_weights[i, 192:256] = a
        return carry

    lax.fori_loop(0, 9, build_near, 0)

    for ox in range(7):
        table_copies[ox].wait()

        def build(oy, carry):
            blocks = [widen(table[ox, oy, k]) for k in range(7)]
            for k in range(6):
                weights[ox, oy, 64 * k : 64 * k + 64] = jnp.where(
                    low, blocks[k + 1], swap(blocks[k])
                )
            return carry

        lax.fori_loop(0, 7, build, 0)
        if 2 <= ox <= 4:
            def build_close(oy, carry):
                weights[ox, oy, 64:128] = swap(widen(table[ox, oy, 1]))
                weights[ox, oy, 256:320] = widen(table[ox, oy, 5])
                return carry

            lax.fori_loop(2, 5, build_close, 0)

    def far_weights(pairs):
        return jnp.concatenate(
            [
                weights[ox, oy, 128 * c : 128 * c + 128]
                for ox, oy in pairs
                for c in chunks(ox, oy)
            ],
            axis=0,
        )

    def shifted(v):
        row = lax.broadcasted_iota(jnp.int32, v.shape, 1)
        below = jnp.where(row == 0, 0.0, pltpu.roll(v, 1, 1))
        above = jnp.where(row == 7, 0.0, pltpu.roll(v, 7, 1))
        return below, v, above

    def multipoles(columns):
        n = columns.shape[0]
        m = lax.dot_general(
            columns.reshape(8 * n, 128), p2m, (((1,), (1,)), ((), ())),
            preferred_element_type=F32,
        )
        return shifted(m.reshape(n, 8, 128))

    def neighbours(columns):
        below, own_rows, above = shifted(columns.astype(F32))
        half = lax.broadcasted_iota(jnp.int32, own_rows.shape, 2) < 64
        return own_rows, jnp.where(half, above, below)

    def pair(a, b):
        return jnp.concatenate([a, b], axis=0).astype(BF)

    zero_rows = jnp.zeros((8, 128), F32)

    arrive(((-1, 0), (0, -1), (-1, -1)))
    far_rows[0:2] = jnp.zeros((2, 6, 16, 384), BF)
    near_rows[0] = jnp.zeros((4, 16, 256), BF)

    def spread(y, carry):
        columns = cells[y, 2:8]
        for part, v in enumerate(multipoles(columns)):
            ln = slice(128 * part, 128 * part + 128)
            for x in range(6):
                first = v[x - 2] if x >= 2 else zero_rows
                far_rows[y, x, :, ln] = pair(first, v[x])
        for part, v in enumerate(neighbours(columns[0:5])):
            ln = slice(128 * part, 128 * part + 128)
            for x in range(1, 5):
                first = v[x - 2] if x >= 2 else zero_rows
                near_rows[y - 1, x - 1, :, ln] = pair(first, v[x])
        return carry

    lax.fori_loop(2, 8, spread, 0)

    close = jnp.zeros((128, 128), F32)
    for dx in range(3):
        for dy in range(3):
            close += dot(
                near_rows[dy : dy + 4, dx : dx + 2].reshape(128, 256), near_weights[3 * dx + dy]
            )
    close_ref[...] = close

    def place(value, ys, pars):
        i = 0
        for y in ys:
            for par in pars:
                total_ref[y, par] += value[16 * i : 16 * i + 16]
                i += 1

    total_ref[...] = jnp.zeros_like(total_ref)
    for pars in ((0, 1), (1,), (0,)):
        for ys, oys in (((0, 1, 2, 3), range(1, 6)), ((1, 3), (0,)), ((0, 2), (6,))):
            acc = jnp.zeros((16 * len(ys) * len(pars), 128), F32)
            for ox in range(7):
                if parities(ox) != pars:
                    continue
                x0 = ox - 1 + pars[0]
                for oy in oys:
                    lhs = jnp.concatenate(
                        [
                            jnp.concatenate(
                                [
                                    far_rows[y + oy - 1, x0 : x0 + len(pars), :, 128 * c : 128 * c + 128]
                                    for y in ys
                                ],
                                axis=0,
                            ).reshape(16 * len(ys) * len(pars), 128)
                            for c in chunks(ox, oy)
                        ],
                        axis=1,
                    )
                    acc += dot(lhs, far_weights([(ox, oy)]))
            place(acc, ys, pars)

    arrive(((1, 0), (0, 1), (1, 1), (1, -1), (-1, 1)))
    columns = cells[:, 0:2].reshape(16, 8, 128)
    for part, v in enumerate(multipoles(columns)):
        ln = slice(128 * part, 128 * part + 128)
        for x in range(2):
            for y in range(6):
                far_x[x, y, :, ln] = pair(v[2 * y + x], v[2 * y + 4 + x])
    for part, v in enumerate(neighbours(cells[1:7, 1])):
        ln = slice(128 * part, 128 * part + 128)
        for y in range(4):
            near_x[y, :, ln] = pair(v[y], v[y + 2])
    columns = cells[0:2, 2:8].reshape(12, 8, 128)
    for part, v in enumerate(multipoles(columns)):
        ln = slice(128 * part, 128 * part + 128)
        for y in range(2):
            for x in range(6):
                first = v[6 * y + x - 2] if x >= 2 else zero_rows
                far_y[y, x, :, ln] = pair(first, v[6 * y + x])
    for part, v in enumerate(neighbours(cells[1, 2:7])):
        ln = slice(128 * part, 128 * part + 128)
        for x in range(1, 5):
            first = v[x - 2] if x >= 2 else zero_rows
            near_y[x - 1, :, ln] = pair(first, v[x])

    near_late = {}
    for axis, ref, places in (("x", near_x, (0, 1, 2)), ("y", near_y, (0, 3, 6))):
        lhs = jnp.concatenate([ref[d : d + 2].reshape(32, 256) for d in range(3)], axis=1)
        rhs = jnp.concatenate([near_weights[i] for i in places], axis=0)
        near_late[axis] = dot(lhs, rhs)

    late = {}
    for units, pairs in late_products().items():
        columns = []
        for ox, oy in pairs:
            for c in chunks(ox, oy):
                ln = slice(128 * c, 128 * c + 128)
                rows = []
                for axis, t, p in units:
                    if axis == "x":
                        rows.append(far_x[t + ox - 1, oy - 1 + p, :, ln])
                    else:
                        rows.append(far_y[t + oy - 1, ox - 1 + p, :, ln])
                columns.append(jnp.concatenate(rows, axis=0))
        value = dot(jnp.concatenate(columns, axis=1), far_weights(pairs))
        for i, unit in enumerate(units):
            part = value[16 * i : 16 * i + 16]
            late[unit] = late[unit] + part if unit in late else part

    def eight(value, i):
        return value[8 * i : 8 * i + 8]

    expansion = []
    for y in range(4):
        for x in range(4):
            value = eight(total_ref[y, x % 2], x // 2)
            if x < 2:
                value = value + eight(late["x", x, y % 2], y // 2)
            if y < 2:
                value = value + eight(late["y", y, x % 2], x // 2)
            expansion.append(value)
    distant = dot(jnp.concatenate(expansion, axis=0).astype(BF), l2p_pair)
    for y in range(4):
        for x in range(4):
            value = eight(distant, 4 * y + x) + eight(close_ref[...], 4 * y + 2 * (x % 2) + x // 2)
            if x == 0:
                value = value + eight(near_late["x"], 2 * (y % 2) + y // 2)
            if y == 0:
                value = value + eight(near_late["y"], 2 * (x % 2) + x // 2)
            for z in range(8):
                out[x, y : y + 1, 128 * z : 128 * z + 128] = value[z : z + 1]

    for k, (dx, dy) in enumerate(SIDES):
        @pl.when(present(dx, dy))
        def _():
            remote(k).wait_send()


def local(density, p2m_operator, m2l_table, near_table, l2p_operator):
    in_hbm = pl.BlockSpec(memory_space=pltpu.HBM)
    operands = [
        pltpu.with_memory_space_constraint(v, pltpu.HBM)
        for v in (density, p2m_operator.T, m2l_table, near_table, l2p_operator)
    ]
    return pl.pallas_call(
        kernel,
        out_shape=jax.ShapeDtypeStruct(density.shape, F32),
        in_specs=[in_hbm] * 5,
        out_specs=pl.BlockSpec(memory_space=pltpu.VMEM),
        scratch_shapes=[
            pltpu.VMEM((4, 4, 1024), BF),
            pltpu.VMEM((8, 8, 8, 128), BF),
            pltpu.VMEM((7, 7, 7, 56, 56), BF),
            pltpu.VMEM((3, 3, 3, 64, 64), BF),
            pltpu.VMEM((56, 64), BF),
            pltpu.VMEM((56, 64), BF),
            pltpu.VMEM((7, 7, 384, 128), BF),
            pltpu.VMEM((9, 256, 128), BF),
            pltpu.VMEM((8, 6, 16, 384), BF),
            pltpu.VMEM((7, 4, 16, 256), BF),
            pltpu.VMEM((2, 6, 16, 384), BF),
            pltpu.VMEM((2, 6, 16, 384), BF),
            pltpu.VMEM((4, 16, 256), BF),
            pltpu.VMEM((4, 16, 256), BF),
            pltpu.VMEM((4, 2, 16, 128), F32),
            pltpu.VMEM((128, 128), F32),
            pltpu.SemaphoreType.DMA((4,)),
            pltpu.SemaphoreType.DMA((7,)),
            pltpu.SemaphoreType.DMA((8,)),
            pltpu.SemaphoreType.DMA((8,)),
        ],
        compiler_params=pltpu.CompilerParams(
            collective_id=0, has_side_effects=True, vmem_limit_bytes=32 * 1024 * 1024
        ),
    )(*operands)


def solution(mesh):
    placed = (P("gx", "gy", None), P(), P(), P(), P())
    return jax.shard_map(
        local, mesh=mesh, in_specs=placed, out_specs=P("gx", "gy", None), check_vma=False
    )
```

```python
import jax
import jax.numpy as jnp
from jax import lax
from jax.experimental import pallas as pl
from jax.experimental.pallas import tpu as pltpu
from jax.sharding import PartitionSpec as P

BF = jnp.bfloat16
F32 = jnp.float32
MESH = pl.DeviceIdType.MESH
HALO = 2
SIDES = [(1, 0), (0, 1), (1, 1), (1, -1), (-1, 1), (-1, 0), (0, -1), (-1, -1)]
LOWER = [(-1, 0), (0, -1), (-1, -1)]
SOURCE = {-1: slice(2, 4), 0: slice(2, 6), 1: slice(4, 6)}
TARGET = {-1: slice(6, 8), 0: slice(2, 6), 1: slice(0, 2)}


def near_offset(ox, oy):
    return 2 <= ox <= 4 and 2 <= oy <= 4


def chunks(ox, oy):
    return (0, 2) if near_offset(ox, oy) else (0, 1, 2)


def parities(offset):
    return tuple(p for p in (0, 1) if 0 <= offset - 1 + p <= 5)


def early_columns():
    return {0: ((1, 0),), 1: ((0, 0), (1, 1)), 2: ((0, 1),)}


def late_products():
    classes = {}
    for ox in range(7):
        for oy in range(7):
            units = []
            for t, s in early_columns().get(ox, ()):
                units += [("x", t, p) for p in parities(oy)]
            for t, s in early_columns().get(oy, ()):
                units += [("y", t, p) for p in parities(ox)]
            if units:
                classes.setdefault(tuple(units), []).append((ox, oy))
    return classes


def dot(a, b):
    return jnp.dot(a, b, preferred_element_type=F32)


def widen(block):
    rows, lanes = block.shape
    block = jnp.concatenate([block, jnp.zeros((rows, 128 - lanes), BF)], axis=1)
    if rows < 64:
        block = jnp.concatenate([block, jnp.zeros((64 - rows, 128), BF)], axis=0)
    return block


def swap(block):
    return pltpu.roll(block, 64, 1)


def kernel(
    density, p2m_t, m2l, near, l2p, out,
    raw, cells, table, near_raw, p2m_raw, l2p_raw, weights, near_weights,
    far_rows, near_rows, far_x, far_y, near_x, near_y, total_ref, close_ref,
    in_sems, table_sems, send_sems, recv_sems, ready,
):
    gx, gy = lax.axis_index("gx"), lax.axis_index("gy")
    nx, ny = lax.axis_size("gx"), lax.axis_size("gy")

    def present(dx, dy):
        ok = None
        for d, g, n in ((dx, gx, nx), (dy, gy, ny)):
            if d:
                test = (g + d >= 0) & (g + d < n)
                ok = test if ok is None else ok & test
        return ok

    copies_in = [
        pltpu.make_async_copy(density, raw, in_sems.at[0]),
        pltpu.make_async_copy(near, near_raw, in_sems.at[1]),
        pltpu.make_async_copy(p2m_t, p2m_raw, in_sems.at[2]),
        pltpu.make_async_copy(l2p, l2p_raw, in_sems.at[3]),
    ]
    copies_in[0].start()
    barrier = pltpu.get_barrier_semaphore()

    def leads(dx, dy):
        return (gx + dx == 0) & (gy + dy == 0)

    def beside(dx, dy):
        return present(dx, dy) & jnp.logical_not(leads(dx, dy))

    count = jnp.int32(0)
    for dx, dy in SIDES:
        count = count + beside(dx, dy).astype(jnp.int32)

        @pl.when(present(dx, dy) & jnp.logical_not(leads(0, 0)))
        def _():
            pl.semaphore_signal(
                barrier, inc=1, device_id=(gx + dx, gy + dy), device_id_type=MESH
            )
    for c in copies_in[1:]:
        c.start()
    table_copies = [
        pltpu.make_async_copy(m2l.at[i], table.at[i], table_sems.at[i]) for i in range(7)
    ]
    for c in table_copies:
        c.start()

    for dx, dy in SIDES:
        @pl.when(jnp.logical_not(present(dx, dy)))
        def _():
            ys, xs = TARGET[-dy], TARGET[-dx]
            cells[ys, xs] = jnp.zeros((ys.stop - ys.start, xs.stop - xs.start, 8, 128), BF)

    copies_in[0].wait()
    own = raw[...].astype(F32)
    for y in range(4):
        for x in range(4):
            tile = jnp.concatenate(
                [own[x, y : y + 1, 128 * z : 128 * z + 128] for z in range(8)], axis=0
            )
            cells[HALO + y, HALO + x] = tile.astype(BF)

    pl.semaphore_wait(barrier, count)
    for dx, dy in LOWER:
        @pl.when(leads(0, 0) & present(-dx, -dy))
        def _():
            pl.semaphore_signal(
                ready, inc=1, device_id=(gx - dx, gy - dy), device_id_type=MESH
            )

    def remote(k):
        dx, dy = SIDES[k]
        return pltpu.make_async_remote_copy(
            src_ref=cells.at[SOURCE[dy], SOURCE[dx]],
            dst_ref=cells.at[TARGET[dy], TARGET[dx]],
            send_sem=send_sems.at[k],
            recv_sem=recv_sems.at[k],
            device_id=(gx + dx, gy + dy),
            device_id_type=MESH,
        )

    for k, (dx, dy) in enumerate(SIDES):
        @pl.when(beside(dx, dy))
        def _():
            remote(k).start()

    def arrive(sides):
        for k, (dx, dy) in enumerate(SIDES):
            if (dx, dy) in sides:
                @pl.when(present(-dx, -dy))
                def _():
                    remote(k).wait_recv()

    for c in copies_in[1:]:
        c.wait()
    p2m_block = widen(p2m_raw[...])
    p2m = jnp.concatenate([p2m_block, swap(p2m_block)], axis=0)
    l2p_block = widen(l2p_raw[...])
    l2p_pair = jnp.concatenate([l2p_block, swap(l2p_block)], axis=0)
    low = lax.broadcasted_iota(jnp.int32, (64, 128), 1) < 64

    def build_near(i, carry):
        a, b, c = (widen(near_raw[i // 3, i % 3, k]) for k in range(3))
        near_weights[i, 0:64] = jnp.where(low, b, swap(a))
        near_weights[i, 64:128] = jnp.where(low, c, swap(b))
        near_weights[i, 128:192] = swap(c)
        near_weights[i, 192:256] = a
        return carry

    lax.fori_loop(0, 9, build_near, 0)

    for ox in range(7):
        table_copies[ox].wait()

        def build(oy, carry):
            blocks = [widen(table[ox, oy, k]) for k in range(7)]
            for k in range(6):
                weights[ox, oy, 64 * k : 64 * k + 64] = jnp.where(
                    low, blocks[k + 1], swap(blocks[k])
                )
            return carry

        lax.fori_loop(0, 7, build, 0)
        if 2 <= ox <= 4:
            def build_close(oy, carry):
                weights[ox, oy, 64:128] = swap(widen(table[ox, oy, 1]))
                weights[ox, oy, 256:320] = widen(table[ox, oy, 5])
                return carry

            lax.fori_loop(2, 5, build_close, 0)

    def far_weights(pairs):
        return jnp.concatenate(
            [
                weights[ox, oy, 128 * c : 128 * c + 128]
                for ox, oy in pairs
                for c in chunks(ox, oy)
            ],
            axis=0,
        )

    def shifted(v):
        row = lax.broadcasted_iota(jnp.int32, v.shape, 1)
        below = jnp.where(row == 0, 0.0, pltpu.roll(v, 1, 1))
        above = jnp.where(row == 7, 0.0, pltpu.roll(v, 7, 1))
        return below, v, above

    def multipoles(columns):
        n = columns.shape[0]
        m = lax.dot_general(
            columns.reshape(8 * n, 128), p2m, (((1,), (1,)), ((), ())),
            preferred_element_type=F32,
        )
        return shifted(m.reshape(n, 8, 128))

    def neighbours(columns):
        below, own_rows, above = shifted(columns.astype(F32))
        half = lax.broadcasted_iota(jnp.int32, own_rows.shape, 2) < 64
        return own_rows, jnp.where(half, above, below)

    def pair(a, b):
        return jnp.concatenate([a, b], axis=0).astype(BF)

    zero_rows = jnp.zeros((8, 128), F32)

    arrive(LOWER)
    far_rows[0:2] = jnp.zeros((2, 6, 16, 384), BF)
    near_rows[0] = jnp.zeros((4, 16, 256), BF)

    def spread(y, carry):
        columns = cells[y, 2:8]
        for part, v in enumerate(multipoles(columns)):
            ln = slice(128 * part, 128 * part + 128)
            for x in range(6):
                first = v[x - 2] if x >= 2 else zero_rows
                far_rows[y, x, :, ln] = pair(first, v[x])
        for part, v in enumerate(neighbours(columns[0:5])):
            ln = slice(128 * part, 128 * part + 128)
            for x in range(1, 5):
                first = v[x - 2] if x >= 2 else zero_rows
                near_rows[y - 1, x - 1, :, ln] = pair(first, v[x])
        return carry

    lax.fori_loop(2, 8, spread, 0)

    close = jnp.zeros((128, 128), F32)
    for dx in range(3):
        for dy in range(3):
            close += dot(
                near_rows[dy : dy + 4, dx : dx + 2].reshape(128, 256), near_weights[3 * dx + dy]
            )
    close_ref[...] = close

    def place(value, ys, pars):
        i = 0
        for y in ys:
            for par in pars:
                total_ref[y, par] += value[16 * i : 16 * i + 16]
                i += 1

    total_ref[...] = jnp.zeros_like(total_ref)
    for pars in ((0, 1), (1,), (0,)):
        for ys, oys in (((0, 1, 2, 3), range(1, 6)), ((1, 3), (0,)), ((0, 2), (6,))):
            acc = jnp.zeros((16 * len(ys) * len(pars), 128), F32)
            for ox in range(7):
                if parities(ox) != pars:
                    continue
                x0 = ox - 1 + pars[0]
                for oy in oys:
                    lhs = jnp.concatenate(
                        [
                            jnp.concatenate(
                                [
                                    far_rows[y + oy - 1, x0 : x0 + len(pars), :, 128 * c : 128 * c + 128]
                                    for y in ys
                                ],
                                axis=0,
                            ).reshape(16 * len(ys) * len(pars), 128)
                            for c in chunks(ox, oy)
                        ],
                        axis=1,
                    )
                    acc += dot(lhs, far_weights([(ox, oy)]))
            place(acc, ys, pars)

    for k, (dx, dy) in enumerate(SIDES):
        if (dx, dy) in LOWER:
            @pl.when(leads(dx, dy))
            def _():
                pl.semaphore_wait(ready, 1)
                remote(k).start()
    arrive(tuple(side for side in SIDES if side not in LOWER))
    columns = cells[:, 0:2].reshape(16, 8, 128)
    for part, v in enumerate(multipoles(columns)):
        ln = slice(128 * part, 128 * part + 128)
        for x in range(2):
            for y in range(6):
                far_x[x, y, :, ln] = pair(v[2 * y + x], v[2 * y + 4 + x])
    for part, v in enumerate(neighbours(cells[1:7, 1])):
        ln = slice(128 * part, 128 * part + 128)
        for y in range(4):
            near_x[y, :, ln] = pair(v[y], v[y + 2])
    columns = cells[0:2, 2:8].reshape(12, 8, 128)
    for part, v in enumerate(multipoles(columns)):
        ln = slice(128 * part, 128 * part + 128)
        for y in range(2):
            for x in range(6):
                first = v[6 * y + x - 2] if x >= 2 else zero_rows
                far_y[y, x, :, ln] = pair(first, v[6 * y + x])
    for part, v in enumerate(neighbours(cells[1, 2:7])):
        ln = slice(128 * part, 128 * part + 128)
        for x in range(1, 5):
            first = v[x - 2] if x >= 2 else zero_rows
            near_y[x - 1, :, ln] = pair(first, v[x])

    near_late = {}
    for axis, ref, places in (("x", near_x, (0, 1, 2)), ("y", near_y, (0, 3, 6))):
        lhs = jnp.concatenate([ref[d : d + 2].reshape(32, 256) for d in range(3)], axis=1)
        rhs = jnp.concatenate([near_weights[i] for i in places], axis=0)
        near_late[axis] = dot(lhs, rhs)

    late = {}
    for units, pairs in late_products().items():
        columns = []
        for ox, oy in pairs:
            for c in chunks(ox, oy):
                ln = slice(128 * c, 128 * c + 128)
                rows = []
                for axis, t, p in units:
                    if axis == "x":
                        rows.append(far_x[t + ox - 1, oy - 1 + p, :, ln])
                    else:
                        rows.append(far_y[t + oy - 1, ox - 1 + p, :, ln])
                columns.append(jnp.concatenate(rows, axis=0))
        value = dot(jnp.concatenate(columns, axis=1), far_weights(pairs))
        for i, unit in enumerate(units):
            part = value[16 * i : 16 * i + 16]
            late[unit] = late[unit] + part if unit in late else part

    def eight(value, i):
        return value[8 * i : 8 * i + 8]

    expansion = []
    for y in range(4):
        for x in range(4):
            value = eight(total_ref[y, x % 2], x // 2)
            if x < 2:
                value = value + eight(late["x", x, y % 2], y // 2)
            if y < 2:
                value = value + eight(late["y", y, x % 2], x // 2)
            expansion.append(value)
    distant = dot(jnp.concatenate(expansion, axis=0).astype(BF), l2p_pair)
    for y in range(4):
        for x in range(4):
            value = eight(distant, 4 * y + x) + eight(close_ref[...], 4 * y + 2 * (x % 2) + x // 2)
            if x == 0:
                value = value + eight(near_late["x"], 2 * (y % 2) + y // 2)
            if y == 0:
                value = value + eight(near_late["y"], 2 * (x % 2) + x // 2)
            for z in range(8):
                out[x, y : y + 1, 128 * z : 128 * z + 128] = value[z : z + 1]

    for k, (dx, dy) in enumerate(SIDES):
        @pl.when(present(dx, dy))
        def _():
            remote(k).wait_send()


def local(density, p2m_operator, m2l_table, near_table, l2p_operator):
    in_hbm = pl.BlockSpec(memory_space=pltpu.HBM)
    operands = [
        pltpu.with_memory_space_constraint(v, pltpu.HBM)
        for v in (density, p2m_operator.T, m2l_table, near_table, l2p_operator)
    ]
    return pl.pallas_call(
        kernel,
        out_shape=jax.ShapeDtypeStruct(density.shape, F32),
        in_specs=[in_hbm] * 5,
        out_specs=pl.BlockSpec(memory_space=pltpu.VMEM),
        scratch_shapes=[
            pltpu.VMEM((4, 4, 1024), BF),
            pltpu.VMEM((8, 8, 8, 128), BF),
            pltpu.VMEM((7, 7, 7, 56, 56), BF),
            pltpu.VMEM((3, 3, 3, 64, 64), BF),
            pltpu.VMEM((56, 64), BF),
            pltpu.VMEM((56, 64), BF),
            pltpu.VMEM((7, 7, 384, 128), BF),
            pltpu.VMEM((9, 256, 128), BF),
            pltpu.VMEM((8, 6, 16, 384), BF),
            pltpu.VMEM((7, 4, 16, 256), BF),
            pltpu.VMEM((2, 6, 16, 384), BF),
            pltpu.VMEM((2, 6, 16, 384), BF),
            pltpu.VMEM((4, 16, 256), BF),
            pltpu.VMEM((4, 16, 256), BF),
            pltpu.VMEM((4, 2, 16, 128), F32),
            pltpu.VMEM((128, 128), F32),
            pltpu.SemaphoreType.DMA((4,)),
            pltpu.SemaphoreType.DMA((7,)),
            pltpu.SemaphoreType.DMA((8,)),
            pltpu.SemaphoreType.DMA((8,)),
            pltpu.SemaphoreType.REGULAR,
        ],
        compiler_params=pltpu.CompilerParams(
            collective_id=0, has_side_effects=True, vmem_limit_bytes=32 * 1024 * 1024
        ),
    )(*operands)


def solution(mesh):
    placed = (P("gx", "gy", None), P(), P(), P(), P())
    return jax.shard_map(
        local, mesh=mesh, in_specs=placed, out_specs=P("gx", "gy", None), check_vma=False
    )
```

```python
import jax
import jax.numpy as jnp
from jax import lax
from jax.experimental import pallas as pl
from jax.experimental.pallas import tpu as pltpu
from jax.sharding import PartitionSpec as P

BF = jnp.bfloat16
F32 = jnp.float32
MESH = pl.DeviceIdType.MESH
HALO = 2
SIDES = [(1, 0), (0, 1), (1, 1), (1, -1), (-1, 1), (-1, 0), (0, -1), (-1, -1)]
LOWER = [(-1, 0), (0, -1), (-1, -1)]
SOURCE = {-1: slice(2, 4), 0: slice(2, 6), 1: slice(4, 6)}
TARGET = {-1: slice(6, 8), 0: slice(2, 6), 1: slice(0, 2)}


def near_offset(ox, oy):
    return 2 <= ox <= 4 and 2 <= oy <= 4


def chunks(ox, oy):
    return (0, 2) if near_offset(ox, oy) else (0, 1, 2)


def parities(offset):
    return tuple(p for p in (0, 1) if 0 <= offset - 1 + p <= 5)


def early_columns():
    return {0: ((1, 0),), 1: ((0, 0), (1, 1)), 2: ((0, 1),)}


def late_products():
    classes = {}
    for ox in range(7):
        for oy in range(7):
            units = []
            for t, s in early_columns().get(ox, ()):
                units += [("x", t, p) for p in parities(oy)]
            for t, s in early_columns().get(oy, ()):
                units += [("y", t, p) for p in parities(ox)]
            if units:
                classes.setdefault(tuple(units), []).append((ox, oy))
    return classes


def dot(a, b):
    return jnp.dot(a, b, preferred_element_type=F32)


def widen(block):
    rows, lanes = block.shape
    block = jnp.concatenate([block, jnp.zeros((rows, 128 - lanes), BF)], axis=1)
    if rows < 64:
        block = jnp.concatenate([block, jnp.zeros((64 - rows, 128), BF)], axis=0)
    return block


def swap(block):
    return pltpu.roll(block, 64, 1)


def kernel(
    density, p2m_t, m2l, near, l2p, out,
    raw, cells, table, near_raw, p2m_raw, l2p_raw, weights, near_weights,
    far_rows, near_rows, far_x, far_y, near_x, near_y, total_ref, close_ref,
    in_sems, table_sems, send_sems, recv_sems, ready,
):
    gx, gy = lax.axis_index("gx"), lax.axis_index("gy")
    nx, ny = lax.axis_size("gx"), lax.axis_size("gy")

    def present(dx, dy):
        ok = None
        for d, g, n in ((dx, gx, nx), (dy, gy, ny)):
            if d:
                test = (g + d >= 0) & (g + d < n)
                ok = test if ok is None else ok & test
        return ok

    copies_in = [
        pltpu.make_async_copy(density, raw, in_sems.at[0]),
        pltpu.make_async_copy(near, near_raw, in_sems.at[1]),
        pltpu.make_async_copy(p2m_t, p2m_raw, in_sems.at[2]),
        pltpu.make_async_copy(l2p, l2p_raw, in_sems.at[3]),
    ]
    copies_in[0].start()
    barrier = pltpu.get_barrier_semaphore()

    def leads(dx, dy):
        return (gx + dx == 0) & (gy + dy == 0)

    def beside(dx, dy):
        return present(dx, dy) & jnp.logical_not(leads(dx, dy))

    count = jnp.int32(0)
    for dx, dy in SIDES:
        count = count + beside(dx, dy).astype(jnp.int32)

        @pl.when(present(dx, dy) & jnp.logical_not(leads(0, 0)))
        def _():
            pl.semaphore_signal(
                barrier, inc=1, device_id=(gx + dx, gy + dy), device_id_type=MESH
            )
    for c in copies_in[1:]:
        c.start()
    table_copies = [
        pltpu.make_async_copy(m2l.at[i], table.at[i], table_sems.at[i]) for i in range(7)
    ]
    for c in table_copies:
        c.start()

    for dx, dy in SIDES:
        @pl.when(jnp.logical_not(present(dx, dy)))
        def _():
            ys, xs = TARGET[-dy], TARGET[-dx]
            cells[ys, xs] = jnp.zeros((ys.stop - ys.start, xs.stop - xs.start, 8, 128), BF)

    copies_in[0].wait()
    own = raw[...].astype(F32)
    for y in range(4):
        for x in range(4):
            tile = jnp.concatenate(
                [own[x, y : y + 1, 128 * z : 128 * z + 128] for z in range(8)], axis=0
            )
            cells[HALO + y, HALO + x] = tile.astype(BF)

    pl.semaphore_wait(barrier, count)
    for dx, dy in LOWER:
        @pl.when(leads(0, 0) & present(-dx, -dy))
        def _():
            pl.semaphore_signal(
                ready, inc=1, device_id=(gx - dx, gy - dy), device_id_type=MESH
            )

    def remote(k):
        dx, dy = SIDES[k]
        return pltpu.make_async_remote_copy(
            src_ref=cells.at[SOURCE[dy], SOURCE[dx]],
            dst_ref=cells.at[TARGET[dy], TARGET[dx]],
            send_sem=send_sems.at[k],
            recv_sem=recv_sems.at[k],
            device_id=(gx + dx, gy + dy),
            device_id_type=MESH,
        )

    for k, (dx, dy) in enumerate(SIDES):
        @pl.when(beside(dx, dy))
        def _():
            remote(k).start()

    def arrive(sides):
        for k, (dx, dy) in enumerate(SIDES):
            if (dx, dy) in sides:
                @pl.when(present(-dx, -dy))
                def _():
                    remote(k).wait_recv()

    for c in copies_in[1:]:
        c.wait()
    p2m_block = widen(p2m_raw[...])
    p2m = jnp.concatenate([p2m_block, swap(p2m_block)], axis=0)
    l2p_block = widen(l2p_raw[...])
    l2p_pair = jnp.concatenate([l2p_block, swap(l2p_block)], axis=0)
    low = lax.broadcasted_iota(jnp.int32, (64, 128), 1) < 64

    def build_near(i, carry):
        a, b, c = (widen(near_raw[i // 3, i % 3, k]) for k in range(3))
        near_weights[i, 0:64] = jnp.where(low, b, swap(a))
        near_weights[i, 64:128] = jnp.where(low, c, swap(b))
        near_weights[i, 128:192] = swap(c)
        near_weights[i, 192:256] = a
        return carry

    lax.fori_loop(0, 9, build_near, 0, unroll=9)

    for ox in range(7):
        table_copies[ox].wait()

        def build(oy, carry):
            blocks = [widen(table[ox, oy, k]) for k in range(7)]
            for k in range(6):
                weights[ox, oy, 64 * k : 64 * k + 64] = jnp.where(
                    low, blocks[k + 1], swap(blocks[k])
                )
            return carry

        lax.fori_loop(0, 7, build, 0, unroll=7)
        if 2 <= ox <= 4:
            def build_close(oy, carry):
                weights[ox, oy, 64:128] = swap(widen(table[ox, oy, 1]))
                weights[ox, oy, 256:320] = widen(table[ox, oy, 5])
                return carry

            lax.fori_loop(2, 5, build_close, 0, unroll=3)

    def far_weights(pairs):
        return jnp.concatenate(
            [
                weights[ox, oy, 128 * c : 128 * c + 128]
                for ox, oy in pairs
                for c in chunks(ox, oy)
            ],
            axis=0,
        )

    def shifted(v):
        row = lax.broadcasted_iota(jnp.int32, v.shape, 1)
        below = jnp.where(row == 0, 0.0, pltpu.roll(v, 1, 1))
        above = jnp.where(row == 7, 0.0, pltpu.roll(v, 7, 1))
        return below, v, above

    def multipoles(columns):
        n = columns.shape[0]
        m = lax.dot_general(
            columns.reshape(8 * n, 128), p2m, (((1,), (1,)), ((), ())),
            preferred_element_type=F32,
        )
        return shifted(m.reshape(n, 8, 128))

    def neighbours(columns):
        below, own_rows, above = shifted(columns.astype(F32))
        half = lax.broadcasted_iota(jnp.int32, own_rows.shape, 2) < 64
        return own_rows, jnp.where(half, above, below)

    def pair(a, b):
        return jnp.concatenate([a, b], axis=0).astype(BF)

    zero_rows = jnp.zeros((8, 128), F32)

    arrive(LOWER)
    far_rows[0:2] = jnp.zeros((2, 6, 16, 384), BF)
    near_rows[0] = jnp.zeros((4, 16, 256), BF)

    def spread(y, carry):
        columns = cells[y, 2:8]
        for part, v in enumerate(multipoles(columns)):
            ln = slice(128 * part, 128 * part + 128)
            for x in range(6):
                first = v[x - 2] if x >= 2 else zero_rows
                far_rows[y, x, :, ln] = pair(first, v[x])
        for part, v in enumerate(neighbours(columns[0:5])):
            ln = slice(128 * part, 128 * part + 128)
            for x in range(1, 5):
                first = v[x - 2] if x >= 2 else zero_rows
                near_rows[y - 1, x - 1, :, ln] = pair(first, v[x])
        return carry

    lax.fori_loop(2, 8, spread, 0, unroll=6)

    close = jnp.zeros((128, 128), F32)
    for dx in range(3):
        for dy in range(3):
            close += dot(
                near_rows[dy : dy + 4, dx : dx + 2].reshape(128, 256), near_weights[3 * dx + dy]
            )
    close_ref[...] = close

    def place(value, ys, pars):
        i = 0
        for y in ys:
            for par in pars:
                total_ref[y, par] += value[16 * i : 16 * i + 16]
                i += 1

    total_ref[...] = jnp.zeros_like(total_ref)
    for pars in ((0, 1), (1,), (0,)):
        for ys, oys in (((0, 1, 2, 3), range(1, 6)), ((1, 3), (0,)), ((0, 2), (6,))):
            acc = jnp.zeros((16 * len(ys) * len(pars), 128), F32)
            for ox in range(7):
                if parities(ox) != pars:
                    continue
                x0 = ox - 1 + pars[0]
                for oy in oys:
                    lhs = jnp.concatenate(
                        [
                            jnp.concatenate(
                                [
                                    far_rows[y + oy - 1, x0 : x0 + len(pars), :, 128 * c : 128 * c + 128]
                                    for y in ys
                                ],
                                axis=0,
                            ).reshape(16 * len(ys) * len(pars), 128)
                            for c in chunks(ox, oy)
                        ],
                        axis=1,
                    )
                    acc += dot(lhs, far_weights([(ox, oy)]))
            place(acc, ys, pars)

    for k, (dx, dy) in enumerate(SIDES):
        if (dx, dy) in LOWER:
            @pl.when(leads(dx, dy))
            def _():
                pl.semaphore_wait(ready, 1)
                remote(k).start()
    arrive(tuple(side for side in SIDES if side not in LOWER))
    columns = cells[:, 0:2].reshape(16, 8, 128)
    for part, v in enumerate(multipoles(columns)):
        ln = slice(128 * part, 128 * part + 128)
        for x in range(2):
            for y in range(6):
                far_x[x, y, :, ln] = pair(v[2 * y + x], v[2 * y + 4 + x])
    for part, v in enumerate(neighbours(cells[1:7, 1])):
        ln = slice(128 * part, 128 * part + 128)
        for y in range(4):
            near_x[y, :, ln] = pair(v[y], v[y + 2])
    columns = cells[0:2, 2:8].reshape(12, 8, 128)
    for part, v in enumerate(multipoles(columns)):
        ln = slice(128 * part, 128 * part + 128)
        for y in range(2):
            for x in range(6):
                first = v[6 * y + x - 2] if x >= 2 else zero_rows
                far_y[y, x, :, ln] = pair(first, v[6 * y + x])
    for part, v in enumerate(neighbours(cells[1, 2:7])):
        ln = slice(128 * part, 128 * part + 128)
        for x in range(1, 5):
            first = v[x - 2] if x >= 2 else zero_rows
            near_y[x - 1, :, ln] = pair(first, v[x])

    near_late = {}
    for axis, ref, places in (("x", near_x, (0, 1, 2)), ("y", near_y, (0, 3, 6))):
        lhs = jnp.concatenate([ref[d : d + 2].reshape(32, 256) for d in range(3)], axis=1)
        rhs = jnp.concatenate([near_weights[i] for i in places], axis=0)
        near_late[axis] = dot(lhs, rhs)

    late = {}
    for units, pairs in late_products().items():
        columns = []
        for ox, oy in pairs:
            for c in chunks(ox, oy):
                ln = slice(128 * c, 128 * c + 128)
                rows = []
                for axis, t, p in units:
                    if axis == "x":
                        rows.append(far_x[t + ox - 1, oy - 1 + p, :, ln])
                    else:
                        rows.append(far_y[t + oy - 1, ox - 1 + p, :, ln])
                columns.append(jnp.concatenate(rows, axis=0))
        value = dot(jnp.concatenate(columns, axis=1), far_weights(pairs))
        for i, unit in enumerate(units):
            part = value[16 * i : 16 * i + 16]
            late[unit] = late[unit] + part if unit in late else part

    def eight(value, i):
        return value[8 * i : 8 * i + 8]

    expansion = []
    for y in range(4):
        for x in range(4):
            value = eight(total_ref[y, x % 2], x // 2)
            if x < 2:
                value = value + eight(late["x", x, y % 2], y // 2)
            if y < 2:
                value = value + eight(late["y", y, x % 2], x // 2)
            expansion.append(value)
    distant = dot(jnp.concatenate(expansion, axis=0).astype(BF), l2p_pair)
    for y in range(4):
        for x in range(4):
            value = eight(distant, 4 * y + x) + eight(close_ref[...], 4 * y + 2 * (x % 2) + x // 2)
            if x == 0:
                value = value + eight(near_late["x"], 2 * (y % 2) + y // 2)
            if y == 0:
                value = value + eight(near_late["y"], 2 * (x % 2) + x // 2)
            for z in range(8):
                out[x, y : y + 1, 128 * z : 128 * z + 128] = value[z : z + 1]

    for k, (dx, dy) in enumerate(SIDES):
        @pl.when(present(dx, dy))
        def _():
            remote(k).wait_send()


def local(density, p2m_operator, m2l_table, near_table, l2p_operator):
    in_hbm = pl.BlockSpec(memory_space=pltpu.HBM)
    operands = [
        pltpu.with_memory_space_constraint(v, pltpu.HBM)
        for v in (density, p2m_operator.T, m2l_table, near_table, l2p_operator)
    ]
    return pl.pallas_call(
        kernel,
        out_shape=jax.ShapeDtypeStruct(density.shape, F32),
        in_specs=[in_hbm] * 5,
        out_specs=pl.BlockSpec(memory_space=pltpu.VMEM),
        scratch_shapes=[
            pltpu.VMEM((4, 4, 1024), BF),
            pltpu.VMEM((8, 8, 8, 128), BF),
            pltpu.VMEM((7, 7, 7, 56, 56), BF),
            pltpu.VMEM((3, 3, 3, 64, 64), BF),
            pltpu.VMEM((56, 64), BF),
            pltpu.VMEM((56, 64), BF),
            pltpu.VMEM((7, 7, 384, 128), BF),
            pltpu.VMEM((9, 256, 128), BF),
            pltpu.VMEM((8, 6, 16, 384), BF),
            pltpu.VMEM((7, 4, 16, 256), BF),
            pltpu.VMEM((2, 6, 16, 384), BF),
            pltpu.VMEM((2, 6, 16, 384), BF),
            pltpu.VMEM((4, 16, 256), BF),
            pltpu.VMEM((4, 16, 256), BF),
            pltpu.VMEM((4, 2, 16, 128), F32),
            pltpu.VMEM((128, 128), F32),
            pltpu.SemaphoreType.DMA((4,)),
            pltpu.SemaphoreType.DMA((7,)),
            pltpu.SemaphoreType.DMA((8,)),
            pltpu.SemaphoreType.DMA((8,)),
            pltpu.SemaphoreType.REGULAR,
        ],
        compiler_params=pltpu.CompilerParams(
            collective_id=0, has_side_effects=True, vmem_limit_bytes=32 * 1024 * 1024
        ),
    )(*operands)


def solution(mesh):
    placed = (P("gx", "gy", None), P(), P(), P(), P())
    return jax.shard_map(
        local, mesh=mesh, in_specs=placed, out_specs=P("gx", "gy", None), check_vma=False
    )
```

```python
import jax
import jax.numpy as jnp
from jax import lax
from jax.experimental import pallas as pl
from jax.experimental.pallas import tpu as pltpu
from jax.sharding import PartitionSpec as P

BF = jnp.bfloat16
F32 = jnp.float32
MESH = pl.DeviceIdType.MESH
HALO = 2
SIDES = [(1, 0), (0, 1), (1, 1), (1, -1), (-1, 1), (-1, 0), (0, -1), (-1, -1)]
LOWER = [(-1, 0), (0, -1), (-1, -1)]
SOURCE = {-1: slice(2, 4), 0: slice(2, 6), 1: slice(4, 6)}
TARGET = {-1: slice(6, 8), 0: slice(2, 6), 1: slice(0, 2)}


def near_offset(ox, oy):
    return 2 <= ox <= 4 and 2 <= oy <= 4


def chunks(ox, oy):
    return (0, 2) if near_offset(ox, oy) else (0, 1, 2)


def parities(offset):
    return tuple(p for p in (0, 1) if 0 <= offset - 1 + p <= 5)


def early_columns():
    return {0: ((1, 0),), 1: ((0, 0), (1, 1)), 2: ((0, 1),)}


def late_products(axis):
    classes = {}
    for ox in range(7):
        for oy in range(7):
            along, across = (ox, oy) if axis == "x" else (oy, ox)
            units = tuple(
                (t, s - t, p) for t, s in early_columns().get(along, ()) for p in parities(across)
            )
            if units:
                classes.setdefault(units, []).append((ox, oy))
    return classes


def dot(a, b):
    return jnp.dot(a, b, preferred_element_type=F32)


def widen(block):
    rows, lanes = block.shape
    block = jnp.concatenate([block, jnp.zeros((rows, 128 - lanes), BF)], axis=1)
    if rows < 64:
        block = jnp.concatenate([block, jnp.zeros((64 - rows, 128), BF)], axis=0)
    return block


def swap(block):
    return pltpu.roll(block, 64, 1)


def kernel(
    density, p2m_t, m2l, near, l2p, out,
    raw, cells, table, near_raw, p2m_raw, l2p_raw, weights, near_weights,
    far_rows, near_rows, far_x, far_y, near_x, near_y, total_ref, close_ref,
    far_late_x, far_late_y, near_late_x, near_late_y,
    in_sems, table_sems, send_sems, recv_sems, ready,
):
    gx, gy = lax.axis_index("gx"), lax.axis_index("gy")
    nx, ny = lax.axis_size("gx"), lax.axis_size("gy")

    def present(dx, dy):
        ok = None
        for d, g, n in ((dx, gx, nx), (dy, gy, ny)):
            if d:
                test = (g + d >= 0) & (g + d < n)
                ok = test if ok is None else ok & test
        return ok

    copies_in = [
        pltpu.make_async_copy(density, raw, in_sems.at[0]),
        pltpu.make_async_copy(near, near_raw, in_sems.at[1]),
        pltpu.make_async_copy(p2m_t, p2m_raw, in_sems.at[2]),
        pltpu.make_async_copy(l2p, l2p_raw, in_sems.at[3]),
    ]
    copies_in[0].start()
    barrier = pltpu.get_barrier_semaphore()

    def leads(dx, dy):
        return (gx + dx == 0) & (gy + dy == 0)

    def beside(dx, dy):
        return present(dx, dy) & jnp.logical_not(leads(dx, dy))

    count = jnp.int32(0)
    for dx, dy in SIDES:
        count = count + beside(dx, dy).astype(jnp.int32)

        @pl.when(present(dx, dy) & jnp.logical_not(leads(0, 0)))
        def _():
            pl.semaphore_signal(
                barrier, inc=1, device_id=(gx + dx, gy + dy), device_id_type=MESH
            )
    for c in copies_in[1:]:
        c.start()
    table_copies = [
        pltpu.make_async_copy(m2l.at[i], table.at[i], table_sems.at[i]) for i in range(7)
    ]
    for c in table_copies:
        c.start()

    for dx, dy in SIDES:
        @pl.when(jnp.logical_not(present(dx, dy)))
        def _():
            ys, xs = TARGET[-dy], TARGET[-dx]
            cells[ys, xs] = jnp.zeros((ys.stop - ys.start, xs.stop - xs.start, 8, 128), BF)

    copies_in[0].wait()
    own = raw[...].astype(F32)
    for y in range(4):
        for x in range(4):
            tile = jnp.concatenate(
                [own[x, y : y + 1, 128 * z : 128 * z + 128] for z in range(8)], axis=0
            )
            cells[HALO + y, HALO + x] = tile.astype(BF)

    pl.semaphore_wait(barrier, count)
    for dx, dy in LOWER:
        @pl.when(leads(0, 0) & present(-dx, -dy))
        def _():
            pl.semaphore_signal(
                ready, inc=1, device_id=(gx - dx, gy - dy), device_id_type=MESH
            )

    def remote(k):
        dx, dy = SIDES[k]
        return pltpu.make_async_remote_copy(
            src_ref=cells.at[SOURCE[dy], SOURCE[dx]],
            dst_ref=cells.at[TARGET[dy], TARGET[dx]],
            send_sem=send_sems.at[k],
            recv_sem=recv_sems.at[k],
            device_id=(gx + dx, gy + dy),
            device_id_type=MESH,
        )

    for k, (dx, dy) in enumerate(SIDES):
        @pl.when(beside(dx, dy))
        def _():
            remote(k).start()

    def arrive(sides):
        for k, (dx, dy) in enumerate(SIDES):
            if (dx, dy) in sides:
                @pl.when(present(-dx, -dy))
                def _():
                    remote(k).wait_recv()

    for c in copies_in[1:]:
        c.wait()
    p2m_block = widen(p2m_raw[...])
    p2m = jnp.concatenate([p2m_block, swap(p2m_block)], axis=0)
    l2p_block = widen(l2p_raw[...])
    l2p_pair = jnp.concatenate([l2p_block, swap(l2p_block)], axis=0)
    low = lax.broadcasted_iota(jnp.int32, (64, 128), 1) < 64

    def build_near(i, carry):
        a, b, c = (widen(near_raw[i // 3, i % 3, k]) for k in range(3))
        near_weights[i, 0:64] = jnp.where(low, b, swap(a))
        near_weights[i, 64:128] = jnp.where(low, c, swap(b))
        near_weights[i, 128:192] = swap(c)
        near_weights[i, 192:256] = a
        return carry

    lax.fori_loop(0, 9, build_near, 0, unroll=9)

    for ox in range(7):
        table_copies[ox].wait()

        def build(oy, carry):
            blocks = [widen(table[ox, oy, k]) for k in range(7)]
            for k in range(6):
                weights[ox, oy, 64 * k : 64 * k + 64] = jnp.where(
                    low, blocks[k + 1], swap(blocks[k])
                )
            return carry

        lax.fori_loop(0, 7, build, 0, unroll=7)
        if 2 <= ox <= 4:
            def build_close(oy, carry):
                weights[ox, oy, 64:128] = swap(widen(table[ox, oy, 1]))
                weights[ox, oy, 256:320] = widen(table[ox, oy, 5])
                return carry

            lax.fori_loop(2, 5, build_close, 0, unroll=3)

    def far_weights(pairs):
        return jnp.concatenate(
            [
                weights[ox, oy, 128 * c : 128 * c + 128]
                for ox, oy in pairs
                for c in chunks(ox, oy)
            ],
            axis=0,
        )

    def shifted(v):
        row = lax.broadcasted_iota(jnp.int32, v.shape, 1)
        below = jnp.where(row == 0, 0.0, pltpu.roll(v, 1, 1))
        above = jnp.where(row == 7, 0.0, pltpu.roll(v, 7, 1))
        return below, v, above

    def multipoles(columns):
        n = columns.shape[0]
        m = lax.dot_general(
            columns.reshape(8 * n, 128), p2m, (((1,), (1,)), ((), ())),
            preferred_element_type=F32,
        )
        return shifted(m.reshape(n, 8, 128))

    def neighbours(columns):
        below, own_rows, above = shifted(columns.astype(F32))
        half = lax.broadcasted_iota(jnp.int32, own_rows.shape, 2) < 64
        return own_rows, jnp.where(half, above, below)

    def pair(a, b):
        return jnp.concatenate([a, b], axis=0).astype(BF)

    zero_rows = jnp.zeros((8, 128), F32)

    arrive(LOWER)
    far_rows[0:2] = jnp.zeros((2, 6, 16, 384), BF)
    near_rows[0] = jnp.zeros((4, 16, 256), BF)

    def spread(y, carry):
        columns = cells[y, 2:8]
        for part, v in enumerate(multipoles(columns)):
            ln = slice(128 * part, 128 * part + 128)
            for x in range(6):
                first = v[x - 2] if x >= 2 else zero_rows
                far_rows[y, x, :, ln] = pair(first, v[x])
        for part, v in enumerate(neighbours(columns[0:5])):
            ln = slice(128 * part, 128 * part + 128)
            for x in range(1, 5):
                first = v[x - 2] if x >= 2 else zero_rows
                near_rows[y - 1, x - 1, :, ln] = pair(first, v[x])
        return carry

    lax.fori_loop(2, 8, spread, 0, unroll=6)

    close = jnp.zeros((128, 128), F32)
    for dx in range(3):
        for dy in range(3):
            close += dot(
                near_rows[dy : dy + 4, dx : dx + 2].reshape(128, 256), near_weights[3 * dx + dy]
            )
    close_ref[...] = close

    def place(value, ys, pars):
        i = 0
        for y in ys:
            for par in pars:
                total_ref[y, par] += value[16 * i : 16 * i + 16]
                i += 1

    total_ref[...] = jnp.zeros_like(total_ref)
    for pars in ((0, 1), (1,), (0,)):
        for ys, oys in (((0, 1, 2, 3), range(1, 6)), ((1, 3), (0,)), ((0, 2), (6,))):
            acc = jnp.zeros((16 * len(ys) * len(pars), 128), F32)
            for ox in range(7):
                if parities(ox) != pars:
                    continue
                x0 = ox - 1 + pars[0]
                for oy in oys:
                    lhs = jnp.concatenate(
                        [
                            jnp.concatenate(
                                [
                                    far_rows[y + oy - 1, x0 : x0 + len(pars), :, 128 * c : 128 * c + 128]
                                    for y in ys
                                ],
                                axis=0,
                            ).reshape(16 * len(ys) * len(pars), 128)
                            for c in chunks(ox, oy)
                        ],
                        axis=1,
                    )
                    acc += dot(lhs, far_weights([(ox, oy)]))
            place(acc, ys, pars)

    for k, (dx, dy) in enumerate(SIDES):
        if (dx, dy) in LOWER:
            @pl.when(leads(dx, dy))
            def _():
                pl.semaphore_wait(ready, 1)
                remote(k).start()

    def late(axis, far_ref, near_ref, far_late, near_late):
        places = (0, 1, 2) if axis == "x" else (0, 3, 6)
        lhs = jnp.concatenate([near_ref[d : d + 2].reshape(32, 256) for d in range(3)], axis=1)
        rhs = jnp.concatenate([near_weights[i] for i in places], axis=0)
        near_late[...] = dot(lhs, rhs)
        sums = {}
        for units, pairs in late_products(axis).items():
            columns = []
            for ox, oy in pairs:
                across = oy if axis == "x" else ox
                for c in chunks(ox, oy):
                    ln = slice(128 * c, 128 * c + 128)
                    columns.append(
                        jnp.concatenate(
                            [far_ref[t + d, across - 1 + p, :, ln] for t, d, p in units], axis=0
                        )
                    )
            value = dot(jnp.concatenate(columns, axis=1), far_weights(pairs))
            for i, (t, _, p) in enumerate(units):
                part = value[16 * i : 16 * i + 16]
                sums[t, p] = sums[t, p] + part if (t, p) in sums else part
        for t, p in sums:
            far_late[t, p] = sums[t, p]

    arrive([side for side in SIDES if side in ((0, 1), (-1, 1))])

    @pl.when(gy == 0)
    def _():
        far_late_y[...] = jnp.zeros_like(far_late_y)
        near_late_y[...] = jnp.zeros_like(near_late_y)

    @pl.when(gy > 0)
    def _():
        columns = cells[0:2, 2:8].reshape(12, 8, 128)
        for part, v in enumerate(multipoles(columns)):
            ln = slice(128 * part, 128 * part + 128)
            for y in range(2):
                for x in range(6):
                    first = v[6 * y + x - 2] if x >= 2 else zero_rows
                    far_y[y, x, :, ln] = pair(first, v[6 * y + x])
        for part, v in enumerate(neighbours(cells[1, 2:7])):
            ln = slice(128 * part, 128 * part + 128)
            for x in range(1, 5):
                first = v[x - 2] if x >= 2 else zero_rows
                near_y[x - 1, :, ln] = pair(first, v[x])
        late("y", far_y, near_y, far_late_y, near_late_y)

    arrive([side for side in SIDES if side in ((1, 0), (1, 1), (1, -1))])

    @pl.when(gx == 0)
    def _():
        far_late_x[...] = jnp.zeros_like(far_late_x)
        near_late_x[...] = jnp.zeros_like(near_late_x)

    @pl.when(gx > 0)
    def _():
        columns = cells[:, 0:2].reshape(16, 8, 128)
        for part, v in enumerate(multipoles(columns)):
            ln = slice(128 * part, 128 * part + 128)
            for x in range(2):
                for y in range(6):
                    far_x[x, y, :, ln] = pair(v[2 * y + x], v[2 * y + 4 + x])
        for part, v in enumerate(neighbours(cells[1:7, 1])):
            ln = slice(128 * part, 128 * part + 128)
            for y in range(4):
                near_x[y, :, ln] = pair(v[y], v[y + 2])
        late("x", far_x, near_x, far_late_x, near_late_x)

    def eight(value, i):
        return value[8 * i : 8 * i + 8]

    expansion = []
    for y in range(4):
        for x in range(4):
            value = eight(total_ref[y, x % 2], x // 2)
            if x < 2:
                value = value + far_late_x[x, y % 2, 8 * (y // 2) : 8 * (y // 2) + 8]
            if y < 2:
                value = value + far_late_y[y, x % 2, 8 * (x // 2) : 8 * (x // 2) + 8]
            expansion.append(value)
    distant = dot(jnp.concatenate(expansion, axis=0).astype(BF), l2p_pair)
    for y in range(4):
        for x in range(4):
            value = eight(distant, 4 * y + x) + eight(close_ref[...], 4 * y + 2 * (x % 2) + x // 2)
            if x == 0:
                value = value + eight(near_late_x[...], 2 * (y % 2) + y // 2)
            if y == 0:
                value = value + eight(near_late_y[...], 2 * (x % 2) + x // 2)
            for z in range(8):
                out[x, y : y + 1, 128 * z : 128 * z + 128] = value[z : z + 1]

    for k, (dx, dy) in enumerate(SIDES):
        @pl.when(present(dx, dy))
        def _():
            remote(k).wait_send()


def local(density, p2m_operator, m2l_table, near_table, l2p_operator):
    in_hbm = pl.BlockSpec(memory_space=pltpu.HBM)
    operands = [
        pltpu.with_memory_space_constraint(v, pltpu.HBM)
        for v in (density, p2m_operator.T, m2l_table, near_table, l2p_operator)
    ]
    return pl.pallas_call(
        kernel,
        out_shape=jax.ShapeDtypeStruct(density.shape, F32),
        in_specs=[in_hbm] * 5,
        out_specs=pl.BlockSpec(memory_space=pltpu.VMEM),
        scratch_shapes=[
            pltpu.VMEM((4, 4, 1024), BF),
            pltpu.VMEM((8, 8, 8, 128), BF),
            pltpu.VMEM((7, 7, 7, 56, 56), BF),
            pltpu.VMEM((3, 3, 3, 64, 64), BF),
            pltpu.VMEM((56, 64), BF),
            pltpu.VMEM((56, 64), BF),
            pltpu.VMEM((7, 7, 384, 128), BF),
            pltpu.VMEM((9, 256, 128), BF),
            pltpu.VMEM((8, 6, 16, 384), BF),
            pltpu.VMEM((7, 4, 16, 256), BF),
            pltpu.VMEM((2, 6, 16, 384), BF),
            pltpu.VMEM((2, 6, 16, 384), BF),
            pltpu.VMEM((4, 16, 256), BF),
            pltpu.VMEM((4, 16, 256), BF),
            pltpu.VMEM((4, 2, 16, 128), F32),
            pltpu.VMEM((128, 128), F32),
            pltpu.VMEM((2, 2, 16, 128), F32),
            pltpu.VMEM((2, 2, 16, 128), F32),
            pltpu.VMEM((32, 128), F32),
            pltpu.VMEM((32, 128), F32),
            pltpu.SemaphoreType.DMA((4,)),
            pltpu.SemaphoreType.DMA((7,)),
            pltpu.SemaphoreType.DMA((8,)),
            pltpu.SemaphoreType.DMA((8,)),
            pltpu.SemaphoreType.REGULAR,
        ],
        compiler_params=pltpu.CompilerParams(
            collective_id=0, has_side_effects=True, vmem_limit_bytes=32 * 1024 * 1024
        ),
    )(*operands)


def solution(mesh):
    placed = (P("gx", "gy", None), P(), P(), P(), P())
    return jax.shard_map(
        local, mesh=mesh, in_specs=placed, out_specs=P("gx", "gy", None), check_vma=False
    )
```

```python
import jax
import jax.numpy as jnp
from jax import lax
from jax.experimental import pallas as pl
from jax.experimental.pallas import tpu as pltpu
from jax.sharding import PartitionSpec as P

BF = jnp.bfloat16
F32 = jnp.float32
MESH = pl.DeviceIdType.MESH
HALO = 2
SIDES = [(1, 1), (0, 1), (1, 0), (1, -1), (-1, 1), (-1, 0), (0, -1), (-1, -1)]
LOWER = [(-1, 0), (0, -1), (-1, -1)]
SOURCE = {-1: slice(2, 4), 0: slice(2, 6), 1: slice(4, 6)}
RAW = {0: slice(0, 4), 1: slice(2, 4)}
TARGET = {-1: slice(6, 8), 0: slice(2, 6), 1: slice(0, 2)}


def near_offset(ox, oy):
    return 2 <= ox <= 4 and 2 <= oy <= 4


def chunks(ox, oy):
    return (0, 2) if near_offset(ox, oy) else (0, 1, 2)


def parities(offset):
    return tuple(p for p in (0, 1) if 0 <= offset - 1 + p <= 5)


def early_columns():
    return {0: ((1, 0),), 1: ((0, 0), (1, 1)), 2: ((0, 1),)}


def late_products(axis):
    classes = {}
    for ox in range(7):
        for oy in range(7):
            along, across = (ox, oy) if axis == "x" else (oy, ox)
            units = tuple(
                (t, s - t, p) for t, s in early_columns().get(along, ()) for p in parities(across)
            )
            if units:
                classes.setdefault(units, []).append((ox, oy))
    return classes


def dot(a, b):
    return jnp.dot(a, b, preferred_element_type=F32)


def widen(block):
    rows, lanes = block.shape
    block = jnp.concatenate([block, jnp.zeros((rows, 128 - lanes), BF)], axis=1)
    if rows < 64:
        block = jnp.concatenate([block, jnp.zeros((64 - rows, 128), BF)], axis=0)
    return block


def swap(block):
    return pltpu.roll(block, 64, 1)


def kernel(
    density, p2m_t, m2l, near, l2p, out,
    raw, cells, table, near_raw, p2m_raw, l2p_raw, weights, near_weights,
    far_rows, near_rows, far_x, far_y, near_x, near_y, total_ref, close_ref,
    far_late_x, far_late_y, near_late_x, near_late_y, raw_corner, raw_y, raw_x,
    in_sems, table_sems, send_sems, recv_sems, ready,
):
    raw_in = [raw_corner, raw_y, raw_x]
    gx, gy = lax.axis_index("gx"), lax.axis_index("gy")
    nx, ny = lax.axis_size("gx"), lax.axis_size("gy")

    def present(dx, dy):
        ok = None
        for d, g, n in ((dx, gx, nx), (dy, gy, ny)):
            if d:
                test = (g + d >= 0) & (g + d < n)
                ok = test if ok is None else ok & test
        return ok

    copies_in = [
        pltpu.make_async_copy(density, raw, in_sems.at[0]),
        pltpu.make_async_copy(near, near_raw, in_sems.at[1]),
        pltpu.make_async_copy(p2m_t, p2m_raw, in_sems.at[2]),
        pltpu.make_async_copy(l2p, l2p_raw, in_sems.at[3]),
    ]
    copies_in[0].start()
    barrier = pltpu.get_barrier_semaphore()

    def leads(dx, dy):
        return (gx + dx == 0) & (gy + dy == 0)

    def beside(dx, dy):
        return present(dx, dy) & jnp.logical_not(leads(dx, dy))

    count = jnp.int32(0)
    for dx, dy in SIDES:
        count = count + beside(dx, dy).astype(jnp.int32)

        @pl.when(present(dx, dy) & jnp.logical_not(leads(0, 0)))
        def _():
            pl.semaphore_signal(
                barrier, inc=1, device_id=(gx + dx, gy + dy), device_id_type=MESH
            )
    def remote(k):
        dx, dy = SIDES[k]
        return pltpu.make_async_remote_copy(
            src_ref=cells.at[SOURCE[dy], SOURCE[dx]],
            dst_ref=cells.at[TARGET[dy], TARGET[dx]],
            send_sem=send_sems.at[k],
            recv_sem=recv_sems.at[k],
            device_id=(gx + dx, gy + dy),
            device_id_type=MESH,
        )

    def straight(k):
        dx, dy = SIDES[k]
        xs, ys = RAW[dx], RAW[dy]
        return pltpu.make_async_remote_copy(
            src_ref=density.at[xs, ys],
            dst_ref=raw_in[k].at[...],
            send_sem=send_sems.at[k],
            recv_sem=recv_sems.at[k],
            device_id=(gx + dx, gy + dy),
            device_id_type=MESH,
        )

    @pl.when(leads(0, 0))
    def _():
        pl.semaphore_wait(barrier, count)
        for k, (dx, dy) in enumerate(SIDES):
            if (-dx, -dy) in LOWER:
                @pl.when(present(dx, dy))
                def _():
                    straight(k).start()
        for dx, dy in LOWER:
            @pl.when(present(-dx, -dy))
            def _():
                pl.semaphore_signal(
                    ready, inc=1, device_id=(gx - dx, gy - dy), device_id_type=MESH
                )

    for c in copies_in[1:]:
        c.start()
    table_copies = [
        pltpu.make_async_copy(m2l.at[i], table.at[i], table_sems.at[i]) for i in range(7)
    ]
    for c in table_copies:
        c.start()

    def take(block, y0, x0):
        block = block.astype(F32)
        for y in range(block.shape[1]):
            for x in range(block.shape[0]):
                tile = jnp.concatenate(
                    [block[x, y : y + 1, 128 * z : 128 * z + 128] for z in range(8)], axis=0
                )
                cells[y0 + y, x0 + x] = tile.astype(BF)

    for dx, dy in SIDES:
        @pl.when(jnp.logical_not(present(dx, dy)))
        def _():
            ys, xs = TARGET[-dy], TARGET[-dx]
            cells[ys, xs] = jnp.zeros((ys.stop - ys.start, xs.stop - xs.start, 8, 128), BF)

    copies_in[0].wait()
    take(raw[...], HALO, HALO)

    @pl.when(jnp.logical_not(leads(0, 0)))
    def _():
        pl.semaphore_wait(barrier, count)

    for k, (dx, dy) in enumerate(SIDES):
        @pl.when(beside(dx, dy) & jnp.logical_not(leads(0, 0)))
        def _():
            remote(k).start()

    def arrive(sides):
        for k, (dx, dy) in enumerate(SIDES):
            if (dx, dy) in sides:
                @pl.when(beside(-dx, -dy))
                def _():
                    remote(k).wait_recv()

                if (-dx, -dy) in LOWER:
                    @pl.when(leads(-dx, -dy))
                    def _():
                        straight(k).wait_recv()
                        ys, xs = TARGET[dy], TARGET[dx]
                        take(raw_in[k][...], ys.start, xs.start)

    for c in copies_in[1:]:
        c.wait()
    p2m_block = widen(p2m_raw[...])
    p2m = jnp.concatenate([p2m_block, swap(p2m_block)], axis=0)
    l2p_block = widen(l2p_raw[...])
    l2p_pair = jnp.concatenate([l2p_block, swap(l2p_block)], axis=0)
    low = lax.broadcasted_iota(jnp.int32, (64, 128), 1) < 64

    def build_near(i, carry):
        a, b, c = (widen(near_raw[i // 3, i % 3, k]) for k in range(3))
        near_weights[i, 0:64] = jnp.where(low, b, swap(a))
        near_weights[i, 64:128] = jnp.where(low, c, swap(b))
        near_weights[i, 128:192] = swap(c)
        near_weights[i, 192:256] = a
        return carry

    lax.fori_loop(0, 9, build_near, 0, unroll=9)

    for ox in range(7):
        table_copies[ox].wait()

        def build(oy, carry):
            blocks = [widen(table[ox, oy, k]) for k in range(7)]
            for k in range(6):
                weights[ox, oy, 64 * k : 64 * k + 64] = jnp.where(
                    low, blocks[k + 1], swap(blocks[k])
                )
            return carry

        lax.fori_loop(0, 7, build, 0, unroll=7)
        if 2 <= ox <= 4:
            def build_close(oy, carry):
                weights[ox, oy, 64:128] = swap(widen(table[ox, oy, 1]))
                weights[ox, oy, 256:320] = widen(table[ox, oy, 5])
                return carry

            lax.fori_loop(2, 5, build_close, 0, unroll=3)

    def far_weights(pairs):
        return jnp.concatenate(
            [
                weights[ox, oy, 128 * c : 128 * c + 128]
                for ox, oy in pairs
                for c in chunks(ox, oy)
            ],
            axis=0,
        )

    def shifted(v):
        row = lax.broadcasted_iota(jnp.int32, v.shape, 1)
        below = jnp.where(row == 0, 0.0, pltpu.roll(v, 1, 1))
        above = jnp.where(row == 7, 0.0, pltpu.roll(v, 7, 1))
        return below, v, above

    def multipoles(columns):
        n = columns.shape[0]
        m = lax.dot_general(
            columns.reshape(8 * n, 128), p2m, (((1,), (1,)), ((), ())),
            preferred_element_type=F32,
        )
        return shifted(m.reshape(n, 8, 128))

    def neighbours(columns):
        below, own_rows, above = shifted(columns.astype(F32))
        half = lax.broadcasted_iota(jnp.int32, own_rows.shape, 2) < 64
        return own_rows, jnp.where(half, above, below)

    def pair(a, b):
        return jnp.concatenate([a, b], axis=0).astype(BF)

    zero_rows = jnp.zeros((8, 128), F32)

    arrive(LOWER)
    far_rows[0:2] = jnp.zeros((2, 6, 16, 384), BF)
    near_rows[0] = jnp.zeros((4, 16, 256), BF)

    def spread(y, carry):
        columns = cells[y, 2:8]
        for part, v in enumerate(multipoles(columns)):
            ln = slice(128 * part, 128 * part + 128)
            for x in range(6):
                first = v[x - 2] if x >= 2 else zero_rows
                far_rows[y, x, :, ln] = pair(first, v[x])
        for part, v in enumerate(neighbours(columns[0:5])):
            ln = slice(128 * part, 128 * part + 128)
            for x in range(1, 5):
                first = v[x - 2] if x >= 2 else zero_rows
                near_rows[y - 1, x - 1, :, ln] = pair(first, v[x])
        return carry

    lax.fori_loop(2, 8, spread, 0, unroll=6)

    close = jnp.zeros((128, 128), F32)
    for dx in range(3):
        for dy in range(3):
            close += dot(
                near_rows[dy : dy + 4, dx : dx + 2].reshape(128, 256), near_weights[3 * dx + dy]
            )
    close_ref[...] = close

    def place(value, ys, pars):
        i = 0
        for y in ys:
            for par in pars:
                total_ref[y, par] += value[16 * i : 16 * i + 16]
                i += 1

    total_ref[...] = jnp.zeros_like(total_ref)
    for pars in ((0, 1), (1,), (0,)):
        for ys, oys in (((0, 1, 2, 3), range(1, 6)), ((1, 3), (0,)), ((0, 2), (6,))):
            acc = jnp.zeros((16 * len(ys) * len(pars), 128), F32)
            for ox in range(7):
                if parities(ox) != pars:
                    continue
                x0 = ox - 1 + pars[0]
                for oy in oys:
                    lhs = jnp.concatenate(
                        [
                            jnp.concatenate(
                                [
                                    far_rows[y + oy - 1, x0 : x0 + len(pars), :, 128 * c : 128 * c + 128]
                                    for y in ys
                                ],
                                axis=0,
                            ).reshape(16 * len(ys) * len(pars), 128)
                            for c in chunks(ox, oy)
                        ],
                        axis=1,
                    )
                    acc += dot(lhs, far_weights([(ox, oy)]))
            place(acc, ys, pars)

    for k, (dx, dy) in enumerate(SIDES):
        if (dx, dy) in LOWER:
            @pl.when(leads(dx, dy))
            def _():
                pl.semaphore_wait(ready, 1)
                remote(k).start()

    def late(axis, far_ref, near_ref, far_late, near_late):
        places = (0, 1, 2) if axis == "x" else (0, 3, 6)
        lhs = jnp.concatenate([near_ref[d : d + 2].reshape(32, 256) for d in range(3)], axis=1)
        rhs = jnp.concatenate([near_weights[i] for i in places], axis=0)
        near_late[...] = dot(lhs, rhs)
        sums = {}
        for units, pairs in late_products(axis).items():
            columns = []
            for ox, oy in pairs:
                across = oy if axis == "x" else ox
                for c in chunks(ox, oy):
                    ln = slice(128 * c, 128 * c + 128)
                    columns.append(
                        jnp.concatenate(
                            [far_ref[t + d, across - 1 + p, :, ln] for t, d, p in units], axis=0
                        )
                    )
            value = dot(jnp.concatenate(columns, axis=1), far_weights(pairs))
            for i, (t, _, p) in enumerate(units):
                part = value[16 * i : 16 * i + 16]
                sums[t, p] = sums[t, p] + part if (t, p) in sums else part
        for t, p in sums:
            far_late[t, p] = sums[t, p]

    arrive([side for side in SIDES if side in ((0, 1), (-1, 1))])

    @pl.when(gy == 0)
    def _():
        far_late_y[...] = jnp.zeros_like(far_late_y)
        near_late_y[...] = jnp.zeros_like(near_late_y)

    @pl.when(gy > 0)
    def _():
        columns = cells[0:2, 2:8].reshape(12, 8, 128)
        for part, v in enumerate(multipoles(columns)):
            ln = slice(128 * part, 128 * part + 128)
            for y in range(2):
                for x in range(6):
                    first = v[6 * y + x - 2] if x >= 2 else zero_rows
                    far_y[y, x, :, ln] = pair(first, v[6 * y + x])
        for part, v in enumerate(neighbours(cells[1, 2:7])):
            ln = slice(128 * part, 128 * part + 128)
            for x in range(1, 5):
                first = v[x - 2] if x >= 2 else zero_rows
                near_y[x - 1, :, ln] = pair(first, v[x])
        late("y", far_y, near_y, far_late_y, near_late_y)

    arrive([side for side in SIDES if side in ((1, 0), (1, 1), (1, -1))])

    @pl.when(gx == 0)
    def _():
        far_late_x[...] = jnp.zeros_like(far_late_x)
        near_late_x[...] = jnp.zeros_like(near_late_x)

    @pl.when(gx > 0)
    def _():
        columns = cells[:, 0:2].reshape(16, 8, 128)
        for part, v in enumerate(multipoles(columns)):
            ln = slice(128 * part, 128 * part + 128)
            for x in range(2):
                for y in range(6):
                    far_x[x, y, :, ln] = pair(v[2 * y + x], v[2 * y + 4 + x])
        for part, v in enumerate(neighbours(cells[1:7, 1])):
            ln = slice(128 * part, 128 * part + 128)
            for y in range(4):
                near_x[y, :, ln] = pair(v[y], v[y + 2])
        late("x", far_x, near_x, far_late_x, near_late_x)

    def eight(value, i):
        return value[8 * i : 8 * i + 8]

    expansion = []
    for y in range(4):
        for x in range(4):
            value = eight(total_ref[y, x % 2], x // 2)
            if x < 2:
                value = value + far_late_x[x, y % 2, 8 * (y // 2) : 8 * (y // 2) + 8]
            if y < 2:
                value = value + far_late_y[y, x % 2, 8 * (x // 2) : 8 * (x // 2) + 8]
            expansion.append(value)
    distant = dot(jnp.concatenate(expansion, axis=0).astype(BF), l2p_pair)
    for y in range(4):
        for x in range(4):
            value = eight(distant, 4 * y + x) + eight(close_ref[...], 4 * y + 2 * (x % 2) + x // 2)
            if x == 0:
                value = value + eight(near_late_x[...], 2 * (y % 2) + y // 2)
            if y == 0:
                value = value + eight(near_late_y[...], 2 * (x % 2) + x // 2)
            for z in range(8):
                out[x, y : y + 1, 128 * z : 128 * z + 128] = value[z : z + 1]

    for k, (dx, dy) in enumerate(SIDES):
        @pl.when(present(dx, dy) & jnp.logical_not(leads(0, 0)))
        def _():
            remote(k).wait_send()

        if (-dx, -dy) in LOWER:
            @pl.when(present(dx, dy) & leads(0, 0))
            def _():
                straight(k).wait_send()


def local(density, p2m_operator, m2l_table, near_table, l2p_operator):
    in_hbm = pl.BlockSpec(memory_space=pltpu.HBM)
    operands = [
        pltpu.with_memory_space_constraint(v, pltpu.HBM)
        for v in (density, p2m_operator.T, m2l_table, near_table, l2p_operator)
    ]
    return pl.pallas_call(
        kernel,
        out_shape=jax.ShapeDtypeStruct(density.shape, F32),
        in_specs=[in_hbm] * 5,
        out_specs=pl.BlockSpec(memory_space=pltpu.VMEM),
        scratch_shapes=[
            pltpu.VMEM((4, 4, 1024), BF),
            pltpu.VMEM((8, 8, 8, 128), BF),
            pltpu.VMEM((7, 7, 7, 56, 56), BF),
            pltpu.VMEM((3, 3, 3, 64, 64), BF),
            pltpu.VMEM((56, 64), BF),
            pltpu.VMEM((56, 64), BF),
            pltpu.VMEM((7, 7, 384, 128), BF),
            pltpu.VMEM((9, 256, 128), BF),
            pltpu.VMEM((8, 6, 16, 384), BF),
            pltpu.VMEM((7, 4, 16, 256), BF),
            pltpu.VMEM((2, 6, 16, 384), BF),
            pltpu.VMEM((2, 6, 16, 384), BF),
            pltpu.VMEM((4, 16, 256), BF),
            pltpu.VMEM((4, 16, 256), BF),
            pltpu.VMEM((4, 2, 16, 128), F32),
            pltpu.VMEM((128, 128), F32),
            pltpu.VMEM((2, 2, 16, 128), F32),
            pltpu.VMEM((2, 2, 16, 128), F32),
            pltpu.VMEM((32, 128), F32),
            pltpu.VMEM((32, 128), F32),
            pltpu.VMEM((2, 2, 1024), BF),
            pltpu.VMEM((4, 2, 1024), BF),
            pltpu.VMEM((2, 4, 1024), BF),
            pltpu.SemaphoreType.DMA((4,)),
            pltpu.SemaphoreType.DMA((7,)),
            pltpu.SemaphoreType.DMA((8,)),
            pltpu.SemaphoreType.DMA((8,)),
            pltpu.SemaphoreType.REGULAR,
        ],
        compiler_params=pltpu.CompilerParams(
            collective_id=0, has_side_effects=True, vmem_limit_bytes=32 * 1024 * 1024
        ),
    )(*operands)


def solution(mesh):
    placed = (P("gx", "gy", None), P(), P(), P(), P())
    return jax.shard_map(
        local, mesh=mesh, in_specs=placed, out_specs=P("gx", "gy", None), check_vma=False
    )
```

```python
import jax
import jax.numpy as jnp
from jax import lax
from jax.experimental import pallas as pl
from jax.experimental.pallas import tpu as pltpu
from jax.sharding import PartitionSpec as P

BF = jnp.bfloat16
F32 = jnp.float32
MESH = pl.DeviceIdType.MESH
HALO = 2
SIDES = [(1, 1), (0, 1), (1, 0), (1, -1), (-1, 1), (-1, 0), (0, -1), (-1, -1)]
LOWER = [(-1, 0), (0, -1), (-1, -1)]
SOURCE = {-1: slice(2, 4), 0: slice(2, 6), 1: slice(4, 6)}
RAW = {0: slice(0, 4), 1: slice(2, 4)}
TARGET = {-1: slice(6, 8), 0: slice(2, 6), 1: slice(0, 2)}


def near_offset(ox, oy):
    return 2 <= ox <= 4 and 2 <= oy <= 4


def chunks(ox, oy):
    return (0, 2) if near_offset(ox, oy) else (0, 1, 2)


def parities(offset):
    return tuple(p for p in (0, 1) if 0 <= offset - 1 + p <= 5)


def early_columns():
    return {0: ((1, 0),), 1: ((0, 0), (1, 1)), 2: ((0, 1),)}


def late_products(axis):
    classes = {}
    for ox in range(7):
        for oy in range(7):
            along, across = (ox, oy) if axis == "x" else (oy, ox)
            units = tuple(
                (t, s - t, p) for t, s in early_columns().get(along, ()) for p in parities(across)
            )
            if units:
                classes.setdefault(units, []).append((ox, oy))
    return classes


def dot(a, b):
    return jnp.dot(a, b, preferred_element_type=F32)


def widen(block):
    rows, lanes = block.shape
    block = jnp.concatenate([block, jnp.zeros((rows, 128 - lanes), BF)], axis=1)
    if rows < 64:
        block = jnp.concatenate([block, jnp.zeros((64 - rows, 128), BF)], axis=0)
    return block


def swap(block):
    return pltpu.roll(block, 64, 1)


def kernel(
    density, p2m_t, m2l, near, l2p, out,
    raw, cells, table, near_raw, p2m_raw, l2p_raw, weights, near_weights,
    far_rows, near_rows, far_x, far_y, near_x, near_y, total_ref, close_ref,
    far_late_x, far_late_y, near_late_x, near_late_y, raw_corner, raw_y, raw_x,
    in_sems, table_sems, send_sems, recv_sems, ready,
):
    raw_in = [raw_corner, raw_y, raw_x]
    gx, gy = lax.axis_index("gx"), lax.axis_index("gy")
    nx, ny = lax.axis_size("gx"), lax.axis_size("gy")

    def present(dx, dy):
        ok = None
        for d, g, n in ((dx, gx, nx), (dy, gy, ny)):
            if d:
                test = (g + d >= 0) & (g + d < n)
                ok = test if ok is None else ok & test
        return ok

    copies_in = [
        pltpu.make_async_copy(density, raw, in_sems.at[0]),
        pltpu.make_async_copy(near, near_raw, in_sems.at[1]),
        pltpu.make_async_copy(p2m_t, p2m_raw, in_sems.at[2]),
        pltpu.make_async_copy(l2p, l2p_raw, in_sems.at[3]),
    ]
    barrier = pltpu.get_barrier_semaphore()

    def leads(dx, dy):
        return (gx + dx == 0) & (gy + dy == 0)

    def beside(dx, dy):
        return present(dx, dy) & jnp.logical_not(leads(dx, dy))

    @pl.when(jnp.logical_not(leads(0, 0)))
    def _():
        for dx, dy in SIDES:
            @pl.when(present(dx, dy))
            def _():
                pl.semaphore_signal(
                    barrier, inc=1, device_id=(gx + dx, gy + dy), device_id_type=MESH
                )

    def remote(k):
        dx, dy = SIDES[k]
        return pltpu.make_async_remote_copy(
            src_ref=cells.at[SOURCE[dy], SOURCE[dx]],
            dst_ref=cells.at[TARGET[dy], TARGET[dx]],
            send_sem=send_sems.at[k],
            recv_sem=recv_sems.at[k],
            device_id=(gx + dx, gy + dy),
            device_id_type=MESH,
        )

    def straight(k):
        dx, dy = SIDES[k]
        xs, ys = RAW[dx], RAW[dy]
        return pltpu.make_async_remote_copy(
            src_ref=density.at[xs, ys],
            dst_ref=raw_in[k].at[...],
            send_sem=send_sems.at[k],
            recv_sem=recv_sems.at[k],
            device_id=(gx + dx, gy + dy),
            device_id_type=MESH,
        )

    @pl.when(leads(0, 0))
    def _():
        pl.semaphore_wait(
            barrier, sum(present(-dx, -dy).astype(jnp.int32) for dx, dy in LOWER)
        )
        for k, (dx, dy) in enumerate(SIDES):
            if (-dx, -dy) in LOWER:
                @pl.when(present(dx, dy))
                def _():
                    straight(k).start()
        for dx, dy in LOWER:
            @pl.when(present(-dx, -dy))
            def _():
                pl.semaphore_signal(
                    ready, inc=1, device_id=(gx - dx, gy - dy), device_id_type=MESH
                )

    for c in copies_in:
        c.start()
    table_copies = [
        pltpu.make_async_copy(m2l.at[i], table.at[i], table_sems.at[i]) for i in range(7)
    ]
    for c in table_copies:
        c.start()

    def take(block, y0, x0):
        block = block.astype(F32)
        for y in range(block.shape[1]):
            for x in range(block.shape[0]):
                tile = jnp.concatenate(
                    [block[x, y : y + 1, 128 * z : 128 * z + 128] for z in range(8)], axis=0
                )
                cells[y0 + y, x0 + x] = tile.astype(BF)

    for dx, dy in SIDES:
        @pl.when(jnp.logical_not(present(dx, dy)))
        def _():
            ys, xs = TARGET[-dy], TARGET[-dx]
            cells[ys, xs] = jnp.zeros((ys.stop - ys.start, xs.stop - xs.start, 8, 128), BF)

    copies_in[0].wait()
    take(raw[...], HALO, HALO)

    def arrive(sides):
        for k, (dx, dy) in enumerate(SIDES):
            if (dx, dy) in sides:
                @pl.when(beside(-dx, -dy))
                def _():
                    remote(k).wait_recv()

                if (-dx, -dy) in LOWER:
                    @pl.when(leads(-dx, -dy))
                    def _():
                        straight(k).wait_recv()
                        ys, xs = TARGET[dy], TARGET[dx]
                        take(raw_in[k][...], ys.start, xs.start)

    for c in copies_in[1:]:
        c.wait()
    p2m_block = widen(p2m_raw[...])
    p2m = jnp.concatenate([p2m_block, swap(p2m_block)], axis=0)
    l2p_block = widen(l2p_raw[...])
    l2p_pair = jnp.concatenate([l2p_block, swap(l2p_block)], axis=0)
    low = lax.broadcasted_iota(jnp.int32, (64, 128), 1) < 64

    def build_near(i, carry):
        a, b, c = (widen(near_raw[i // 3, i % 3, k]) for k in range(3))
        near_weights[i, 0:64] = jnp.where(low, b, swap(a))
        near_weights[i, 64:128] = jnp.where(low, c, swap(b))
        near_weights[i, 128:192] = swap(c)
        near_weights[i, 192:256] = a
        return carry

    lax.fori_loop(0, 9, build_near, 0, unroll=9)

    @pl.when(jnp.logical_not(leads(0, 0)))
    def _():
        pl.semaphore_wait(
            barrier, sum(beside(dx, dy).astype(jnp.int32) for dx, dy in SIDES)
        )

    for k, (dx, dy) in enumerate(SIDES):
        @pl.when(beside(dx, dy) & jnp.logical_not(leads(0, 0)))
        def _():
            remote(k).start()

    for ox in range(7):
        table_copies[ox].wait()

        def build(oy, carry):
            blocks = [widen(table[ox, oy, k]) for k in range(7)]
            for k in range(6):
                weights[ox, oy, 64 * k : 64 * k + 64] = jnp.where(
                    low, blocks[k + 1], swap(blocks[k])
                )
            return carry

        lax.fori_loop(0, 7, build, 0, unroll=7)
        if 2 <= ox <= 4:
            def build_close(oy, carry):
                weights[ox, oy, 64:128] = swap(widen(table[ox, oy, 1]))
                weights[ox, oy, 256:320] = widen(table[ox, oy, 5])
                return carry

            lax.fori_loop(2, 5, build_close, 0, unroll=3)

    def far_weights(pairs):
        return jnp.concatenate(
            [
                weights[ox, oy, 128 * c : 128 * c + 128]
                for ox, oy in pairs
                for c in chunks(ox, oy)
            ],
            axis=0,
        )

    def shifted(v):
        row = lax.broadcasted_iota(jnp.int32, v.shape, 1)
        below = jnp.where(row == 0, 0.0, pltpu.roll(v, 1, 1))
        above = jnp.where(row == 7, 0.0, pltpu.roll(v, 7, 1))
        return below, v, above

    def multipoles(columns):
        n = columns.shape[0]
        m = lax.dot_general(
            columns.reshape(8 * n, 128), p2m, (((1,), (1,)), ((), ())),
            preferred_element_type=F32,
        )
        return shifted(m.reshape(n, 8, 128))

    def neighbours(columns):
        below, own_rows, above = shifted(columns.astype(F32))
        half = lax.broadcasted_iota(jnp.int32, own_rows.shape, 2) < 64
        return own_rows, jnp.where(half, above, below)

    def pair(a, b):
        return jnp.concatenate([a, b], axis=0).astype(BF)

    zero_rows = jnp.zeros((8, 128), F32)

    arrive(LOWER)
    far_rows[0:2] = jnp.zeros((2, 6, 16, 384), BF)
    near_rows[0] = jnp.zeros((4, 16, 256), BF)

    def spread(y, carry):
        columns = cells[y, 2:8]
        for part, v in enumerate(multipoles(columns)):
            ln = slice(128 * part, 128 * part + 128)
            for x in range(6):
                first = v[x - 2] if x >= 2 else zero_rows
                far_rows[y, x, :, ln] = pair(first, v[x])
        for part, v in enumerate(neighbours(columns[0:5])):
            ln = slice(128 * part, 128 * part + 128)
            for x in range(1, 5):
                first = v[x - 2] if x >= 2 else zero_rows
                near_rows[y - 1, x - 1, :, ln] = pair(first, v[x])
        return carry

    lax.fori_loop(2, 8, spread, 0, unroll=6)

    close = jnp.zeros((128, 128), F32)
    for dx in range(3):
        for dy in range(3):
            close += dot(
                near_rows[dy : dy + 4, dx : dx + 2].reshape(128, 256), near_weights[3 * dx + dy]
            )
    close_ref[...] = close

    def place(value, ys, pars):
        i = 0
        for y in ys:
            for par in pars:
                total_ref[y, par] += value[16 * i : 16 * i + 16]
                i += 1

    total_ref[...] = jnp.zeros_like(total_ref)
    for pars in ((0, 1), (1,), (0,)):
        for ys, oys in (((0, 1, 2, 3), range(1, 6)), ((1, 3), (0,)), ((0, 2), (6,))):
            acc = jnp.zeros((16 * len(ys) * len(pars), 128), F32)
            for ox in range(7):
                if parities(ox) != pars:
                    continue
                x0 = ox - 1 + pars[0]
                for oy in oys:
                    lhs = jnp.concatenate(
                        [
                            jnp.concatenate(
                                [
                                    far_rows[y + oy - 1, x0 : x0 + len(pars), :, 128 * c : 128 * c + 128]
                                    for y in ys
                                ],
                                axis=0,
                            ).reshape(16 * len(ys) * len(pars), 128)
                            for c in chunks(ox, oy)
                        ],
                        axis=1,
                    )
                    acc += dot(lhs, far_weights([(ox, oy)]))
            place(acc, ys, pars)

    for k, (dx, dy) in enumerate(SIDES):
        if (dx, dy) in LOWER:
            @pl.when(leads(dx, dy))
            def _():
                pl.semaphore_wait(ready, 1)
                remote(k).start()

    def late(axis, far_ref, near_ref, far_late, near_late):
        places = (0, 1, 2) if axis == "x" else (0, 3, 6)
        lhs = jnp.concatenate([near_ref[d : d + 2].reshape(32, 256) for d in range(3)], axis=1)
        rhs = jnp.concatenate([near_weights[i] for i in places], axis=0)
        near_late[...] = dot(lhs, rhs)
        sums = {}
        for units, pairs in late_products(axis).items():
            columns = []
            for ox, oy in pairs:
                across = oy if axis == "x" else ox
                for c in chunks(ox, oy):
                    ln = slice(128 * c, 128 * c + 128)
                    columns.append(
                        jnp.concatenate(
                            [far_ref[t + d, across - 1 + p, :, ln] for t, d, p in units], axis=0
                        )
                    )
            value = dot(jnp.concatenate(columns, axis=1), far_weights(pairs))
            for i, (t, _, p) in enumerate(units):
                part = value[16 * i : 16 * i + 16]
                sums[t, p] = sums[t, p] + part if (t, p) in sums else part
        for t, p in sums:
            far_late[t, p] = sums[t, p]

    arrive([side for side in SIDES if side in ((0, 1), (-1, 1))])

    @pl.when(gy == 0)
    def _():
        far_late_y[...] = jnp.zeros_like(far_late_y)
        near_late_y[...] = jnp.zeros_like(near_late_y)

    @pl.when(gy > 0)
    def _():
        columns = cells[0:2, 2:8].reshape(12, 8, 128)
        for part, v in enumerate(multipoles(columns)):
            ln = slice(128 * part, 128 * part + 128)
            for y in range(2):
                for x in range(6):
                    first = v[6 * y + x - 2] if x >= 2 else zero_rows
                    far_y[y, x, :, ln] = pair(first, v[6 * y + x])
        for part, v in enumerate(neighbours(cells[1, 2:7])):
            ln = slice(128 * part, 128 * part + 128)
            for x in range(1, 5):
                first = v[x - 2] if x >= 2 else zero_rows
                near_y[x - 1, :, ln] = pair(first, v[x])
        late("y", far_y, near_y, far_late_y, near_late_y)

    arrive([side for side in SIDES if side in ((1, 0), (1, 1), (1, -1))])

    @pl.when(gx == 0)
    def _():
        far_late_x[...] = jnp.zeros_like(far_late_x)
        near_late_x[...] = jnp.zeros_like(near_late_x)

    @pl.when(gx > 0)
    def _():
        columns = cells[:, 0:2].reshape(16, 8, 128)
        for part, v in enumerate(multipoles(columns)):
            ln = slice(128 * part, 128 * part + 128)
            for x in range(2):
                for y in range(6):
                    far_x[x, y, :, ln] = pair(v[2 * y + x], v[2 * y + 4 + x])
        for part, v in enumerate(neighbours(cells[1:7, 1])):
            ln = slice(128 * part, 128 * part + 128)
            for y in range(4):
                near_x[y, :, ln] = pair(v[y], v[y + 2])
        late("x", far_x, near_x, far_late_x, near_late_x)

    def eight(value, i):
        return value[8 * i : 8 * i + 8]

    expansion = []
    for y in range(4):
        for x in range(4):
            value = eight(total_ref[y, x % 2], x // 2)
            if x < 2:
                value = value + far_late_x[x, y % 2, 8 * (y // 2) : 8 * (y // 2) + 8]
            if y < 2:
                value = value + far_late_y[y, x % 2, 8 * (x // 2) : 8 * (x // 2) + 8]
            expansion.append(value)
    distant = dot(jnp.concatenate(expansion, axis=0).astype(BF), l2p_pair)
    for y in range(4):
        for x in range(4):
            value = eight(distant, 4 * y + x) + eight(close_ref[...], 4 * y + 2 * (x % 2) + x // 2)
            if x == 0:
                value = value + eight(near_late_x[...], 2 * (y % 2) + y // 2)
            if y == 0:
                value = value + eight(near_late_y[...], 2 * (x % 2) + x // 2)
            for z in range(8):
                out[x, y : y + 1, 128 * z : 128 * z + 128] = value[z : z + 1]

    for k, (dx, dy) in enumerate(SIDES):
        @pl.when(present(dx, dy) & jnp.logical_not(leads(0, 0)))
        def _():
            remote(k).wait_send()

        if (-dx, -dy) in LOWER:
            @pl.when(present(dx, dy) & leads(0, 0))
            def _():
                straight(k).wait_send()


def local(density, p2m_operator, m2l_table, near_table, l2p_operator):
    in_hbm = pl.BlockSpec(memory_space=pltpu.HBM)
    operands = [
        pltpu.with_memory_space_constraint(v, pltpu.HBM)
        for v in (density, p2m_operator.T, m2l_table, near_table, l2p_operator)
    ]
    return pl.pallas_call(
        kernel,
        out_shape=jax.ShapeDtypeStruct(density.shape, F32),
        in_specs=[in_hbm] * 5,
        out_specs=pl.BlockSpec(memory_space=pltpu.VMEM),
        scratch_shapes=[
            pltpu.VMEM((4, 4, 1024), BF),
            pltpu.VMEM((8, 8, 8, 128), BF),
            pltpu.VMEM((7, 7, 7, 56, 56), BF),
            pltpu.VMEM((3, 3, 3, 64, 64), BF),
            pltpu.VMEM((56, 64), BF),
            pltpu.VMEM((56, 64), BF),
            pltpu.VMEM((7, 7, 384, 128), BF),
            pltpu.VMEM((9, 256, 128), BF),
            pltpu.VMEM((8, 6, 16, 384), BF),
            pltpu.VMEM((7, 4, 16, 256), BF),
            pltpu.VMEM((2, 6, 16, 384), BF),
            pltpu.VMEM((2, 6, 16, 384), BF),
            pltpu.VMEM((4, 16, 256), BF),
            pltpu.VMEM((4, 16, 256), BF),
            pltpu.VMEM((4, 2, 16, 128), F32),
            pltpu.VMEM((128, 128), F32),
            pltpu.VMEM((2, 2, 16, 128), F32),
            pltpu.VMEM((2, 2, 16, 128), F32),
            pltpu.VMEM((32, 128), F32),
            pltpu.VMEM((32, 128), F32),
            pltpu.VMEM((2, 2, 1024), BF),
            pltpu.VMEM((4, 2, 1024), BF),
            pltpu.VMEM((2, 4, 1024), BF),
            pltpu.SemaphoreType.DMA((4,)),
            pltpu.SemaphoreType.DMA((7,)),
            pltpu.SemaphoreType.DMA((8,)),
            pltpu.SemaphoreType.DMA((8,)),
            pltpu.SemaphoreType.REGULAR,
        ],
        compiler_params=pltpu.CompilerParams(
            collective_id=0, has_side_effects=True, vmem_limit_bytes=32 * 1024 * 1024
        ),
    )(*operands)


def solution(mesh):
    placed = (P("gx", "gy", None), P(), P(), P(), P())
    return jax.shard_map(
        local, mesh=mesh, in_specs=placed, out_specs=P("gx", "gy", None), check_vma=False
    )
```

```python
import jax
import jax.numpy as jnp
from jax import lax
from jax.experimental import pallas as pl
from jax.experimental.pallas import tpu as pltpu
from jax.sharding import PartitionSpec as P

BF = jnp.bfloat16
F32 = jnp.float32
MESH = pl.DeviceIdType.MESH
HALO = 2
SIDES = [(1, 1), (0, 1), (1, 0), (1, -1), (-1, 1), (-1, 0), (0, -1), (-1, -1)]
LOWER = [(-1, 0), (0, -1), (-1, -1)]
SOURCE = {-1: slice(2, 4), 0: slice(2, 6), 1: slice(4, 6)}
RAW = {0: slice(0, 4), 1: slice(2, 4)}
TARGET = {-1: slice(6, 8), 0: slice(2, 6), 1: slice(0, 2)}


def near_offset(ox, oy):
    return 2 <= ox <= 4 and 2 <= oy <= 4


def chunks(ox, oy):
    return (0, 2) if near_offset(ox, oy) else (0, 1, 2)


def parities(offset):
    return tuple(p for p in (0, 1) if 0 <= offset - 1 + p <= 5)


def early_columns():
    return {0: ((1, 0),), 1: ((0, 0), (1, 1)), 2: ((0, 1),)}


def late_products(axis):
    classes = {}
    for ox in range(7):
        for oy in range(7):
            along, across = (ox, oy) if axis == "x" else (oy, ox)
            units = tuple(
                (t, s - t, p) for t, s in early_columns().get(along, ()) for p in parities(across)
            )
            if units:
                classes.setdefault(units, []).append((ox, oy))
    return classes


def dot(a, b):
    return jnp.dot(a, b, preferred_element_type=F32)


def widen(block):
    rows, lanes = block.shape
    block = jnp.concatenate([block, jnp.zeros((rows, 128 - lanes), BF)], axis=1)
    if rows < 64:
        block = jnp.concatenate([block, jnp.zeros((64 - rows, 128), BF)], axis=0)
    return block


def swap(block):
    return pltpu.roll(block, 64, 1)


def kernel(
    density, p2m_t, m2l, near, l2p, out,
    raw, cells, table, near_raw, p2m_raw, l2p_raw, weights, near_weights,
    far_rows, near_rows, far_x, far_y, near_x, near_y, total_ref, close_ref,
    far_late_x, far_late_y, near_late_x, near_late_y, raw_corner, raw_y, raw_x,
    in_sems, send_sems, recv_sems, ready,
):
    raw_in = [raw_corner, raw_y, raw_x]
    gx, gy = lax.axis_index("gx"), lax.axis_index("gy")
    nx, ny = lax.axis_size("gx"), lax.axis_size("gy")

    def present(dx, dy):
        ok = None
        for d, g, n in ((dx, gx, nx), (dy, gy, ny)):
            if d:
                test = (g + d >= 0) & (g + d < n)
                ok = test if ok is None else ok & test
        return ok

    copies_in = [
        pltpu.make_async_copy(density, raw, in_sems.at[0]),
        pltpu.make_async_copy(near, near_raw, in_sems.at[1]),
        pltpu.make_async_copy(p2m_t, p2m_raw, in_sems.at[2]),
        pltpu.make_async_copy(l2p, l2p_raw, in_sems.at[3]),
    ]
    barrier = pltpu.get_barrier_semaphore()

    def leads(dx, dy):
        return (gx + dx == 0) & (gy + dy == 0)

    def beside(dx, dy):
        return present(dx, dy) & jnp.logical_not(leads(dx, dy))

    @pl.when(jnp.logical_not(leads(0, 0)))
    def _():
        for dx, dy in SIDES:
            @pl.when(present(dx, dy))
            def _():
                pl.semaphore_signal(
                    barrier, inc=1, device_id=(gx + dx, gy + dy), device_id_type=MESH
                )

    def remote(k):
        dx, dy = SIDES[k]
        return pltpu.make_async_remote_copy(
            src_ref=cells.at[SOURCE[dy], SOURCE[dx]],
            dst_ref=cells.at[TARGET[dy], TARGET[dx]],
            send_sem=send_sems.at[k],
            recv_sem=recv_sems.at[k],
            device_id=(gx + dx, gy + dy),
            device_id_type=MESH,
        )

    def straight(k):
        dx, dy = SIDES[k]
        xs, ys = RAW[dx], RAW[dy]
        return pltpu.make_async_remote_copy(
            src_ref=density.at[xs, ys],
            dst_ref=raw_in[k].at[...],
            send_sem=send_sems.at[k],
            recv_sem=recv_sems.at[k],
            device_id=(gx + dx, gy + dy),
            device_id_type=MESH,
        )

    @pl.when(leads(0, 0))
    def _():
        pl.semaphore_wait(
            barrier, sum(present(-dx, -dy).astype(jnp.int32) for dx, dy in LOWER)
        )
        for k, (dx, dy) in enumerate(SIDES):
            if (-dx, -dy) in LOWER:
                @pl.when(present(dx, dy))
                def _():
                    straight(k).start()
        for dx, dy in LOWER:
            @pl.when(present(-dx, -dy))
            def _():
                pl.semaphore_signal(
                    ready, inc=1, device_id=(gx - dx, gy - dy), device_id_type=MESH
                )

    for c in copies_in:
        c.start()
    table_copy = pltpu.make_async_copy(m2l, table, in_sems.at[4])
    table_copy.start()

    def take(block, y0, x0):
        block = block.astype(F32)
        for y in range(block.shape[1]):
            for x in range(block.shape[0]):
                tile = jnp.concatenate(
                    [block[x, y : y + 1, 128 * z : 128 * z + 128] for z in range(8)], axis=0
                )
                cells[y0 + y, x0 + x] = tile.astype(BF)

    for dx, dy in SIDES:
        @pl.when(jnp.logical_not(present(dx, dy)))
        def _():
            ys, xs = TARGET[-dy], TARGET[-dx]
            cells[ys, xs] = jnp.zeros((ys.stop - ys.start, xs.stop - xs.start, 8, 128), BF)

    copies_in[0].wait()
    take(raw[...], HALO, HALO)

    def arrive(sides):
        for k, (dx, dy) in enumerate(SIDES):
            if (dx, dy) in sides:
                @pl.when(beside(-dx, -dy))
                def _():
                    remote(k).wait_recv()

                if (-dx, -dy) in LOWER:
                    @pl.when(leads(-dx, -dy))
                    def _():
                        straight(k).wait_recv()
                        ys, xs = TARGET[dy], TARGET[dx]
                        take(raw_in[k][...], ys.start, xs.start)

    for c in copies_in[1:]:
        c.wait()
    p2m_block = widen(p2m_raw[...])
    p2m = jnp.concatenate([p2m_block, swap(p2m_block)], axis=0)
    l2p_block = widen(l2p_raw[...])
    l2p_pair = jnp.concatenate([l2p_block, swap(l2p_block)], axis=0)
    low = lax.broadcasted_iota(jnp.int32, (64, 128), 1) < 64

    def build_near(i, carry):
        a, b, c = (widen(near_raw[i // 3, i % 3, k]) for k in range(3))
        near_weights[i, 0:64] = jnp.where(low, b, swap(a))
        near_weights[i, 64:128] = jnp.where(low, c, swap(b))
        near_weights[i, 128:192] = swap(c)
        near_weights[i, 192:256] = a
        return carry

    lax.fori_loop(0, 9, build_near, 0, unroll=9)

    @pl.when(jnp.logical_not(leads(0, 0)))
    def _():
        pl.semaphore_wait(
            barrier, sum(beside(dx, dy).astype(jnp.int32) for dx, dy in SIDES)
        )

    for k, (dx, dy) in enumerate(SIDES):
        @pl.when(beside(dx, dy) & jnp.logical_not(leads(0, 0)))
        def _():
            remote(k).start()

    table_copy.wait()
    for ox in range(7):
        def build(oy, carry):
            blocks = [widen(table[ox, oy, k]) for k in range(7)]
            for k in range(6):
                weights[ox, oy, 64 * k : 64 * k + 64] = jnp.where(
                    low, blocks[k + 1], swap(blocks[k])
                )
            return carry

        lax.fori_loop(0, 7, build, 0, unroll=7)
        if 2 <= ox <= 4:
            def build_close(oy, carry):
                weights[ox, oy, 64:128] = swap(widen(table[ox, oy, 1]))
                weights[ox, oy, 256:320] = widen(table[ox, oy, 5])
                return carry

            lax.fori_loop(2, 5, build_close, 0, unroll=3)

    def far_weights(pairs):
        return jnp.concatenate(
            [
                weights[ox, oy, 128 * c : 128 * c + 128]
                for ox, oy in pairs
                for c in chunks(ox, oy)
            ],
            axis=0,
        )

    def shifted(v):
        row = lax.broadcasted_iota(jnp.int32, v.shape, 1)
        below = jnp.where(row == 0, 0.0, pltpu.roll(v, 1, 1))
        above = jnp.where(row == 7, 0.0, pltpu.roll(v, 7, 1))
        return below, v, above

    def multipoles(columns):
        n = columns.shape[0]
        m = lax.dot_general(
            columns.reshape(8 * n, 128), p2m, (((1,), (1,)), ((), ())),
            preferred_element_type=F32,
        )
        return shifted(m.reshape(n, 8, 128))

    def neighbours(columns):
        below, own_rows, above = shifted(columns.astype(F32))
        half = lax.broadcasted_iota(jnp.int32, own_rows.shape, 2) < 64
        return own_rows, jnp.where(half, above, below)

    def pair(a, b):
        return jnp.concatenate([a, b], axis=0).astype(BF)

    zero_rows = jnp.zeros((8, 128), F32)

    arrive(LOWER)
    far_rows[0:2] = jnp.zeros((2, 6, 16, 384), BF)
    near_rows[0] = jnp.zeros((4, 16, 256), BF)

    def spread(y, carry):
        columns = cells[y, 2:8]
        for part, v in enumerate(multipoles(columns)):
            ln = slice(128 * part, 128 * part + 128)
            for x in range(6):
                first = v[x - 2] if x >= 2 else zero_rows
                far_rows[y, x, :, ln] = pair(first, v[x])
        for part, v in enumerate(neighbours(columns[0:5])):
            ln = slice(128 * part, 128 * part + 128)
            for x in range(1, 5):
                first = v[x - 2] if x >= 2 else zero_rows
                near_rows[y - 1, x - 1, :, ln] = pair(first, v[x])
        return carry

    lax.fori_loop(2, 8, spread, 0, unroll=6)

    close = jnp.zeros((128, 128), F32)
    for dx in range(3):
        for dy in range(3):
            close += dot(
                near_rows[dy : dy + 4, dx : dx + 2].reshape(128, 256), near_weights[3 * dx + dy]
            )
    close_ref[...] = close

    def place(value, ys, pars):
        i = 0
        for y in ys:
            for par in pars:
                total_ref[y, par] += value[16 * i : 16 * i + 16]
                i += 1

    total_ref[...] = jnp.zeros_like(total_ref)
    for pars in ((0, 1), (1,), (0,)):
        for ys, oys in (((0, 1, 2, 3), range(1, 6)), ((1, 3), (0,)), ((0, 2), (6,))):
            acc = jnp.zeros((16 * len(ys) * len(pars), 128), F32)
            for ox in range(7):
                if parities(ox) != pars:
                    continue
                x0 = ox - 1 + pars[0]
                for oy in oys:
                    lhs = jnp.concatenate(
                        [
                            jnp.concatenate(
                                [
                                    far_rows[y + oy - 1, x0 : x0 + len(pars), :, 128 * c : 128 * c + 128]
                                    for y in ys
                                ],
                                axis=0,
                            ).reshape(16 * len(ys) * len(pars), 128)
                            for c in chunks(ox, oy)
                        ],
                        axis=1,
                    )
                    acc += dot(lhs, far_weights([(ox, oy)]))
            place(acc, ys, pars)

    for k, (dx, dy) in enumerate(SIDES):
        @pl.when(beside(dx, dy) & jnp.logical_not(leads(0, 0)))
        def _():
            remote(k).wait_send()

        if (-dx, -dy) in LOWER:
            @pl.when(present(dx, dy) & leads(0, 0))
            def _():
                straight(k).wait_send()
    for k, (dx, dy) in enumerate(SIDES):
        if (dx, dy) in LOWER:
            @pl.when(leads(dx, dy))
            def _():
                pl.semaphore_wait(ready, 1)
                remote(k).start()

    def late(axis, far_ref, near_ref, far_late, near_late):
        places = (0, 1, 2) if axis == "x" else (0, 3, 6)
        lhs = jnp.concatenate([near_ref[d : d + 2].reshape(32, 256) for d in range(3)], axis=1)
        rhs = jnp.concatenate([near_weights[i] for i in places], axis=0)
        near_late[...] = dot(lhs, rhs)
        sums = {}
        for units, pairs in sorted(late_products(axis).items(), key=lambda c: -len(c[0])):
            columns = []
            for ox, oy in pairs:
                across = oy if axis == "x" else ox
                for c in chunks(ox, oy):
                    ln = slice(128 * c, 128 * c + 128)
                    columns.append(
                        jnp.concatenate(
                            [far_ref[t + d, across - 1 + p, :, ln] for t, d, p in units], axis=0
                        )
                    )
            value = dot(jnp.concatenate(columns, axis=1), far_weights(pairs))
            for i, (t, _, p) in enumerate(units):
                part = value[16 * i : 16 * i + 16]
                sums[t, p] = sums[t, p] + part if (t, p) in sums else part
        for t, p in sums:
            far_late[t, p] = sums[t, p]

    arrive([side for side in SIDES if side in ((0, 1), (-1, 1))])

    @pl.when(gy == 0)
    def _():
        far_late_y[...] = jnp.zeros_like(far_late_y)
        near_late_y[...] = jnp.zeros_like(near_late_y)

    @pl.when(gy > 0)
    def _():
        columns = cells[0:2, 2:8].reshape(12, 8, 128)
        for part, v in enumerate(multipoles(columns)):
            ln = slice(128 * part, 128 * part + 128)
            for y in range(2):
                for x in range(6):
                    first = v[6 * y + x - 2] if x >= 2 else zero_rows
                    far_y[y, x, :, ln] = pair(first, v[6 * y + x])
        for part, v in enumerate(neighbours(cells[1, 2:7])):
            ln = slice(128 * part, 128 * part + 128)
            for x in range(1, 5):
                first = v[x - 2] if x >= 2 else zero_rows
                near_y[x - 1, :, ln] = pair(first, v[x])
        late("y", far_y, near_y, far_late_y, near_late_y)

    arrive([side for side in SIDES if side in ((1, 0), (1, 1), (1, -1))])

    @pl.when(gx == 0)
    def _():
        far_late_x[...] = jnp.zeros_like(far_late_x)
        near_late_x[...] = jnp.zeros_like(near_late_x)

    @pl.when(gx > 0)
    def _():
        columns = cells[:, 0:2].reshape(16, 8, 128)
        for part, v in enumerate(multipoles(columns)):
            ln = slice(128 * part, 128 * part + 128)
            for x in range(2):
                for y in range(6):
                    far_x[x, y, :, ln] = pair(v[2 * y + x], v[2 * y + 4 + x])
        for part, v in enumerate(neighbours(cells[1:7, 1])):
            ln = slice(128 * part, 128 * part + 128)
            for y in range(4):
                near_x[y, :, ln] = pair(v[y], v[y + 2])
        late("x", far_x, near_x, far_late_x, near_late_x)

    def eight(value, i):
        return value[8 * i : 8 * i + 8]

    expansion = []
    for y in range(4):
        for x in range(4):
            value = eight(total_ref[y, x % 2], x // 2)
            if x < 2:
                value = value + far_late_x[x, y % 2, 8 * (y // 2) : 8 * (y // 2) + 8]
            if y < 2:
                value = value + far_late_y[y, x % 2, 8 * (x // 2) : 8 * (x // 2) + 8]
            expansion.append(value)
    distant = dot(jnp.concatenate(expansion, axis=0).astype(BF), l2p_pair)
    for y in range(4):
        for x in range(4):
            value = eight(distant, 4 * y + x) + eight(close_ref[...], 4 * y + 2 * (x % 2) + x // 2)
            if x == 0:
                value = value + eight(near_late_x[...], 2 * (y % 2) + y // 2)
            if y == 0:
                value = value + eight(near_late_y[...], 2 * (x % 2) + x // 2)
            for z in range(8):
                out[x, y : y + 1, 128 * z : 128 * z + 128] = value[z : z + 1]

    for k, (dx, dy) in enumerate(SIDES):
        if (dx, dy) in LOWER:
            @pl.when(leads(dx, dy))
            def _():
                remote(k).wait_send()


def local(density, p2m_operator, m2l_table, near_table, l2p_operator):
    in_hbm = pl.BlockSpec(memory_space=pltpu.HBM)
    operands = [
        pltpu.with_memory_space_constraint(v, pltpu.HBM)
        for v in (density, p2m_operator.T, m2l_table, near_table, l2p_operator)
    ]
    return pl.pallas_call(
        kernel,
        out_shape=jax.ShapeDtypeStruct(density.shape, F32),
        in_specs=[in_hbm] * 5,
        out_specs=pl.BlockSpec(memory_space=pltpu.VMEM),
        scratch_shapes=[
            pltpu.VMEM((4, 4, 1024), BF),
            pltpu.VMEM((8, 8, 8, 128), BF),
            pltpu.VMEM((7, 7, 7, 56, 56), BF),
            pltpu.VMEM((3, 3, 3, 64, 64), BF),
            pltpu.VMEM((56, 64), BF),
            pltpu.VMEM((56, 64), BF),
            pltpu.VMEM((7, 7, 384, 128), BF),
            pltpu.VMEM((9, 256, 128), BF),
            pltpu.VMEM((8, 6, 16, 384), BF),
            pltpu.VMEM((7, 4, 16, 256), BF),
            pltpu.VMEM((2, 6, 16, 384), BF),
            pltpu.VMEM((2, 6, 16, 384), BF),
            pltpu.VMEM((4, 16, 256), BF),
            pltpu.VMEM((4, 16, 256), BF),
            pltpu.VMEM((4, 2, 16, 128), F32),
            pltpu.VMEM((128, 128), F32),
            pltpu.VMEM((2, 2, 16, 128), F32),
            pltpu.VMEM((2, 2, 16, 128), F32),
            pltpu.VMEM((32, 128), F32),
            pltpu.VMEM((32, 128), F32),
            pltpu.VMEM((2, 2, 1024), BF),
            pltpu.VMEM((4, 2, 1024), BF),
            pltpu.VMEM((2, 4, 1024), BF),
            pltpu.SemaphoreType.DMA((5,)),
            pltpu.SemaphoreType.DMA((8,)),
            pltpu.SemaphoreType.DMA((8,)),
            pltpu.SemaphoreType.REGULAR,
        ],
        compiler_params=pltpu.CompilerParams(
            collective_id=0, has_side_effects=True, vmem_limit_bytes=32 * 1024 * 1024
        ),
    )(*operands)


def solution(mesh):
    placed = (P("gx", "gy", None), P(), P(), P(), P())
    return jax.shard_map(
        local, mesh=mesh, in_specs=placed, out_specs=P("gx", "gy", None), check_vma=False
    )
```

```python
import jax
import jax.numpy as jnp
from jax import lax
from jax.experimental import pallas as pl
from jax.experimental.pallas import tpu as pltpu
from jax.sharding import PartitionSpec as P

BF = jnp.bfloat16
F32 = jnp.float32
MESH = pl.DeviceIdType.MESH
HALO = 2
SIDES = [(0, 1), (1, 1), (1, 0), (1, -1), (-1, 1), (-1, 0), (0, -1), (-1, -1)]
LOWER = [(-1, 0), (0, -1), (-1, -1)]
SOURCE = {-1: slice(2, 4), 0: slice(2, 6), 1: slice(4, 6)}
RAW = {0: slice(0, 4), 1: slice(2, 4)}
TARGET = {-1: slice(6, 8), 0: slice(2, 6), 1: slice(0, 2)}


def near_offset(ox, oy):
    return 2 <= ox <= 4 and 2 <= oy <= 4


def chunks(ox, oy):
    return (0, 2) if near_offset(ox, oy) else (0, 1, 2)


def parities(offset):
    return tuple(p for p in (0, 1) if 0 <= offset - 1 + p <= 5)


def early_columns():
    return {0: ((1, 0),), 1: ((0, 0), (1, 1)), 2: ((0, 1),)}


def late_products(axis):
    classes = {}
    for ox in range(7):
        for oy in range(7):
            along, across = (ox, oy) if axis == "x" else (oy, ox)
            units = tuple(
                (t, s - t, p) for t, s in early_columns().get(along, ()) for p in parities(across)
            )
            if units:
                classes.setdefault(units, []).append((ox, oy))
    return classes


def dot(a, b):
    return jnp.dot(a, b, preferred_element_type=F32)


def widen(block):
    rows, lanes = block.shape
    block = jnp.concatenate([block, jnp.zeros((rows, 128 - lanes), BF)], axis=1)
    if rows < 64:
        block = jnp.concatenate([block, jnp.zeros((64 - rows, 128), BF)], axis=0)
    return block


def swap(block):
    return pltpu.roll(block, 64, 1)


def kernel(
    density, p2m_t, m2l, near, l2p, out,
    raw, cells, table, near_raw, p2m_raw, l2p_raw, weights, near_weights,
    far_rows, near_rows, far_x, far_y, near_x, near_y, total_ref, close_ref,
    far_late_x, far_late_y, near_late_x, near_late_y, raw_corner, raw_y, raw_x,
    in_sems, send_sems, recv_sems, ready,
):
    raw_in = [raw_y, raw_corner, raw_x]
    gx, gy = lax.axis_index("gx"), lax.axis_index("gy")
    nx, ny = lax.axis_size("gx"), lax.axis_size("gy")

    def present(dx, dy):
        ok = None
        for d, g, n in ((dx, gx, nx), (dy, gy, ny)):
            if d:
                test = (g + d >= 0) & (g + d < n)
                ok = test if ok is None else ok & test
        return ok

    copies_in = [
        pltpu.make_async_copy(density, raw, in_sems.at[0]),
        pltpu.make_async_copy(near, near_raw, in_sems.at[1]),
        pltpu.make_async_copy(p2m_t, p2m_raw, in_sems.at[2]),
        pltpu.make_async_copy(l2p, l2p_raw, in_sems.at[3]),
    ]
    barrier = pltpu.get_barrier_semaphore()

    def leads(dx, dy):
        return (gx + dx == 0) & (gy + dy == 0)

    def beside(dx, dy):
        return present(dx, dy) & jnp.logical_not(leads(dx, dy))

    @pl.when(jnp.logical_not(leads(0, 0)))
    def _():
        for dx, dy in SIDES:
            @pl.when(present(dx, dy))
            def _():
                pl.semaphore_signal(
                    barrier, inc=1, device_id=(gx + dx, gy + dy), device_id_type=MESH
                )

    def remote(k):
        dx, dy = SIDES[k]
        return pltpu.make_async_remote_copy(
            src_ref=cells.at[SOURCE[dy], SOURCE[dx]],
            dst_ref=cells.at[TARGET[dy], TARGET[dx]],
            send_sem=send_sems.at[k],
            recv_sem=recv_sems.at[k],
            device_id=(gx + dx, gy + dy),
            device_id_type=MESH,
        )

    def straight(k):
        dx, dy = SIDES[k]
        xs, ys = RAW[dx], RAW[dy]
        return pltpu.make_async_remote_copy(
            src_ref=density.at[xs, ys],
            dst_ref=raw_in[k].at[...],
            send_sem=send_sems.at[k],
            recv_sem=recv_sems.at[k],
            device_id=(gx + dx, gy + dy),
            device_id_type=MESH,
        )

    @pl.when(leads(0, 0))
    def _():
        pl.semaphore_wait(
            barrier, sum(present(-dx, -dy).astype(jnp.int32) for dx, dy in LOWER)
        )
        for k, (dx, dy) in enumerate(SIDES):
            if (-dx, -dy) in LOWER:
                @pl.when(present(dx, dy))
                def _():
                    straight(k).start()
        for dx, dy in LOWER:
            @pl.when(present(-dx, -dy))
            def _():
                pl.semaphore_signal(
                    ready, inc=1, device_id=(gx - dx, gy - dy), device_id_type=MESH
                )

    for c in copies_in:
        c.start()
    table_copy = pltpu.make_async_copy(m2l, table, in_sems.at[4])
    table_copy.start()

    def take(block, y0, x0):
        block = block.astype(F32)
        for y in range(block.shape[1]):
            for x in range(block.shape[0]):
                tile = jnp.concatenate(
                    [block[x, y : y + 1, 128 * z : 128 * z + 128] for z in range(8)], axis=0
                )
                cells[y0 + y, x0 + x] = tile.astype(BF)

    for dx, dy in SIDES:
        @pl.when(jnp.logical_not(present(dx, dy)))
        def _():
            ys, xs = TARGET[-dy], TARGET[-dx]
            cells[ys, xs] = jnp.zeros((ys.stop - ys.start, xs.stop - xs.start, 8, 128), BF)

    copies_in[0].wait()
    take(raw[...], HALO, HALO)

    def arrive(sides):
        for k, (dx, dy) in enumerate(SIDES):
            if (dx, dy) in sides:
                @pl.when(beside(-dx, -dy))
                def _():
                    remote(k).wait_recv()

                if (-dx, -dy) in LOWER:
                    @pl.when(leads(-dx, -dy))
                    def _():
                        straight(k).wait_recv()
                        ys, xs = TARGET[dy], TARGET[dx]
                        take(raw_in[k][...], ys.start, xs.start)

    for c in copies_in[1:]:
        c.wait()
    p2m_block = widen(p2m_raw[...])
    p2m = jnp.concatenate([p2m_block, swap(p2m_block)], axis=0)
    l2p_block = widen(l2p_raw[...])
    l2p_pair = jnp.concatenate([l2p_block, swap(l2p_block)], axis=0)
    low = lax.broadcasted_iota(jnp.int32, (64, 128), 1) < 64

    def build_near(i, carry):
        a, b, c = (widen(near_raw[i // 3, i % 3, k]) for k in range(3))
        near_weights[i, 0:64] = jnp.where(low, b, swap(a))
        near_weights[i, 64:128] = jnp.where(low, c, swap(b))
        near_weights[i, 128:192] = swap(c)
        near_weights[i, 192:256] = a
        return carry

    lax.fori_loop(0, 9, build_near, 0, unroll=9)

    @pl.when(jnp.logical_not(leads(0, 0)))
    def _():
        pl.semaphore_wait(
            barrier, sum(beside(dx, dy).astype(jnp.int32) for dx, dy in SIDES)
        )

    for k, (dx, dy) in enumerate(SIDES):
        @pl.when(beside(dx, dy) & jnp.logical_not(leads(0, 0)))
        def _():
            remote(k).start()

    table_copy.wait()
    for ox in range(7):
        def build(oy, carry):
            blocks = [widen(table[ox, oy, k]) for k in range(7)]
            for k in range(6):
                weights[ox, oy, 64 * k : 64 * k + 64] = jnp.where(
                    low, blocks[k + 1], swap(blocks[k])
                )
            return carry

        lax.fori_loop(0, 7, build, 0, unroll=7)
        if 2 <= ox <= 4:
            def build_close(oy, carry):
                weights[ox, oy, 64:128] = swap(widen(table[ox, oy, 1]))
                weights[ox, oy, 256:320] = widen(table[ox, oy, 5])
                return carry

            lax.fori_loop(2, 5, build_close, 0, unroll=3)

    def far_weights(pairs):
        return jnp.concatenate(
            [
                weights[ox, oy, 128 * c : 128 * c + 128]
                for ox, oy in pairs
                for c in chunks(ox, oy)
            ],
            axis=0,
        )

    def shifted(v):
        row = lax.broadcasted_iota(jnp.int32, v.shape, 1)
        below = jnp.where(row == 0, 0.0, pltpu.roll(v, 1, 1))
        above = jnp.where(row == 7, 0.0, pltpu.roll(v, 7, 1))
        return below, v, above

    def multipoles(columns):
        n = columns.shape[0]
        m = lax.dot_general(
            columns.reshape(8 * n, 128), p2m, (((1,), (1,)), ((), ())),
            preferred_element_type=F32,
        )
        return shifted(m.reshape(n, 8, 128))

    def neighbours(columns):
        below, own_rows, above = shifted(columns.astype(F32))
        half = lax.broadcasted_iota(jnp.int32, own_rows.shape, 2) < 64
        return own_rows, jnp.where(half, above, below)

    def pair(a, b):
        return jnp.concatenate([a, b], axis=0).astype(BF)

    zero_rows = jnp.zeros((8, 128), F32)

    arrive(LOWER)
    far_rows[0:2] = jnp.zeros((2, 6, 16, 384), BF)
    near_rows[0] = jnp.zeros((4, 16, 256), BF)

    def spread(y, carry):
        columns = cells[y, 2:8]
        for part, v in enumerate(multipoles(columns)):
            ln = slice(128 * part, 128 * part + 128)
            for x in range(6):
                first = v[x - 2] if x >= 2 else zero_rows
                far_rows[y, x, :, ln] = pair(first, v[x])
        for part, v in enumerate(neighbours(columns[0:5])):
            ln = slice(128 * part, 128 * part + 128)
            for x in range(1, 5):
                first = v[x - 2] if x >= 2 else zero_rows
                near_rows[y - 1, x - 1, :, ln] = pair(first, v[x])
        return carry

    lax.fori_loop(2, 8, spread, 0, unroll=6)

    close = jnp.zeros((128, 128), F32)
    for dx in range(3):
        for dy in range(3):
            close += dot(
                near_rows[dy : dy + 4, dx : dx + 2].reshape(128, 256), near_weights[3 * dx + dy]
            )
    close_ref[...] = close

    def place(value, ys, pars):
        i = 0
        for y in ys:
            for par in pars:
                total_ref[y, par] += value[16 * i : 16 * i + 16]
                i += 1

    total_ref[...] = jnp.zeros_like(total_ref)
    for pars in ((0, 1), (1,), (0,)):
        for ys, oys in (((0, 1, 2, 3), range(1, 6)), ((1, 3), (0,)), ((0, 2), (6,))):
            acc = jnp.zeros((16 * len(ys) * len(pars), 128), F32)
            for ox in range(7):
                if parities(ox) != pars:
                    continue
                x0 = ox - 1 + pars[0]
                for oy in oys:
                    lhs = jnp.concatenate(
                        [
                            jnp.concatenate(
                                [
                                    far_rows[y + oy - 1, x0 : x0 + len(pars), :, 128 * c : 128 * c + 128]
                                    for y in ys
                                ],
                                axis=0,
                            ).reshape(16 * len(ys) * len(pars), 128)
                            for c in chunks(ox, oy)
                        ],
                        axis=1,
                    )
                    acc += dot(lhs, far_weights([(ox, oy)]))
            place(acc, ys, pars)

    for k, (dx, dy) in enumerate(SIDES):
        @pl.when(beside(dx, dy) & jnp.logical_not(leads(0, 0)))
        def _():
            remote(k).wait_send()

        if (-dx, -dy) in LOWER:
            @pl.when(present(dx, dy) & leads(0, 0))
            def _():
                straight(k).wait_send()
    for k, (dx, dy) in enumerate(SIDES):
        if (dx, dy) in LOWER:
            @pl.when(leads(dx, dy))
            def _():
                pl.semaphore_wait(ready, 1)
                remote(k).start()

    def late(axis, far_ref, near_ref, far_late, near_late):
        places = (0, 1, 2) if axis == "x" else (0, 3, 6)
        lhs = jnp.concatenate([near_ref[d : d + 2].reshape(32, 256) for d in range(3)], axis=1)
        rhs = jnp.concatenate([near_weights[i] for i in places], axis=0)
        near_late[...] = dot(lhs, rhs)
        sums = {}
        for units, pairs in sorted(late_products(axis).items(), key=lambda c: -len(c[0])):
            columns = []
            for ox, oy in pairs:
                across = oy if axis == "x" else ox
                for c in chunks(ox, oy):
                    ln = slice(128 * c, 128 * c + 128)
                    columns.append(
                        jnp.concatenate(
                            [far_ref[t + d, across - 1 + p, :, ln] for t, d, p in units], axis=0
                        )
                    )
            value = dot(jnp.concatenate(columns, axis=1), far_weights(pairs))
            for i, (t, _, p) in enumerate(units):
                part = value[16 * i : 16 * i + 16]
                sums[t, p] = sums[t, p] + part if (t, p) in sums else part
        for t, p in sums:
            far_late[t, p] = sums[t, p]

    arrive([side for side in SIDES if side in ((0, 1), (-1, 1))])

    @pl.when(gy == 0)
    def _():
        far_late_y[...] = jnp.zeros_like(far_late_y)
        near_late_y[...] = jnp.zeros_like(near_late_y)

    @pl.when(gy > 0)
    def _():
        columns = cells[0:2, 2:8].reshape(12, 8, 128)
        for part, v in enumerate(multipoles(columns)):
            ln = slice(128 * part, 128 * part + 128)
            for y in range(2):
                for x in range(6):
                    first = v[6 * y + x - 2] if x >= 2 else zero_rows
                    far_y[y, x, :, ln] = pair(first, v[6 * y + x])
        for part, v in enumerate(neighbours(cells[1, 2:7])):
            ln = slice(128 * part, 128 * part + 128)
            for x in range(1, 5):
                first = v[x - 2] if x >= 2 else zero_rows
                near_y[x - 1, :, ln] = pair(first, v[x])
        late("y", far_y, near_y, far_late_y, near_late_y)

    arrive([side for side in SIDES if side in ((1, 0), (1, 1), (1, -1))])

    @pl.when(gx == 0)
    def _():
        far_late_x[...] = jnp.zeros_like(far_late_x)
        near_late_x[...] = jnp.zeros_like(near_late_x)

    @pl.when(gx > 0)
    def _():
        columns = cells[:, 0:2].reshape(16, 8, 128)
        for part, v in enumerate(multipoles(columns)):
            ln = slice(128 * part, 128 * part + 128)
            for x in range(2):
                for y in range(6):
                    far_x[x, y, :, ln] = pair(v[2 * y + x], v[2 * y + 4 + x])
        for part, v in enumerate(neighbours(cells[1:7, 1])):
            ln = slice(128 * part, 128 * part + 128)
            for y in range(4):
                near_x[y, :, ln] = pair(v[y], v[y + 2])
        late("x", far_x, near_x, far_late_x, near_late_x)

    def eight(value, i):
        return value[8 * i : 8 * i + 8]

    expansion = []
    for y in range(4):
        for x in range(4):
            value = eight(total_ref[y, x % 2], x // 2)
            if x < 2:
                value = value + far_late_x[x, y % 2, 8 * (y // 2) : 8 * (y // 2) + 8]
            if y < 2:
                value = value + far_late_y[y, x % 2, 8 * (x // 2) : 8 * (x // 2) + 8]
            expansion.append(value)
    distant = dot(jnp.concatenate(expansion, axis=0).astype(BF), l2p_pair)
    for y in range(4):
        for x in range(4):
            value = eight(distant, 4 * y + x) + eight(close_ref[...], 4 * y + 2 * (x % 2) + x // 2)
            if x == 0:
                value = value + eight(near_late_x[...], 2 * (y % 2) + y // 2)
            if y == 0:
                value = value + eight(near_late_y[...], 2 * (x % 2) + x // 2)
            out[x, pl.ds(y, 8, stride=4), :] = value

    for k, (dx, dy) in enumerate(SIDES):
        if (dx, dy) in LOWER:
            @pl.when(leads(dx, dy))
            def _():
                remote(k).wait_send()


def local(density, p2m_operator, m2l_table, near_table, l2p_operator):
    in_hbm = pl.BlockSpec(memory_space=pltpu.HBM)
    operands = [
        pltpu.with_memory_space_constraint(v, pltpu.HBM)
        for v in (density, p2m_operator.T, m2l_table, near_table, l2p_operator)
    ]
    rows = pl.pallas_call(
        kernel,
        out_shape=jax.ShapeDtypeStruct((4, 32, 128), F32),
        in_specs=[in_hbm] * 5,
        out_specs=pl.BlockSpec(memory_space=pltpu.VMEM),
        scratch_shapes=[
            pltpu.VMEM((4, 4, 1024), BF),
            pltpu.VMEM((8, 8, 8, 128), BF),
            pltpu.VMEM((7, 7, 7, 56, 56), BF),
            pltpu.VMEM((3, 3, 3, 64, 64), BF),
            pltpu.VMEM((56, 64), BF),
            pltpu.VMEM((56, 64), BF),
            pltpu.VMEM((7, 7, 384, 128), BF),
            pltpu.VMEM((9, 256, 128), BF),
            pltpu.VMEM((8, 6, 16, 384), BF),
            pltpu.VMEM((7, 4, 16, 256), BF),
            pltpu.VMEM((2, 6, 16, 384), BF),
            pltpu.VMEM((2, 6, 16, 384), BF),
            pltpu.VMEM((4, 16, 256), BF),
            pltpu.VMEM((4, 16, 256), BF),
            pltpu.VMEM((4, 2, 16, 128), F32),
            pltpu.VMEM((128, 128), F32),
            pltpu.VMEM((2, 2, 16, 128), F32),
            pltpu.VMEM((2, 2, 16, 128), F32),
            pltpu.VMEM((32, 128), F32),
            pltpu.VMEM((32, 128), F32),
            pltpu.VMEM((2, 2, 1024), BF),
            pltpu.VMEM((4, 2, 1024), BF),
            pltpu.VMEM((2, 4, 1024), BF),
            pltpu.SemaphoreType.DMA((5,)),
            pltpu.SemaphoreType.DMA((8,)),
            pltpu.SemaphoreType.DMA((8,)),
            pltpu.SemaphoreType.REGULAR,
        ],
        compiler_params=pltpu.CompilerParams(
            collective_id=0, has_side_effects=True, vmem_limit_bytes=32 * 1024 * 1024
        ),
    )(*operands)
    return rows.reshape(4, 8, 4, 128).transpose(0, 2, 1, 3).reshape(density.shape)


def solution(mesh):
    placed = (P("gx", "gy", None), P(), P(), P(), P())
    return jax.shard_map(
        local, mesh=mesh, in_specs=placed, out_specs=P("gx", "gy", None), check_vma=False
    )
```

```python
import jax
import jax.numpy as jnp
from jax import lax
from jax.experimental import pallas as pl
from jax.experimental.pallas import tpu as pltpu
from jax.sharding import PartitionSpec as P

BF = jnp.bfloat16
F32 = jnp.float32
MESH = pl.DeviceIdType.MESH
HALO = 2
SIDES = [(1, 1), (0, 1), (1, 0), (1, -1), (-1, 1), (-1, 0), (0, -1), (-1, -1)]
LOWER = [(-1, 0), (0, -1), (-1, -1)]
SOURCE = {-1: slice(2, 4), 0: slice(2, 6), 1: slice(4, 6)}
RAW = {0: slice(0, 4), 1: slice(2, 4)}
TARGET = {-1: slice(6, 8), 0: slice(2, 6), 1: slice(0, 2)}


def near_offset(ox, oy):
    return 2 <= ox <= 4 and 2 <= oy <= 4


def chunks(ox, oy):
    return (0, 2) if near_offset(ox, oy) else (0, 1, 2)


def parities(offset):
    return tuple(p for p in (0, 1) if 0 <= offset - 1 + p <= 5)


def early_columns():
    return {0: ((1, 0),), 1: ((0, 0), (1, 1)), 2: ((0, 1),)}


def late_products(axis):
    classes = {}
    for ox in range(7):
        for oy in range(7):
            along, across = (ox, oy) if axis == "x" else (oy, ox)
            units = tuple(
                (t, s - t, p) for t, s in early_columns().get(along, ()) for p in parities(across)
            )
            if units:
                classes.setdefault(units, []).append((ox, oy))
    return classes


def dot(a, b):
    return jnp.dot(a, b, preferred_element_type=F32)


def widen(block):
    rows, lanes = block.shape
    block = jnp.concatenate([block, jnp.zeros((rows, 128 - lanes), BF)], axis=1)
    if rows < 64:
        block = jnp.concatenate([block, jnp.zeros((64 - rows, 128), BF)], axis=0)
    return block


def swap(block):
    return pltpu.roll(block, 64, 1)


def kernel(
    density, p2m_t, m2l, near, l2p, out,
    raw, cells, table, near_raw, p2m_raw, l2p_raw, weights, near_weights,
    far_rows, near_rows, far_x, far_y, near_x, near_y, total_ref, close_ref,
    far_late_x, far_late_y, near_late_x, near_late_y, raw_corner, raw_y, raw_x,
    in_sems, send_sems, recv_sems, ready,
):
    raw_in = [raw_corner, raw_y, raw_x]
    gx, gy = lax.axis_index("gx"), lax.axis_index("gy")
    nx, ny = lax.axis_size("gx"), lax.axis_size("gy")

    def present(dx, dy):
        ok = None
        for d, g, n in ((dx, gx, nx), (dy, gy, ny)):
            if d:
                test = (g + d >= 0) & (g + d < n)
                ok = test if ok is None else ok & test
        return ok

    copies_in = [
        pltpu.make_async_copy(density, raw, in_sems.at[0]),
        pltpu.make_async_copy(near, near_raw, in_sems.at[1]),
        pltpu.make_async_copy(p2m_t, p2m_raw, in_sems.at[2]),
        pltpu.make_async_copy(l2p, l2p_raw, in_sems.at[3]),
    ]
    barrier = pltpu.get_barrier_semaphore()

    def leads(dx, dy):
        return (gx + dx == 0) & (gy + dy == 0)

    def beside(dx, dy):
        return present(dx, dy) & jnp.logical_not(leads(dx, dy))

    @pl.when(jnp.logical_not(leads(0, 0)))
    def _():
        for dx, dy in SIDES:
            @pl.when(present(dx, dy))
            def _():
                pl.semaphore_signal(
                    barrier, inc=1, device_id=(gx + dx, gy + dy), device_id_type=MESH
                )

    def remote(k):
        dx, dy = SIDES[k]
        return pltpu.make_async_remote_copy(
            src_ref=cells.at[SOURCE[dy], SOURCE[dx]],
            dst_ref=cells.at[TARGET[dy], TARGET[dx]],
            send_sem=send_sems.at[k],
            recv_sem=recv_sems.at[k],
            device_id=(gx + dx, gy + dy),
            device_id_type=MESH,
        )

    def straight(k):
        dx, dy = SIDES[k]
        return pltpu.make_async_remote_copy(
            src_ref=density.at[RAW[dx]],
            dst_ref=raw_in[k].at[...],
            send_sem=send_sems.at[k],
            recv_sem=recv_sems.at[k],
            device_id=(gx + dx, gy + dy),
            device_id_type=MESH,
        )

    @pl.when(leads(0, 0))
    def _():
        pl.semaphore_wait(
            barrier, sum(present(-dx, -dy).astype(jnp.int32) for dx, dy in LOWER)
        )
        for k, (dx, dy) in enumerate(SIDES):
            if (-dx, -dy) in LOWER:
                @pl.when(present(dx, dy))
                def _():
                    straight(k).start()
        for dx, dy in LOWER:
            @pl.when(present(-dx, -dy))
            def _():
                pl.semaphore_signal(
                    ready, inc=1, device_id=(gx - dx, gy - dy), device_id_type=MESH
                )

    for c in copies_in:
        c.start()
    table_copy = pltpu.make_async_copy(m2l, table, in_sems.at[4])
    table_copy.start()

    def take(block, ys, y0, x0):
        block = block.astype(F32)
        for i, y in enumerate(range(ys.start, ys.stop)):
            for x in range(block.shape[0]):
                tile = jnp.concatenate(
                    [block[x, y : y + 1, 128 * z : 128 * z + 128] for z in range(8)], axis=0
                )
                cells[y0 + i, x0 + x] = tile.astype(BF)

    for dx, dy in SIDES:
        @pl.when(jnp.logical_not(present(dx, dy)))
        def _():
            ys, xs = TARGET[-dy], TARGET[-dx]
            cells[ys, xs] = jnp.zeros((ys.stop - ys.start, xs.stop - xs.start, 8, 128), BF)

    copies_in[0].wait()
    take(raw[...], slice(0, 4), HALO, HALO)

    def arrive(sides):
        for k, (dx, dy) in enumerate(SIDES):
            if (dx, dy) in sides:
                @pl.when(beside(-dx, -dy))
                def _():
                    remote(k).wait_recv()

                if (-dx, -dy) in LOWER:
                    @pl.when(leads(-dx, -dy))
                    def _():
                        straight(k).wait_recv()
                        ys, xs = TARGET[dy], TARGET[dx]
                        take(raw_in[k][...], RAW[dy], ys.start, xs.start)

    for c in copies_in[1:]:
        c.wait()
    p2m_block = widen(p2m_raw[...])
    p2m = jnp.concatenate([p2m_block, swap(p2m_block)], axis=0)
    l2p_block = widen(l2p_raw[...])
    l2p_pair = jnp.concatenate([l2p_block, swap(l2p_block)], axis=0)
    low = lax.broadcasted_iota(jnp.int32, (64, 128), 1) < 64

    def build_near(i, carry):
        a, b, c = (widen(near_raw[i // 3, i % 3, k]) for k in range(3))
        near_weights[i, 0:64] = jnp.where(low, b, swap(a))
        near_weights[i, 64:128] = jnp.where(low, c, swap(b))
        near_weights[i, 128:192] = swap(c)
        near_weights[i, 192:256] = a
        return carry

    lax.fori_loop(0, 9, build_near, 0, unroll=9)

    @pl.when(jnp.logical_not(leads(0, 0)))
    def _():
        pl.semaphore_wait(
            barrier, sum(beside(dx, dy).astype(jnp.int32) for dx, dy in SIDES)
        )

    for k, (dx, dy) in enumerate(SIDES):
        @pl.when(beside(dx, dy) & jnp.logical_not(leads(0, 0)))
        def _():
            remote(k).start()

    table_copy.wait()
    for ox in range(7):
        def build(oy, carry):
            blocks = [widen(table[ox, oy, k]) for k in range(7)]
            for k in range(6):
                weights[ox, oy, 64 * k : 64 * k + 64] = jnp.where(
                    low, blocks[k + 1], swap(blocks[k])
                )
            return carry

        lax.fori_loop(0, 7, build, 0, unroll=7)
        if 2 <= ox <= 4:
            def build_close(oy, carry):
                weights[ox, oy, 64:128] = swap(widen(table[ox, oy, 1]))
                weights[ox, oy, 256:320] = widen(table[ox, oy, 5])
                return carry

            lax.fori_loop(2, 5, build_close, 0, unroll=3)

    def far_weights(pairs):
        return jnp.concatenate(
            [
                weights[ox, oy, 128 * c : 128 * c + 128]
                for ox, oy in pairs
                for c in chunks(ox, oy)
            ],
            axis=0,
        )

    def shifted(v):
        row = lax.broadcasted_iota(jnp.int32, v.shape, 1)
        below = jnp.where(row == 0, 0.0, pltpu.roll(v, 1, 1))
        above = jnp.where(row == 7, 0.0, pltpu.roll(v, 7, 1))
        return below, v, above

    def multipoles(columns):
        n = columns.shape[0]
        m = lax.dot_general(
            columns.reshape(8 * n, 128), p2m, (((1,), (1,)), ((), ())),
            preferred_element_type=F32,
        )
        return shifted(m.reshape(n, 8, 128))

    def neighbours(columns):
        below, own_rows, above = shifted(columns.astype(F32))
        half = lax.broadcasted_iota(jnp.int32, own_rows.shape, 2) < 64
        return own_rows, jnp.where(half, above, below)

    def pair(a, b):
        return jnp.concatenate([a, b], axis=0).astype(BF)

    zero_rows = jnp.zeros((8, 128), F32)

    arrive(LOWER)
    far_rows[0:2] = jnp.zeros((2, 6, 16, 384), BF)
    near_rows[0] = jnp.zeros((4, 16, 256), BF)

    def spread(y, carry):
        columns = cells[y, 2:8]
        for part, v in enumerate(multipoles(columns)):
            ln = slice(128 * part, 128 * part + 128)
            for x in range(6):
                first = v[x - 2] if x >= 2 else zero_rows
                far_rows[y, x, :, ln] = pair(first, v[x])
        for part, v in enumerate(neighbours(columns[0:5])):
            ln = slice(128 * part, 128 * part + 128)
            for x in range(1, 5):
                first = v[x - 2] if x >= 2 else zero_rows
                near_rows[y - 1, x - 1, :, ln] = pair(first, v[x])
        return carry

    lax.fori_loop(2, 8, spread, 0, unroll=6)

    close = jnp.zeros((128, 128), F32)
    for dx in range(3):
        for dy in range(3):
            close += dot(
                near_rows[dy : dy + 4, dx : dx + 2].reshape(128, 256), near_weights[3 * dx + dy]
            )
    close_ref[...] = close

    def place(value, ys, pars):
        i = 0
        for y in ys:
            for par in pars:
                total_ref[y, par] += value[16 * i : 16 * i + 16]
                i += 1

    total_ref[...] = jnp.zeros_like(total_ref)
    for pars in ((0, 1), (1,), (0,)):
        for ys, oys in (((0, 1, 2, 3), range(1, 6)), ((1, 3), (0,)), ((0, 2), (6,))):
            acc = jnp.zeros((16 * len(ys) * len(pars), 128), F32)
            for ox in range(7):
                if parities(ox) != pars:
                    continue
                x0 = ox - 1 + pars[0]
                for oy in oys:
                    lhs = jnp.concatenate(
                        [
                            jnp.concatenate(
                                [
                                    far_rows[y + oy - 1, x0 : x0 + len(pars), :, 128 * c : 128 * c + 128]
                                    for y in ys
                                ],
                                axis=0,
                            ).reshape(16 * len(ys) * len(pars), 128)
                            for c in chunks(ox, oy)
                        ],
                        axis=1,
                    )
                    acc += dot(lhs, far_weights([(ox, oy)]))
            place(acc, ys, pars)

    for k, (dx, dy) in enumerate(SIDES):
        @pl.when(beside(dx, dy) & jnp.logical_not(leads(0, 0)))
        def _():
            remote(k).wait_send()

        if (-dx, -dy) in LOWER:
            @pl.when(present(dx, dy) & leads(0, 0))
            def _():
                straight(k).wait_send()
    for k, (dx, dy) in enumerate(SIDES):
        if (dx, dy) in LOWER:
            @pl.when(leads(dx, dy))
            def _():
                pl.semaphore_wait(ready, 1)
                remote(k).start()

    def late(axis, far_ref, near_ref, far_late, near_late):
        places = (0, 1, 2) if axis == "x" else (0, 3, 6)
        lhs = jnp.concatenate([near_ref[d : d + 2].reshape(32, 256) for d in range(3)], axis=1)
        rhs = jnp.concatenate([near_weights[i] for i in places], axis=0)
        near_late[...] = dot(lhs, rhs)
        sums = {}
        for units, pairs in sorted(late_products(axis).items(), key=lambda c: -len(c[0])):
            columns = []
            for ox, oy in pairs:
                across = oy if axis == "x" else ox
                for c in chunks(ox, oy):
                    ln = slice(128 * c, 128 * c + 128)
                    columns.append(
                        jnp.concatenate(
                            [far_ref[t + d, across - 1 + p, :, ln] for t, d, p in units], axis=0
                        )
                    )
            value = dot(jnp.concatenate(columns, axis=1), far_weights(pairs))
            for i, (t, _, p) in enumerate(units):
                part = value[16 * i : 16 * i + 16]
                sums[t, p] = sums[t, p] + part if (t, p) in sums else part
        for t, p in sums:
            far_late[t, p] = sums[t, p]

    arrive([side for side in SIDES if side in ((0, 1), (-1, 1))])

    @pl.when(gy == 0)
    def _():
        far_late_y[...] = jnp.zeros_like(far_late_y)
        near_late_y[...] = jnp.zeros_like(near_late_y)

    @pl.when(gy > 0)
    def _():
        columns = cells[0:2, 2:8].reshape(12, 8, 128)
        for part, v in enumerate(multipoles(columns)):
            ln = slice(128 * part, 128 * part + 128)
            for y in range(2):
                for x in range(6):
                    first = v[6 * y + x - 2] if x >= 2 else zero_rows
                    far_y[y, x, :, ln] = pair(first, v[6 * y + x])
        for part, v in enumerate(neighbours(cells[1, 2:7])):
            ln = slice(128 * part, 128 * part + 128)
            for x in range(1, 5):
                first = v[x - 2] if x >= 2 else zero_rows
                near_y[x - 1, :, ln] = pair(first, v[x])
        late("y", far_y, near_y, far_late_y, near_late_y)

    arrive([side for side in SIDES if side in ((1, 0), (1, 1), (1, -1))])

    @pl.when(gx == 0)
    def _():
        far_late_x[...] = jnp.zeros_like(far_late_x)
        near_late_x[...] = jnp.zeros_like(near_late_x)

    @pl.when(gx > 0)
    def _():
        columns = cells[:, 0:2].reshape(16, 8, 128)
        for part, v in enumerate(multipoles(columns)):
            ln = slice(128 * part, 128 * part + 128)
            for x in range(2):
                for y in range(6):
                    far_x[x, y, :, ln] = pair(v[2 * y + x], v[2 * y + 4 + x])
        for part, v in enumerate(neighbours(cells[1:7, 1])):
            ln = slice(128 * part, 128 * part + 128)
            for y in range(4):
                near_x[y, :, ln] = pair(v[y], v[y + 2])
        late("x", far_x, near_x, far_late_x, near_late_x)

    def eight(value, i):
        return value[8 * i : 8 * i + 8]

    expansion = []
    for y in range(4):
        for x in range(4):
            value = eight(total_ref[y, x % 2], x // 2)
            if x < 2:
                value = value + far_late_x[x, y % 2, 8 * (y // 2) : 8 * (y // 2) + 8]
            if y < 2:
                value = value + far_late_y[y, x % 2, 8 * (x // 2) : 8 * (x // 2) + 8]
            expansion.append(value)
    distant = dot(jnp.concatenate(expansion, axis=0).astype(BF), l2p_pair)
    for y in range(4):
        for x in range(4):
            value = eight(distant, 4 * y + x) + eight(close_ref[...], 4 * y + 2 * (x % 2) + x // 2)
            if x == 0:
                value = value + eight(near_late_x[...], 2 * (y % 2) + y // 2)
            if y == 0:
                value = value + eight(near_late_y[...], 2 * (x % 2) + x // 2)
            out[x, pl.ds(y, 8, stride=4), :] = value

    for k, (dx, dy) in enumerate(SIDES):
        if (dx, dy) in LOWER:
            @pl.when(leads(dx, dy))
            def _():
                remote(k).wait_send()


def local(density, p2m_operator, m2l_table, near_table, l2p_operator):
    in_hbm = pl.BlockSpec(memory_space=pltpu.HBM)
    operands = [
        pltpu.with_memory_space_constraint(v, pltpu.HBM)
        for v in (density, p2m_operator.T, m2l_table, near_table, l2p_operator)
    ]
    rows = pl.pallas_call(
        kernel,
        out_shape=jax.ShapeDtypeStruct((4, 32, 128), F32),
        in_specs=[in_hbm] * 5,
        out_specs=pl.BlockSpec(memory_space=pltpu.VMEM),
        scratch_shapes=[
            pltpu.VMEM((4, 4, 1024), BF),
            pltpu.VMEM((8, 8, 8, 128), BF),
            pltpu.VMEM((7, 7, 7, 56, 56), BF),
            pltpu.VMEM((3, 3, 3, 64, 64), BF),
            pltpu.VMEM((56, 64), BF),
            pltpu.VMEM((56, 64), BF),
            pltpu.VMEM((7, 7, 384, 128), BF),
            pltpu.VMEM((9, 256, 128), BF),
            pltpu.VMEM((8, 6, 16, 384), BF),
            pltpu.VMEM((7, 4, 16, 256), BF),
            pltpu.VMEM((2, 6, 16, 384), BF),
            pltpu.VMEM((2, 6, 16, 384), BF),
            pltpu.VMEM((4, 16, 256), BF),
            pltpu.VMEM((4, 16, 256), BF),
            pltpu.VMEM((4, 2, 16, 128), F32),
            pltpu.VMEM((128, 128), F32),
            pltpu.VMEM((2, 2, 16, 128), F32),
            pltpu.VMEM((2, 2, 16, 128), F32),
            pltpu.VMEM((32, 128), F32),
            pltpu.VMEM((32, 128), F32),
            pltpu.VMEM((2, 4, 1024), BF),
            pltpu.VMEM((4, 4, 1024), BF),
            pltpu.VMEM((2, 4, 1024), BF),
            pltpu.SemaphoreType.DMA((5,)),
            pltpu.SemaphoreType.DMA((8,)),
            pltpu.SemaphoreType.DMA((8,)),
            pltpu.SemaphoreType.REGULAR,
        ],
        compiler_params=pltpu.CompilerParams(
            collective_id=0, has_side_effects=True, vmem_limit_bytes=32 * 1024 * 1024
        ),
    )(*operands)
    return rows.reshape(4, 8, 4, 128).transpose(0, 2, 1, 3).reshape(density.shape)


def solution(mesh):
    placed = (P("gx", "gy", None), P(), P(), P(), P())
    return jax.shard_map(
        local, mesh=mesh, in_specs=placed, out_specs=P("gx", "gy", None), check_vma=False
    )
```

```python
import jax
import jax.numpy as jnp
from jax import lax
from jax.experimental import pallas as pl
from jax.experimental.pallas import tpu as pltpu
from jax.sharding import PartitionSpec as P

BF = jnp.bfloat16
F32 = jnp.float32
MESH = pl.DeviceIdType.MESH
HALO = 2
SIDES = [(1, 1), (0, 1), (1, 0), (1, -1), (-1, 1), (-1, 0), (0, -1), (-1, -1)]
LOWER = [(-1, 0), (0, -1), (-1, -1)]
SOURCE = {-1: slice(2, 4), 0: slice(2, 6), 1: slice(4, 6)}
RAW = {0: slice(0, 4), 1: slice(2, 4)}
TARGET = {-1: slice(6, 8), 0: slice(2, 6), 1: slice(0, 2)}


def near_offset(ox, oy):
    return 2 <= ox <= 4 and 2 <= oy <= 4


def chunks(ox, oy):
    return (0, 2) if near_offset(ox, oy) else (0, 1, 2)


def parities(offset):
    return tuple(p for p in (0, 1) if 0 <= offset - 1 + p <= 5)


def early_columns():
    return {0: ((1, 0),), 1: ((0, 0), (1, 1)), 2: ((0, 1),)}


def late_products(axis):
    classes = {}
    for ox in range(7):
        for oy in range(7):
            along, across = (ox, oy) if axis == "x" else (oy, ox)
            units = tuple(
                (t, s - t, p) for t, s in early_columns().get(along, ()) for p in parities(across)
            )
            if units:
                classes.setdefault(units, []).append((ox, oy))
    return classes


def dot(a, b):
    return jnp.dot(a, b, preferred_element_type=F32)


def widen(block):
    rows, lanes = block.shape
    block = jnp.concatenate([block, jnp.zeros((rows, 128 - lanes), BF)], axis=1)
    if rows < 64:
        block = jnp.concatenate([block, jnp.zeros((64 - rows, 128), BF)], axis=0)
    return block


def swap(block):
    return pltpu.roll(block, 64, 1)


def kernel(
    density, p2m_t, m2l, near, l2p, out,
    raw, cells, table, near_raw, p2m_raw, l2p_raw, weights, near_weights,
    far_rows, near_rows, far_x, far_y, near_x, near_y, total_ref, close_ref,
    far_late_x, far_late_y, near_late_x, near_late_y, raw_corner, raw_y, raw_x,
    in_sems, send_sems, recv_sems, ready,
):
    raw_in = [raw_corner, raw_y, raw_x]
    gx, gy = lax.axis_index("gx"), lax.axis_index("gy")
    nx, ny = lax.axis_size("gx"), lax.axis_size("gy")

    def present(dx, dy):
        ok = None
        for d, g, n in ((dx, gx, nx), (dy, gy, ny)):
            if d:
                test = (g + d >= 0) & (g + d < n)
                ok = test if ok is None else ok & test
        return ok

    copies_in = [
        pltpu.make_async_copy(density, raw, in_sems.at[0]),
        pltpu.make_async_copy(near, near_raw, in_sems.at[1]),
        pltpu.make_async_copy(p2m_t, p2m_raw, in_sems.at[2]),
        pltpu.make_async_copy(l2p, l2p_raw, in_sems.at[3]),
    ]
    barrier = pltpu.get_barrier_semaphore()

    def leads(dx, dy):
        return (gx + dx == 0) & (gy + dy == 0)

    def beside(dx, dy):
        return present(dx, dy) & jnp.logical_not(leads(dx, dy))

    @pl.when(jnp.logical_not(leads(0, 0)))
    def _():
        for dx, dy in SIDES:
            @pl.when(present(dx, dy))
            def _():
                pl.semaphore_signal(
                    barrier, inc=1, device_id=(gx + dx, gy + dy), device_id_type=MESH
                )

    def remote(k):
        dx, dy = SIDES[k]
        return pltpu.make_async_remote_copy(
            src_ref=cells.at[SOURCE[dy], SOURCE[dx]],
            dst_ref=cells.at[TARGET[dy], TARGET[dx]],
            send_sem=send_sems.at[k],
            recv_sem=recv_sems.at[k],
            device_id=(gx + dx, gy + dy),
            device_id_type=MESH,
        )

    def straight(k):
        dx, dy = SIDES[k]
        xs, ys = RAW[dx], RAW[dy]
        return pltpu.make_async_remote_copy(
            src_ref=density.at[xs, ys],
            dst_ref=raw_in[k].at[...],
            send_sem=send_sems.at[k],
            recv_sem=recv_sems.at[k],
            device_id=(gx + dx, gy + dy),
            device_id_type=MESH,
        )

    @pl.when(leads(0, 0))
    def _():
        pl.semaphore_wait(
            barrier, sum(present(-dx, -dy).astype(jnp.int32) for dx, dy in LOWER)
        )
        for k, (dx, dy) in enumerate(SIDES):
            if (-dx, -dy) in LOWER:
                @pl.when(present(dx, dy))
                def _():
                    straight(k).start()
        for dx, dy in LOWER:
            @pl.when(present(-dx, -dy))
            def _():
                pl.semaphore_signal(
                    ready, inc=1, device_id=(gx - dx, gy - dy), device_id_type=MESH
                )

    for c in copies_in:
        c.start()
    table_copy = pltpu.make_async_copy(m2l, table, in_sems.at[4])
    table_copy.start()

    def take(block, y0, x0):
        block = block.astype(F32)
        for y in range(block.shape[1]):
            for x in range(block.shape[0]):
                tile = jnp.concatenate(
                    [block[x, y : y + 1, 128 * z : 128 * z + 128] for z in range(8)], axis=0
                )
                cells[y0 + y, x0 + x] = tile.astype(BF)

    for dx, dy in SIDES:
        @pl.when(jnp.logical_not(present(dx, dy)))
        def _():
            ys, xs = TARGET[-dy], TARGET[-dx]
            cells[ys, xs] = jnp.zeros((ys.stop - ys.start, xs.stop - xs.start, 8, 128), BF)

    copies_in[0].wait()
    take(raw[...], HALO, HALO)

    def arrive(sides):
        for k, (dx, dy) in enumerate(SIDES):
            if (dx, dy) in sides:
                @pl.when(beside(-dx, -dy))
                def _():
                    remote(k).wait_recv()

                if (-dx, -dy) in LOWER:
                    @pl.when(leads(-dx, -dy))
                    def _():
                        straight(k).wait_recv()
                        ys, xs = TARGET[dy], TARGET[dx]
                        take(raw_in[k][...], ys.start, xs.start)

    for c in copies_in[1:]:
        c.wait()
    p2m_block = widen(p2m_raw[...])
    p2m = jnp.concatenate([p2m_block, swap(p2m_block)], axis=0)
    l2p_block = widen(l2p_raw[...])
    l2p_pair = jnp.concatenate([l2p_block, swap(l2p_block)], axis=0)
    low = lax.broadcasted_iota(jnp.int32, (64, 128), 1) < 64

    def build_near(i, carry):
        a, b, c = (widen(near_raw[i // 3, i % 3, k]) for k in range(3))
        near_weights[i, 0:64] = jnp.where(low, b, swap(a))
        near_weights[i, 64:128] = jnp.where(low, c, swap(b))
        near_weights[i, 128:192] = swap(c)
        near_weights[i, 192:256] = a
        return carry

    lax.fori_loop(0, 9, build_near, 0, unroll=9)

    @pl.when(jnp.logical_not(leads(0, 0)))
    def _():
        pl.semaphore_wait(
            barrier, sum(beside(dx, dy).astype(jnp.int32) for dx, dy in SIDES)
        )

    for k, (dx, dy) in enumerate(SIDES):
        @pl.when(beside(dx, dy) & jnp.logical_not(leads(0, 0)))
        def _():
            remote(k).start()

    table_copy.wait()
    for ox in range(7):
        def build(oy, carry):
            blocks = [widen(table[ox, oy, k]) for k in range(7)]
            for k in range(6):
                weights[ox, oy, 64 * k : 64 * k + 64] = jnp.where(
                    low, blocks[k + 1], swap(blocks[k])
                )
            return carry

        lax.fori_loop(0, 7, build, 0, unroll=7)
        if 2 <= ox <= 4:
            def build_close(oy, carry):
                weights[ox, oy, 64:128] = swap(widen(table[ox, oy, 1]))
                weights[ox, oy, 256:320] = widen(table[ox, oy, 5])
                return carry

            lax.fori_loop(2, 5, build_close, 0, unroll=3)

    def far_weights(pairs):
        return jnp.concatenate(
            [
                weights[ox, oy, 128 * c : 128 * c + 128]
                for ox, oy in pairs
                for c in chunks(ox, oy)
            ],
            axis=0,
        )

    def shifted(v):
        row = lax.broadcasted_iota(jnp.int32, v.shape, 1)
        below = jnp.where(row == 0, 0.0, pltpu.roll(v, 1, 1))
        above = jnp.where(row == 7, 0.0, pltpu.roll(v, 7, 1))
        return below, v, above

    def multipoles(columns):
        n = columns.shape[0]
        m = lax.dot_general(
            columns.reshape(8 * n, 128), p2m, (((1,), (1,)), ((), ())),
            preferred_element_type=F32,
        )
        return shifted(m.reshape(n, 8, 128))

    def neighbours(columns):
        below, own_rows, above = shifted(columns.astype(F32))
        half = lax.broadcasted_iota(jnp.int32, own_rows.shape, 2) < 64
        return own_rows, jnp.where(half, above, below)

    def pair(a, b):
        return jnp.concatenate([a, b], axis=0).astype(BF)

    zero_rows = jnp.zeros((8, 128), F32)

    arrive(LOWER)
    far_rows[0:2] = jnp.zeros((2, 6, 16, 384), BF)
    near_rows[0] = jnp.zeros((4, 16, 256), BF)

    def spread(y, carry):
        columns = cells[y, 2:8]
        for part, v in enumerate(multipoles(columns)):
            ln = slice(128 * part, 128 * part + 128)
            for x in range(6):
                first = v[x - 2] if x >= 2 else zero_rows
                far_rows[y, x, :, ln] = pair(first, v[x])
        for part, v in enumerate(neighbours(columns[0:5])):
            ln = slice(128 * part, 128 * part + 128)
            for x in range(1, 5):
                first = v[x - 2] if x >= 2 else zero_rows
                near_rows[y - 1, x - 1, :, ln] = pair(first, v[x])
        return carry

    lax.fori_loop(2, 8, spread, 0, unroll=6)

    close = jnp.zeros((128, 128), F32)
    for dx in range(3):
        for dy in range(3):
            close += dot(
                near_rows[dy : dy + 4, dx : dx + 2].reshape(128, 256), near_weights[3 * dx + dy]
            )
    close_ref[...] = close

    def place(value, ys, pars):
        i = 0
        for y in ys:
            for par in pars:
                total_ref[y, par] += value[16 * i : 16 * i + 16]
                i += 1

    total_ref[...] = jnp.zeros_like(total_ref)
    for pars in ((0, 1), (1,), (0,)):
        for ys, oys in (((0, 1, 2, 3), range(1, 6)), ((1, 3), (0,)), ((0, 2), (6,))):
            acc = jnp.zeros((16 * len(ys) * len(pars), 128), F32)
            for ox in range(7):
                if parities(ox) != pars:
                    continue
                x0 = ox - 1 + pars[0]
                for oy in oys:
                    lhs = jnp.concatenate(
                        [
                            jnp.concatenate(
                                [
                                    far_rows[y + oy - 1, x0 : x0 + len(pars), :, 128 * c : 128 * c + 128]
                                    for y in ys
                                ],
                                axis=0,
                            ).reshape(16 * len(ys) * len(pars), 128)
                            for c in chunks(ox, oy)
                        ],
                        axis=1,
                    )
                    acc += dot(lhs, far_weights([(ox, oy)]))
            place(acc, ys, pars)

    for k, (dx, dy) in enumerate(SIDES):
        @pl.when(beside(dx, dy) & jnp.logical_not(leads(0, 0)))
        def _():
            remote(k).wait_send()

        if (-dx, -dy) in LOWER:
            @pl.when(present(dx, dy) & leads(0, 0))
            def _():
                straight(k).wait_send()
    for k, (dx, dy) in enumerate(SIDES):
        if (dx, dy) in LOWER:
            @pl.when(leads(dx, dy))
            def _():
                pl.semaphore_wait(ready, 1)
                remote(k).start()

    def late(axis, far_ref, near_ref, far_late, near_late):
        places = (0, 1, 2) if axis == "x" else (0, 3, 6)
        lhs = jnp.concatenate([near_ref[d : d + 2].reshape(32, 256) for d in range(3)], axis=1)
        rhs = jnp.concatenate([near_weights[i] for i in places], axis=0)
        near_late[...] = dot(lhs, rhs)
        sums = {}
        for units, pairs in sorted(late_products(axis).items(), key=lambda c: -len(c[0])):
            columns = []
            for ox, oy in pairs:
                across = oy if axis == "x" else ox
                for c in chunks(ox, oy):
                    ln = slice(128 * c, 128 * c + 128)
                    columns.append(
                        jnp.concatenate(
                            [far_ref[t + d, across - 1 + p, :, ln] for t, d, p in units], axis=0
                        )
                    )
            value = dot(jnp.concatenate(columns, axis=1), far_weights(pairs))
            for i, (t, _, p) in enumerate(units):
                part = value[16 * i : 16 * i + 16]
                sums[t, p] = sums[t, p] + part if (t, p) in sums else part
        for t, p in sums:
            far_late[t, p] = sums[t, p]

    arrive([side for side in SIDES if side in ((0, 1), (-1, 1))])

    @pl.when(gy == 0)
    def _():
        far_late_y[...] = jnp.zeros_like(far_late_y)
        near_late_y[...] = jnp.zeros_like(near_late_y)

    @pl.when(gy > 0)
    def _():
        columns = cells[0:2, 2:8].reshape(12, 8, 128)
        for part, v in enumerate(multipoles(columns)):
            ln = slice(128 * part, 128 * part + 128)
            for y in range(2):
                for x in range(6):
                    first = v[6 * y + x - 2] if x >= 2 else zero_rows
                    far_y[y, x, :, ln] = pair(first, v[6 * y + x])
        for part, v in enumerate(neighbours(cells[1, 2:7])):
            ln = slice(128 * part, 128 * part + 128)
            for x in range(1, 5):
                first = v[x - 2] if x >= 2 else zero_rows
                near_y[x - 1, :, ln] = pair(first, v[x])
        late("y", far_y, near_y, far_late_y, near_late_y)

    arrive([side for side in SIDES if side in ((1, 0), (1, 1), (1, -1))])

    @pl.when(gx == 0)
    def _():
        far_late_x[...] = jnp.zeros_like(far_late_x)
        near_late_x[...] = jnp.zeros_like(near_late_x)

    @pl.when(gx > 0)
    def _():
        columns = cells[:, 0:2].reshape(16, 8, 128)
        for part, v in enumerate(multipoles(columns)):
            ln = slice(128 * part, 128 * part + 128)
            for x in range(2):
                for y in range(6):
                    far_x[x, y, :, ln] = pair(v[2 * y + x], v[2 * y + 4 + x])
        for part, v in enumerate(neighbours(cells[1:7, 1])):
            ln = slice(128 * part, 128 * part + 128)
            for y in range(4):
                near_x[y, :, ln] = pair(v[y], v[y + 2])
        late("x", far_x, near_x, far_late_x, near_late_x)

    def eight(value, i):
        return value[8 * i : 8 * i + 8]

    expansion = []
    for y in range(4):
        for x in range(4):
            value = eight(total_ref[y, x % 2], x // 2)
            if x < 2:
                value = value + far_late_x[x, y % 2, 8 * (y // 2) : 8 * (y // 2) + 8]
            if y < 2:
                value = value + far_late_y[y, x % 2, 8 * (x // 2) : 8 * (x // 2) + 8]
            expansion.append(value)
    distant = dot(jnp.concatenate(expansion, axis=0).astype(BF), l2p_pair)
    for y in range(4):
        for x in range(4):
            value = eight(distant, 4 * y + x) + eight(close_ref[...], 4 * y + 2 * (x % 2) + x // 2)
            if x == 0:
                value = value + eight(near_late_x[...], 2 * (y % 2) + y // 2)
            if y == 0:
                value = value + eight(near_late_y[...], 2 * (x % 2) + x // 2)
            out[x, pl.ds(y, 8, stride=4), :] = value

    for k, (dx, dy) in enumerate(SIDES):
        if (dx, dy) in LOWER:
            @pl.when(leads(dx, dy))
            def _():
                remote(k).wait_send()


def local(density, p2m_operator, m2l_table, near_table, l2p_operator):
    in_hbm = pl.BlockSpec(memory_space=pltpu.HBM)
    operands = [
        pltpu.with_memory_space_constraint(v, pltpu.HBM)
        for v in (density, p2m_operator.T, m2l_table, near_table, l2p_operator)
    ]
    rows = pl.pallas_call(
        kernel,
        out_shape=jax.ShapeDtypeStruct((4, 32, 128), F32),
        in_specs=[in_hbm] * 5,
        out_specs=pl.BlockSpec(memory_space=pltpu.VMEM),
        scratch_shapes=[
            pltpu.VMEM((4, 4, 1024), BF),
            pltpu.VMEM((8, 8, 8, 128), BF),
            pltpu.VMEM((7, 7, 7, 56, 56), BF),
            pltpu.VMEM((3, 3, 3, 64, 64), BF),
            pltpu.VMEM((56, 64), BF),
            pltpu.VMEM((56, 64), BF),
            pltpu.VMEM((7, 7, 384, 128), BF),
            pltpu.VMEM((9, 256, 128), BF),
            pltpu.VMEM((8, 6, 16, 384), BF),
            pltpu.VMEM((7, 4, 16, 256), BF),
            pltpu.VMEM((2, 6, 16, 384), BF),
            pltpu.VMEM((2, 6, 16, 384), BF),
            pltpu.VMEM((4, 16, 256), BF),
            pltpu.VMEM((4, 16, 256), BF),
            pltpu.VMEM((4, 2, 16, 128), F32),
            pltpu.VMEM((128, 128), F32),
            pltpu.VMEM((2, 2, 16, 128), F32),
            pltpu.VMEM((2, 2, 16, 128), F32),
            pltpu.VMEM((32, 128), F32),
            pltpu.VMEM((32, 128), F32),
            pltpu.VMEM((2, 2, 1024), BF),
            pltpu.VMEM((4, 2, 1024), BF),
            pltpu.VMEM((2, 4, 1024), BF),
            pltpu.SemaphoreType.DMA((5,)),
            pltpu.SemaphoreType.DMA((8,)),
            pltpu.SemaphoreType.DMA((8,)),
            pltpu.SemaphoreType.REGULAR,
        ],
        compiler_params=pltpu.CompilerParams(
            collective_id=0, has_side_effects=True, vmem_limit_bytes=32 * 1024 * 1024
        ),
    )(*operands)
    return rows.reshape(4, 8, 4, 128).transpose(0, 2, 1, 3).reshape(density.shape)


def solution(mesh):
    placed = (P("gx", "gy", None), P(), P(), P(), P())
    return jax.shard_map(
        local, mesh=mesh, in_specs=placed, out_specs=P("gx", "gy", None), check_vma=False
    )
```

```python
import jax
import jax.numpy as jnp
from jax import lax
from jax.experimental import pallas as pl
from jax.experimental.pallas import tpu as pltpu
from jax.sharding import PartitionSpec as P

BF = jnp.bfloat16
F32 = jnp.float32
MESH = pl.DeviceIdType.MESH
HALO = 2
SIDES = [(1, 1), (0, 1), (1, 0), (1, -1), (-1, 1), (-1, 0), (0, -1), (-1, -1)]
LOWER = [(-1, 0), (0, -1), (-1, -1)]
SOURCE = {-1: slice(2, 4), 0: slice(2, 6), 1: slice(4, 6)}
RAW = {0: slice(0, 4), 1: slice(2, 4)}
TARGET = {-1: slice(6, 8), 0: slice(2, 6), 1: slice(0, 2)}


def near_offset(ox, oy):
    return 2 <= ox <= 4 and 2 <= oy <= 4


def chunks(ox, oy):
    return (0, 2) if near_offset(ox, oy) else (0, 1, 2)


def parities(offset):
    return tuple(p for p in (0, 1) if 0 <= offset - 1 + p <= 5)


def early_columns():
    return {0: ((1, 0),), 1: ((0, 0), (1, 1)), 2: ((0, 1),)}


def late_products(axis):
    classes = {}
    for ox in range(7):
        for oy in range(7):
            along, across = (ox, oy) if axis == "x" else (oy, ox)
            units = tuple(
                (t, s - t, p) for t, s in early_columns().get(along, ()) for p in parities(across)
            )
            if units:
                classes.setdefault(units, []).append((ox, oy))
    return classes


def dot(a, b):
    return jnp.dot(a, b, preferred_element_type=F32)


def widen(block):
    rows, lanes = block.shape
    block = jnp.concatenate([block, jnp.zeros((rows, 128 - lanes), BF)], axis=1)
    if rows < 64:
        block = jnp.concatenate([block, jnp.zeros((64 - rows, 128), BF)], axis=0)
    return block


def swap(block):
    return pltpu.roll(block, 64, 1)


def kernel(
    density, p2m_t, m2l, near, l2p, out,
    raw, cells, table, near_raw, p2m_raw, l2p_raw, weights, near_weights,
    far_rows, near_rows, far_x, far_y, near_x, near_y, total_ref, close_ref,
    far_late_x, far_late_y, near_late_x, near_late_y, raw_corner, raw_y, raw_x,
    in_sems, send_sems, recv_sems, ready,
):
    raw_in = [raw_corner, raw_y, raw_x]
    gx, gy = lax.axis_index("gx"), lax.axis_index("gy")
    nx, ny = lax.axis_size("gx"), lax.axis_size("gy")

    def present(dx, dy):
        ok = None
        for d, g, n in ((dx, gx, nx), (dy, gy, ny)):
            if d:
                test = (g + d >= 0) & (g + d < n)
                ok = test if ok is None else ok & test
        return ok

    copies_in = [
        pltpu.make_async_copy(density, raw, in_sems.at[0]),
        pltpu.make_async_copy(near, near_raw, in_sems.at[1]),
        pltpu.make_async_copy(p2m_t, p2m_raw, in_sems.at[2]),
        pltpu.make_async_copy(l2p, l2p_raw, in_sems.at[3]),
    ]
    barrier = pltpu.get_barrier_semaphore()

    def leads(dx, dy):
        return (gx + dx == 0) & (gy + dy == 0)

    def beside(dx, dy):
        return present(dx, dy) & jnp.logical_not(leads(dx, dy))

    @pl.when(jnp.logical_not(leads(0, 0)))
    def _():
        for dx, dy in SIDES:
            @pl.when(present(dx, dy))
            def _():
                pl.semaphore_signal(
                    barrier, inc=1, device_id=(gx + dx, gy + dy), device_id_type=MESH
                )

    def remote(k):
        dx, dy = SIDES[k]
        return pltpu.make_async_remote_copy(
            src_ref=cells.at[SOURCE[dy], SOURCE[dx]],
            dst_ref=cells.at[TARGET[dy], TARGET[dx]],
            send_sem=send_sems.at[k],
            recv_sem=recv_sems.at[k],
            device_id=(gx + dx, gy + dy),
            device_id_type=MESH,
        )

    def straight(k):
        dx, dy = SIDES[k]
        xs, ys = RAW[dx], RAW[dy]
        return pltpu.make_async_remote_copy(
            src_ref=density.at[xs, ys],
            dst_ref=raw_in[k].at[...],
            send_sem=send_sems.at[k],
            recv_sem=recv_sems.at[k],
            device_id=(gx + dx, gy + dy),
            device_id_type=MESH,
        )

    @pl.when(leads(0, 0))
    def _():
        pl.semaphore_wait(
            barrier, sum(present(-dx, -dy).astype(jnp.int32) for dx, dy in LOWER)
        )
        for k, (dx, dy) in enumerate(SIDES):
            if (-dx, -dy) in LOWER:
                @pl.when(present(dx, dy))
                def _():
                    straight(k).start()
        for dx, dy in LOWER:
            @pl.when(present(-dx, -dy))
            def _():
                pl.semaphore_signal(
                    ready, inc=1, device_id=(gx - dx, gy - dy), device_id_type=MESH
                )

    for c in copies_in:
        c.start()
    table_copy = pltpu.make_async_copy(m2l, table, in_sems.at[4])
    table_copy.start()

    def take(block, y0, x0):
        block = block.astype(F32)
        for y in range(block.shape[1]):
            for x in range(block.shape[0]):
                tile = jnp.concatenate(
                    [block[x, y : y + 1, 128 * z : 128 * z + 128] for z in range(8)], axis=0
                )
                cells[y0 + y, x0 + x] = tile.astype(BF)

    for dx, dy in SIDES:
        @pl.when(jnp.logical_not(present(dx, dy)))
        def _():
            ys, xs = TARGET[-dy], TARGET[-dx]
            cells[ys, xs] = jnp.zeros((ys.stop - ys.start, xs.stop - xs.start, 8, 128), BF)

    copies_in[0].wait()
    take(raw[...], HALO, HALO)

    def arrive(sides):
        for k, (dx, dy) in enumerate(SIDES):
            if (dx, dy) in sides:
                @pl.when(beside(-dx, -dy))
                def _():
                    remote(k).wait_recv()

                if (-dx, -dy) in LOWER:
                    @pl.when(leads(-dx, -dy))
                    def _():
                        straight(k).wait_recv()
                        ys, xs = TARGET[dy], TARGET[dx]
                        take(raw_in[k][...], ys.start, xs.start)

    for c in copies_in[1:]:
        c.wait()
    p2m_block = widen(p2m_raw[...])
    p2m = jnp.concatenate([p2m_block, swap(p2m_block)], axis=0)
    l2p_block = widen(l2p_raw[...])
    l2p_pair = jnp.concatenate([l2p_block, swap(l2p_block)], axis=0)
    low = lax.broadcasted_iota(jnp.int32, (64, 128), 1) < 64

    def build_near(i, carry):
        a, b, c = (widen(near_raw[i // 3, i % 3, k]) for k in range(3))
        near_weights[i, 0:64] = jnp.where(low, b, swap(a))
        near_weights[i, 64:128] = jnp.where(low, c, swap(b))
        near_weights[i, 128:192] = swap(c)
        near_weights[i, 192:256] = a
        return carry

    lax.fori_loop(0, 9, build_near, 0, unroll=9)

    @pl.when(jnp.logical_not(leads(0, 0)))
    def _():
        pl.semaphore_wait(
            barrier, sum(beside(dx, dy).astype(jnp.int32) for dx, dy in SIDES)
        )

    for k, (dx, dy) in enumerate(SIDES):
        @pl.when(beside(dx, dy) & jnp.logical_not(leads(0, 0)))
        def _():
            remote(k).start()

    table_copy.wait()
    for ox in range(7):
        def build(oy, carry):
            blocks = [widen(table[ox, oy, k]) for k in range(7)]
            for k in range(6):
                weights[ox, oy, 64 * k : 64 * k + 64] = jnp.where(
                    low, blocks[k + 1], swap(blocks[k])
                )
            return carry

        lax.fori_loop(0, 7, build, 0, unroll=7)
        if 2 <= ox <= 4:
            def build_close(oy, carry):
                weights[ox, oy, 64:128] = swap(widen(table[ox, oy, 1]))
                weights[ox, oy, 256:320] = widen(table[ox, oy, 5])
                return carry

            lax.fori_loop(2, 5, build_close, 0, unroll=3)

    def far_weights(pairs):
        return jnp.concatenate(
            [
                weights[ox, oy, 128 * c : 128 * c + 128]
                for ox, oy in pairs
                for c in chunks(ox, oy)
            ],
            axis=0,
        )

    def shifted(v):
        row = lax.broadcasted_iota(jnp.int32, v.shape, 1)
        below = jnp.where(row == 0, 0.0, pltpu.roll(v, 1, 1))
        above = jnp.where(row == 7, 0.0, pltpu.roll(v, 7, 1))
        return below, v, above

    def multipoles(columns):
        n = columns.shape[0]
        m = lax.dot_general(
            columns.reshape(8 * n, 128), p2m, (((1,), (1,)), ((), ())),
            preferred_element_type=F32,
        )
        return shifted(m.reshape(n, 8, 128))

    def neighbours(columns):
        below, own_rows, above = shifted(columns.astype(F32))
        half = lax.broadcasted_iota(jnp.int32, own_rows.shape, 2) < 64
        return own_rows, jnp.where(half, above, below)

    def pair(a, b):
        return jnp.concatenate([a, b], axis=0).astype(BF)

    zero_rows = jnp.zeros((8, 128), F32)

    arrive(LOWER)
    far_rows[0:2] = jnp.zeros((2, 6, 16, 384), BF)
    near_rows[0] = jnp.zeros((4, 16, 256), BF)

    def spread(y, carry):
        columns = cells[y, 2:8]
        for part, v in enumerate(multipoles(columns)):
            ln = slice(128 * part, 128 * part + 128)
            for x in range(6):
                first = v[x - 2] if x >= 2 else zero_rows
                far_rows[y, x, :, ln] = pair(first, v[x])
        for part, v in enumerate(neighbours(columns[0:5])):
            ln = slice(128 * part, 128 * part + 128)
            for x in range(1, 5):
                first = v[x - 2] if x >= 2 else zero_rows
                near_rows[y - 1, x - 1, :, ln] = pair(first, v[x])
        return carry

    lax.fori_loop(2, 8, spread, 0, unroll=6)

    close = jnp.zeros((128, 128), F32)
    for dx in range(3):
        for dy in range(3):
            close += dot(
                near_rows[dy : dy + 4, dx : dx + 2].reshape(128, 256), near_weights[3 * dx + dy]
            )
    close_ref[...] = close

    def place(value, ys, pars):
        i = 0
        for y in ys:
            for par in pars:
                total_ref[y, par] += value[16 * i : 16 * i + 16]
                i += 1

    total_ref[...] = jnp.zeros_like(total_ref)
    for pars in ((0, 1), (1,), (0,)):
        for ys, oys in (((0, 1, 2, 3), range(1, 6)), ((1, 3), (0,)), ((0, 2), (6,))):
            acc = jnp.zeros((16 * len(ys) * len(pars), 128), F32)
            for ox in range(7):
                if parities(ox) != pars:
                    continue
                x0 = ox - 1 + pars[0]
                for oy in oys:
                    lhs = jnp.concatenate(
                        [
                            jnp.concatenate(
                                [
                                    far_rows[y + oy - 1, x0 : x0 + len(pars), :, 128 * c : 128 * c + 128]
                                    for y in ys
                                ],
                                axis=0,
                            ).reshape(16 * len(ys) * len(pars), 128)
                            for c in chunks(ox, oy)
                        ],
                        axis=1,
                    )
                    acc += dot(lhs, far_weights([(ox, oy)]))
            place(acc, ys, pars)

    for k, (dx, dy) in enumerate(SIDES):
        @pl.when(beside(dx, dy) & jnp.logical_not(leads(0, 0)))
        def _():
            remote(k).wait_send()

        if (-dx, -dy) in LOWER:
            @pl.when(present(dx, dy) & leads(0, 0))
            def _():
                straight(k).wait_send()
    for k, (dx, dy) in enumerate(SIDES):
        if (dx, dy) in LOWER:
            @pl.when(leads(dx, dy))
            def _():
                pl.semaphore_wait(ready, 1)
                remote(k).start()

    def late(axis, far_ref, near_ref, far_late, near_late):
        places = (0, 1, 2) if axis == "x" else (0, 3, 6)
        lhs = jnp.concatenate([near_ref[d : d + 2].reshape(32, 256) for d in range(3)], axis=1)
        rhs = jnp.concatenate([near_weights[i] for i in places], axis=0)
        near_late[...] = dot(lhs, rhs)
        sums = {}
        for units, pairs in sorted(late_products(axis).items(), key=lambda c: -len(c[0])):
            columns = []
            for ox, oy in pairs:
                across = oy if axis == "x" else ox
                for c in chunks(ox, oy):
                    ln = slice(128 * c, 128 * c + 128)
                    columns.append(
                        jnp.concatenate(
                            [far_ref[t + d, across - 1 + p, :, ln] for t, d, p in units], axis=0
                        )
                    )
            value = dot(jnp.concatenate(columns, axis=1), far_weights(pairs))
            for i, (t, _, p) in enumerate(units):
                part = value[16 * i : 16 * i + 16]
                sums[t, p] = sums[t, p] + part if (t, p) in sums else part
        for t, p in sums:
            far_late[t, p] = sums[t, p]

    @pl.when(gx == 0)
    def _():
        far_late_x[...] = jnp.zeros_like(far_late_x)
        near_late_x[...] = jnp.zeros_like(near_late_x)

    @pl.when(gy == 0)
    def _():
        far_late_y[...] = jnp.zeros_like(far_late_y)
        near_late_y[...] = jnp.zeros_like(near_late_y)

    arrive([side for side in SIDES if side in ((0, 1), (-1, 1))])

    @pl.when(gy > 0)
    def _():
        columns = cells[0:2, 2:8].reshape(12, 8, 128)
        for part, v in enumerate(multipoles(columns)):
            ln = slice(128 * part, 128 * part + 128)
            for y in range(2):
                for x in range(6):
                    first = v[6 * y + x - 2] if x >= 2 else zero_rows
                    far_y[y, x, :, ln] = pair(first, v[6 * y + x])
        for part, v in enumerate(neighbours(cells[1, 2:7])):
            ln = slice(128 * part, 128 * part + 128)
            for x in range(1, 5):
                first = v[x - 2] if x >= 2 else zero_rows
                near_y[x - 1, :, ln] = pair(first, v[x])
        late("y", far_y, near_y, far_late_y, near_late_y)

    arrive([side for side in SIDES if side in ((1, 0), (1, 1), (1, -1))])

    @pl.when(gx > 0)
    def _():
        columns = cells[:, 0:2].reshape(16, 8, 128)
        for part, v in enumerate(multipoles(columns)):
            ln = slice(128 * part, 128 * part + 128)
            for x in range(2):
                for y in range(6):
                    far_x[x, y, :, ln] = pair(v[2 * y + x], v[2 * y + 4 + x])
        for part, v in enumerate(neighbours(cells[1:7, 1])):
            ln = slice(128 * part, 128 * part + 128)
            for y in range(4):
                near_x[y, :, ln] = pair(v[y], v[y + 2])
        late("x", far_x, near_x, far_late_x, near_late_x)

    def eight(value, i):
        return value[8 * i : 8 * i + 8]

    expansion = []
    for y in range(4):
        for x in range(4):
            value = eight(total_ref[y, x % 2], x // 2)
            if x < 2:
                value = value + far_late_x[x, y % 2, 8 * (y // 2) : 8 * (y // 2) + 8]
            if y < 2:
                value = value + far_late_y[y, x % 2, 8 * (x // 2) : 8 * (x // 2) + 8]
            expansion.append(value)
    distant = dot(jnp.concatenate(expansion, axis=0).astype(BF), l2p_pair)
    for y in range(4):
        for x in range(4):
            value = eight(distant, 4 * y + x) + eight(close_ref[...], 4 * y + 2 * (x % 2) + x // 2)
            if x == 0:
                value = value + eight(near_late_x[...], 2 * (y % 2) + y // 2)
            if y == 0:
                value = value + eight(near_late_y[...], 2 * (x % 2) + x // 2)
            for z in range(8):
                out[x, y : y + 1, 128 * z : 128 * z + 128] = value[z : z + 1]

    for k, (dx, dy) in enumerate(SIDES):
        if (dx, dy) in LOWER:
            @pl.when(leads(dx, dy))
            def _():
                remote(k).wait_send()


def local(density, p2m_operator, m2l_table, near_table, l2p_operator):
    in_hbm = pl.BlockSpec(memory_space=pltpu.HBM)
    operands = [
        pltpu.with_memory_space_constraint(v, pltpu.HBM)
        for v in (density, p2m_operator.T, m2l_table, near_table, l2p_operator)
    ]
    return pl.pallas_call(
        kernel,
        out_shape=jax.ShapeDtypeStruct(density.shape, F32),
        in_specs=[in_hbm] * 5,
        out_specs=pl.BlockSpec(memory_space=pltpu.VMEM),
        scratch_shapes=[
            pltpu.VMEM((4, 4, 1024), BF),
            pltpu.VMEM((8, 8, 8, 128), BF),
            pltpu.VMEM((7, 7, 7, 56, 56), BF),
            pltpu.VMEM((3, 3, 3, 64, 64), BF),
            pltpu.VMEM((56, 64), BF),
            pltpu.VMEM((56, 64), BF),
            pltpu.VMEM((7, 7, 384, 128), BF),
            pltpu.VMEM((9, 256, 128), BF),
            pltpu.VMEM((8, 6, 16, 384), BF),
            pltpu.VMEM((7, 4, 16, 256), BF),
            pltpu.VMEM((2, 6, 16, 384), BF),
            pltpu.VMEM((2, 6, 16, 384), BF),
            pltpu.VMEM((4, 16, 256), BF),
            pltpu.VMEM((4, 16, 256), BF),
            pltpu.VMEM((4, 2, 16, 128), F32),
            pltpu.VMEM((128, 128), F32),
            pltpu.VMEM((2, 2, 16, 128), F32),
            pltpu.VMEM((2, 2, 16, 128), F32),
            pltpu.VMEM((32, 128), F32),
            pltpu.VMEM((32, 128), F32),
            pltpu.VMEM((2, 2, 1024), BF),
            pltpu.VMEM((4, 2, 1024), BF),
            pltpu.VMEM((2, 4, 1024), BF),
            pltpu.SemaphoreType.DMA((5,)),
            pltpu.SemaphoreType.DMA((8,)),
            pltpu.SemaphoreType.DMA((8,)),
            pltpu.SemaphoreType.REGULAR,
        ],
        compiler_params=pltpu.CompilerParams(
            collective_id=0, has_side_effects=True, vmem_limit_bytes=32 * 1024 * 1024
        ),
    )(*operands)


def solution(mesh):
    placed = (P("gx", "gy", None), P(), P(), P(), P())
    return jax.shard_map(
        local, mesh=mesh, in_specs=placed, out_specs=P("gx", "gy", None), check_vma=False
    )
```
